32 devices in a mesh: grp: 2 (over y), freq: 4 (over z), tm: 2 (over x), pol: 2 (over core).
Axes of the slice: x: 2, y: 2, z: 4, core: 2. Of those that a mesh axis runs over, the one named last changes fastest.
Arguments:
- voltages: bfloat16 [2, 8, 1024, 4, 2, 256], P('pol', ('grp', 'freq'), 'tm'), parts along dimension 1, may hold values from -6 to 6
- feed_gains: float32 [8, 2, 4, 2, 256], P(('grp', 'freq'), 'pol'), parts along dimension 0, may hold values from -5 to 5
- owner_table: int32 [64], replicated, may hold values from 0 to 3, as said below
- keep_flags: int32 [1024], replicated, may hold values 0 or 1
Outputs:
- owned: bfloat16 [128, 64, 2048], P(('grp', 'tm', 'pol'), None, 'freq'), parts along dimension 0
The draws below stay inside these ranges and needn't reach their ends.
There are 2 independent parts, one for each index of `grp`. The reference program is written for one: setup_inputs(seed, part) draws one part's arguments, and reference() takes and returns one part's arrays. A program takes and returns all parts, laid end to end along the dimension named above; an argument that names none is the same for every part. Nothing has to cross between parts.
Inputs may be any that keep to these rules, and one draw needn't show every extreme that they name: `owner_table`: each index of freq owns from 0 to 32 beam sets; one owns exactly 32.
All inputs are finite; a program needn't handle non-finite values.
Results may differ from the reference program's by a relative error of at most 0.0058.
Values may be sent and summed in bfloat16 or wider, within the bound.
No kernel may reach another device: no remote copies, remote signals or barrier semaphores. Data moves between devices by JAX's collectives and lax.ppermute only.
A program may use at most 64 MiB of HBM per device.

```python
import jax
import jax.numpy as jnp
from jax import lax

NS = 256
CYL = 4
UPCH = 16
TAPS = 16
SET_BEAMS = 16
BEAMS = 1024
SETS = 64
MOST = 32
CHANNELS = 4
FRAMES = 64
SAMPLES = 1024
N_FREQ = 4


def draw_owner_table(key, part):
    key_big = jax.random.fold_in(key, 11)
    key_slots = jax.random.fold_in(key, 23)
    key_order = jax.random.fold_in(key, 37)
    biggest = jax.random.randint(key_big, (), 0, N_FREQ).astype(jnp.int32)
    others = (biggest + 1 + jnp.arange(N_FREQ - 1, dtype=jnp.int32)) % N_FREQ
    shuffled = jax.random.permutation(key_slots, (N_FREQ - 1) * MOST)
    chosen = shuffled[:SETS - MOST]
    extra_owner = jnp.take(others, chosen // MOST)
    sequence = jnp.concatenate([jnp.zeros((MOST,), jnp.int32) + biggest, extra_owner.astype(jnp.int32)])
    order = jax.random.permutation(key_order, SETS)
    return jnp.take(sequence, order).astype(jnp.int32)


def plant(entries, stream_key, smallest, largest):
    shape = entries.shape
    spot = [jax.random.randint(jax.random.fold_in(stream_key, axis), (), 0, shape[axis]) for axis in range(len(shape))]
    entries = entries.at[tuple(spot)].set(smallest)
    longest = shape.index(max(shape))
    spot[longest] = (spot[longest] + 1) % shape[longest]
    return entries.at[tuple(spot)].set(largest)


def shard_levels(own_key, extent, cuts, low, high):
    level = 1.0
    for axis_at, parts in cuts:
        draws = jax.random.uniform(jax.random.fold_in(jax.random.fold_in(own_key, 6), axis_at), (parts,), jnp.float32, low / len(cuts), high / len(cuts))
        level = level * jnp.repeat(jnp.exp(draws), extent[axis_at] // parts).reshape((-1,) + (1,) * (len(extent) - 1 - axis_at))
    return level


def centred(own_key, extent, spread, limit, cuts=(), kind=jnp.bfloat16):
    result = jax.random.normal(own_key, extent, jnp.float32) * spread
    if len(cuts) > 0:
        result = shard_levels(own_key, extent, cuts, -0.22, 0.18) * result
    return jnp.clip(result, min=-limit, max=limit).astype(kind)


def setup_inputs(seed: int = 0, part: int = 0) -> dict:
    key_list = jax.random.split(jax.random.key(seed), 5)
    own_keys = jax.random.split(jax.random.fold_in(key_list[4], part), 5)
    voltages = centred(own_keys[0], (2, CHANNELS, SAMPLES, CYL, 2, NS), 1.0, 6.0, ((0, 2), (1, 4), (2, 2)))
    feed_gains = centred(own_keys[1], (CHANNELS, 2, CYL, 2, NS), 1.0, 5.0, ((0, 4), (1, 2)), jnp.float32)
    owner_table = draw_owner_table(jax.random.fold_in(key_list[4], 71), part)
    keep_flags = plant((jax.random.randint(key_list[3], (BEAMS,), 0, 4) < 3).astype(jnp.int32), jax.random.fold_in(key_list[3], 1), 0, 1)
    return dict(voltages=voltages, feed_gains=feed_gains, owner_table=owner_table, keep_flags=keep_flags)


def window_taps():
    span = TAPS * UPCH
    steps = jnp.arange(span, dtype=jnp.float32)
    weights = jnp.sinc((steps - (span - 1) / 2.0) / UPCH) * jnp.sin(jnp.pi * (steps + 0.5) / span) ** 2
    weights = weights / jnp.sqrt(jnp.sum(weights * weights))
    return weights.reshape(TAPS, UPCH)

def fine_tables():
    rows = jnp.arange(UPCH, dtype=jnp.int32)
    phase = rows[:, None] * rows[None, :] % UPCH
    angle = 2.0 * jnp.pi * phase.astype(jnp.float32) / UPCH
    return (jnp.cos(angle), jnp.sin(angle))

def beam_matrix():
    rows = jnp.arange(NS, dtype=jnp.int32)
    phase = rows[:, None] * rows[None, :] % NS
    angle = 2.0 * jnp.pi * phase.astype(jnp.float32) / NS
    scale = 1.0 / jnp.sqrt(jnp.float32(NS))
    cosine = jnp.cos(angle) * scale
    sine = jnp.sin(angle) * scale
    upper = jnp.concatenate([cosine, -sine], axis=1)
    lower = jnp.concatenate([sine, cosine], axis=1)
    return jnp.concatenate([upper, lower], axis=0).astype(jnp.bfloat16)

def cylinder_tables():
    rows = jnp.arange(CYL, dtype=jnp.int32)
    phase = rows[:, None] * rows[None, :] % CYL
    angle = 2.0 * jnp.pi * phase.astype(jnp.float32) / CYL
    return (0.5 * jnp.cos(angle), 0.5 * jnp.sin(angle))

def power_frames(frames, gain_pol, n_out):
    window = window_taps()
    fine_cos, fine_sin = fine_tables()
    beam_table = beam_matrix()
    cyl_cos, cyl_sin = cylinder_tables()
    highest = lax.Precision.HIGHEST
    chan_count = frames.shape[0]
    summed = jnp.zeros((chan_count, n_out) + frames.shape[2:], jnp.float32)
    for tap_index in range(TAPS):
        weights = window[tap_index].reshape(1, 1, UPCH, 1, 1, 1)
        summed = summed + weights * frames[:, tap_index:tap_index + n_out].astype(jnp.float32)
    real_part = summed[:, :, :, :, 0, :]
    imag_part = summed[:, :, :, :, 1, :]
    spec_real = jnp.einsum('qk,cmkxn->mcqxn', fine_cos, real_part, precision=highest) + jnp.einsum('qk,cmkxn->mcqxn', fine_sin, imag_part, precision=highest)
    spec_imag = jnp.einsum('qk,cmkxn->mcqxn', fine_cos, imag_part, precision=highest) - jnp.einsum('qk,cmkxn->mcqxn', fine_sin, real_part, precision=highest)
    gain_real = gain_pol[:, :, 0, :][None, :, None]
    gain_imag = gain_pol[:, :, 1, :][None, :, None]
    cal_real = spec_real * gain_real - spec_imag * gain_imag
    cal_imag = spec_real * gain_imag + spec_imag * gain_real
    calibrated = jnp.stack([cal_real, cal_imag], axis=4).astype(jnp.bfloat16)
    row_count = n_out * chan_count * UPCH
    flat = calibrated.reshape(row_count * CYL, 2 * NS)
    partial_value = jnp.dot(flat.astype(jnp.float32), beam_table.astype(jnp.float32), precision=highest, preferred_element_type=jnp.float32)
    partial_value = partial_value.reshape(row_count, CYL, 2, NS)
    beam_real = partial_value[:, :, 0, :]
    beam_imag = partial_value[:, :, 1, :]
    form_real = jnp.einsum('ec,rcn->ren', cyl_cos, beam_real, precision=highest) + jnp.einsum('ec,rcn->ren', cyl_sin, beam_imag, precision=highest)
    form_imag = jnp.einsum('ec,rcn->ren', cyl_cos, beam_imag, precision=highest) - jnp.einsum('ec,rcn->ren', cyl_sin, beam_real, precision=highest)
    powers = (form_real * form_real + form_imag * form_imag).astype(jnp.bfloat16)
    return powers.reshape(n_out, chan_count * UPCH, CYL * NS)

def slot_columns(owner_table, keep_flags, n_owner, most_sets):
    count = owner_table.shape[0]
    order = jnp.arange(count, dtype=jnp.int32)
    same_owner = owner_table[:, None] == owner_table[None, :]
    earlier = order[None, :] < order[:, None]
    set_rank = lax.optimization_barrier(jnp.sum(jnp.logical_and(same_owner, earlier).astype(jnp.int32), axis=1))
    slot_index = owner_table * most_sets + set_rank
    places = jnp.arange(n_owner * most_sets, dtype=jnp.int32)
    matches = (slot_index[None, :] == places[:, None]).astype(jnp.int32)
    filled = lax.optimization_barrier(jnp.sum(matches, axis=1))
    set_of = lax.optimization_barrier(jnp.sum(matches * order[None, :], axis=1))
    within = jnp.arange(SET_BEAMS, dtype=jnp.int32)
    beam_index = (set_of[:, None] * SET_BEAMS + within[None, :]).reshape(-1).astype(jnp.int32)
    kept = jnp.take(keep_flags, beam_index).reshape(-1, SET_BEAMS)
    column_mask = (filled[:, None] * kept).reshape(-1)
    return (beam_index, column_mask)

def reference(voltages, feed_gains, owner_table, keep_flags):
    pad_count = (TAPS - 1) * UPCH

    def one_channel(chan_index):
        volts_here = lax.dynamic_index_in_dim(voltages, chan_index, 1, keepdims=False)
        gains_here = lax.dynamic_index_in_dim(feed_gains, chan_index, 0, keepdims=False)
        summed = jnp.zeros((FRAMES, UPCH, CYL * NS), jnp.float32)
        for pol_index in range(2):
            padded = jnp.concatenate([jnp.zeros((pad_count, CYL, 2, NS), jnp.bfloat16), volts_here[pol_index]], axis=0)
            frames = padded.reshape(1, FRAMES + TAPS - 1, UPCH, CYL, 2, NS)
            summed = summed + power_frames(frames, gains_here[pol_index][None], FRAMES).astype(jnp.float32)
        return summed.astype(jnp.bfloat16)
    per_channel = lax.map(one_channel, jnp.arange(CHANNELS, dtype=jnp.int32))
    intensity = jnp.transpose(per_channel, (1, 0, 2, 3)).reshape(FRAMES, CHANNELS * UPCH, CYL * NS)
    beam_index, column_mask = slot_columns(owner_table, keep_flags, N_FREQ, MOST)
    return jnp.take(intensity, beam_index, axis=2) * column_mask.astype(jnp.bfloat16)[None, None, :]
```

```python
import functools

import jax
import jax.numpy as jnp
import numpy as np
from jax import lax
from jax.experimental import pallas as pl
from jax.experimental.pallas import tpu as pltpu
from jax.sharding import PartitionSpec as P

NS = 256
CYL = 4
UPCH = 16
TAPS = 16
SET_BEAMS = 16
BLOCK = 8
ROWS = 2 * UPCH


def window_taps():
    span = TAPS * UPCH
    steps = np.arange(span, dtype=np.float64)
    weights = np.sinc((steps - (span - 1) / 2.0) / UPCH) * np.sin(np.pi * (steps + 0.5) / span) ** 2
    return weights / np.sqrt(np.sum(weights * weights))


def filter_matrix():
    weights = window_taps()
    fine = np.arange(UPCH)
    sample = np.arange(TAPS * UPCH)
    phase = 2.0 * np.pi * ((fine[:, None] * sample[None, :]) % UPCH) / UPCH
    cosine = np.cos(phase) * weights
    sine = np.sin(phase) * weights
    table = np.zeros((2, BLOCK, UPCH, TAPS + BLOCK, UPCH, 2))
    for frame in range(BLOCK):
        taps = slice(frame + 1, frame + 1 + TAPS)
        cos_part = cosine.reshape(UPCH, TAPS, UPCH)
        sin_part = sine.reshape(UPCH, TAPS, UPCH)
        table[0, frame, :, taps, :, 0] = cos_part
        table[0, frame, :, taps, :, 1] = sin_part
        table[1, frame, :, taps, :, 0] = -sin_part
        table[1, frame, :, taps, :, 1] = cos_part
    table = table.reshape(2 * BLOCK * UPCH, (TAPS + BLOCK) * ROWS).astype(np.float32)
    high = table.astype(jnp.bfloat16)
    low = (table - high.astype(np.float32)).astype(jnp.bfloat16)
    return np.concatenate([high, low], axis=0)


def beam_matrix():
    rows = np.arange(NS)
    angle = 2.0 * np.pi * (rows[:, None] * rows[None, :] % NS) / NS
    scale = 1.0 / np.sqrt(NS)
    cosine = (np.cos(angle) * scale).astype(np.float32)
    sine = (np.sin(angle) * scale).astype(np.float32)
    upper = np.concatenate([cosine, -sine], axis=1)
    lower = np.concatenate([sine, cosine], axis=1)
    table = np.concatenate([upper, lower], axis=0).astype(jnp.bfloat16)
    return (table.astype(np.float32) * 0.5).astype(jnp.bfloat16)


def form_powers(parts, gain_ref, beam_ref, out_ref, out_start):
    half = BLOCK * UPCH
    beams = []
    for cyl in range(CYL):
        total = None
        for table, samples in parts(cyl):
            term = jnp.dot(table, samples, preferred_element_type=jnp.float32)
            total = term if total is None else total + term
        spec = total[: 2 * half] + total[2 * half :]
        real, imag = spec[:half], spec[half:]
        gain_real = gain_ref[cyl, 0:1, :]
        gain_imag = gain_ref[cyl, 1:2, :]
        cal_real = (real * gain_real - imag * gain_imag).astype(jnp.bfloat16)
        cal_imag = (real * gain_imag + imag * gain_real).astype(jnp.bfloat16)
        beam = jnp.dot(cal_real, beam_ref[:NS, :], preferred_element_type=jnp.float32)
        beam = beam + jnp.dot(cal_imag, beam_ref[NS:, :], preferred_element_type=jnp.float32)
        beams.append((beam[:, :NS], beam[:, NS:]))
    (r0, i0), (r1, i1), (r2, i2), (r3, i3) = beams
    pr, pi, mr, mi = r0 + r2, i0 + i2, r0 - r2, i0 - i2
    sr, si, dr, di = r1 + r3, i1 + i3, r1 - r3, i1 - i3
    formed = [(pr + sr, pi + si), (mr + di, mi - dr), (pr - sr, pi - si), (mr - di, mi + dr)]
    for element, (fr, fi) in enumerate(formed):
        power = (fr * fr + fi * fi).astype(jnp.bfloat16)
        out_ref[pl.ds(out_start, half), element * NS : (element + 1) * NS] = power


def columns(cyl):
    return slice(cyl * NS, (cyl + 1) * NS)


def local_kernel(blocks, first, filt_ref, x_ref, gain_ref, beam_ref, out_ref):
    depth = (TAPS + BLOCK) * ROWS

    def step(block, carry):
        start = pl.multiple_of((first - TAPS + block * BLOCK) * ROWS, 256)

        def parts(cyl):
            return [(filt_ref[...], x_ref[pl.ds(start, depth), columns(cyl)])]

        form_powers(parts, gain_ref, beam_ref, out_ref, pl.multiple_of(block * BLOCK * UPCH, 128))
        return carry

    lax.fori_loop(0, blocks, step, 0)


def near_kernel(filt_ref, near_ref, x_ref, gain_ref, beam_ref, out_ref):
    reach = BLOCK * ROWS

    def parts(cyl):
        return [
            (filt_ref[:, :reach], near_ref[:, columns(cyl)]),
            (filt_ref[:, reach:], x_ref[: 2 * reach, columns(cyl)]),
        ]

    form_powers(parts, gain_ref, beam_ref, out_ref, 0)


def far_kernel(filt_ref, edge_ref, far_ref, near_ref, x_ref, gain_ref, beam_ref, out_ref):
    reach = BLOCK * ROWS

    def parts(cyl):
        return [
            (filt_ref[:, reach : 2 * reach], near_ref[:, columns(cyl)]),
            (filt_ref[:, 2 * reach :], x_ref[:reach, columns(cyl)]),
            (edge_ref[...], far_ref[:, columns(cyl)]),
        ]

    form_powers(parts, gain_ref, beam_ref, out_ref, 0)


def place_table_kernel(most_sets, me_ref, owner_ref, out_ref):
    n_owner, beams, width = out_ref.shape
    sets = owner_ref.shape[1]
    owner = owner_ref[...].astype(jnp.float32)
    set_of = lax.broadcasted_iota(jnp.int32, (beams, sets), 0) // SET_BEAMS
    lane = lax.broadcasted_iota(jnp.int32, (beams, sets), 1)
    own = jnp.sum(jnp.where(set_of == lane, owner, 0.0), axis=1, keepdims=True)
    same = jnp.logical_and(owner == own, lane < set_of)
    rank = jnp.sum(jnp.where(same, 1.0, 0.0), axis=1, keepdims=True)
    within = lax.broadcasted_iota(jnp.int32, (beams, 1), 0) % SET_BEAMS
    column = (own * most_sets + rank).astype(jnp.int32) * SET_BEAMS + within
    place = lax.broadcasted_iota(jnp.int32, (beams, width), 1)
    for k in range(n_owner):
        owner_k = lax.rem(me_ref[0] + k, n_owner)
        hit = (column - owner_k * width) == place
        out_ref[k] = jnp.where(hit, 1.0, 0.0).astype(jnp.bfloat16)


def place_kernel(mine_ref, other_ref, keep_ref, table_ref, *out_refs):
    total = mine_ref[...].astype(jnp.float32) + other_ref[...].astype(jnp.float32)
    total = (total * keep_ref[...].astype(jnp.float32)).astype(jnp.bfloat16)
    for k, out_ref in enumerate(out_refs):
        placed = jnp.dot(total, table_ref[k], preferred_element_type=jnp.float32)
        out_ref[...] = placed.astype(jnp.bfloat16)


def gather_kernel(n_owner, where_ref, *refs):
    late, near, far, out_ref = refs[:n_owner], refs[n_owner : 2 * n_owner], refs[2 * n_owner : -1], refs[-1]
    me = where_ref[0]

    def copy(block, frame, k):
        source = lax.rem(me + n_owner - k, n_owner)
        rows = pl.ds(pl.multiple_of(source * UPCH, UPCH), UPCH)
        count = block.shape[0] // UPCH
        out_ref[frame : frame + count, rows, :] = block[...].reshape(count, UPCH, block.shape[1])

    @pl.when(where_ref[1] == 1)
    def _():
        for k in range(n_owner):
            copy(late[k], 0, k)

    @pl.when(where_ref[1] == 0)
    def _():
        for k in range(n_owner):
            copy(far[k], 0, k)
            copy(near[k], BLOCK, k)


VMEM = pl.BlockSpec(memory_space=pltpu.VMEM)
SMEM = pl.BlockSpec(memory_space=pltpu.SMEM)


def call(body, out_shape, n_in, flops, nbytes, scalars=0):
    many = isinstance(out_shape, (list, tuple))
    return pl.pallas_call(
        body,
        out_shape=out_shape,
        in_specs=[SMEM] * scalars + [VMEM] * n_in,
        out_specs=[VMEM] * len(out_shape) if many else VMEM,
        cost_estimate=pl.CostEstimate(flops=flops, bytes_accessed=nbytes, transcendentals=0),
        compiler_params=pltpu.CompilerParams(vmem_limit_bytes=40 << 20),
    )


def per_device(voltages, feed_gains, owner_table, keep_flags):
    samples = voltages[0, 0]
    gain = feed_gains[0, 0]
    frame_count = samples.shape[0] // UPCH
    kept = frame_count // 2
    assert voltages.shape[1] == 1 and kept == 2 * BLOCK and kept >= TAPS
    n_owner = lax.axis_size("freq")
    n_tm = lax.axis_size("tm")
    me = lax.axis_index("freq")
    pol = lax.axis_index("pol")
    most_sets = 2 * owner_table.shape[0] // n_owner
    beams = keep_flags.shape[0]
    width = most_sets * SET_BEAMS
    bf16 = jnp.bfloat16
    filt = jnp.asarray(filter_matrix())
    edge = jnp.asarray(filter_matrix()[:, ROWS : BLOCK * ROWS])
    beam_table = jnp.asarray(beam_matrix())

    def rows_of(part):
        return part.transpose(0, 2, 1, 3).reshape(part.shape[0] * 2, CYL * NS)

    def ahead(part):
        return lax.ppermute(part, "tm", [(i, i + 1) for i in range(n_tm - 1)])

    length = samples.shape[0]
    near_at = length - BLOCK * UPCH
    far_at = length - (TAPS - 1) * UPCH
    near = ahead(rows_of(samples[near_at:]))
    far = ahead(rows_of(samples[far_at:near_at]))
    x = rows_of(samples)

    def powers(body, frames, *args):
        rows = frames * UPCH
        flops = frames // BLOCK * 2 * 512 * 1024 * 1024
        return call(body, jax.ShapeDtypeStruct((rows, CYL * NS), bf16), len(args), flops, 3 << 20)(*args)

    def swap(block, source):
        return lax.ppermute(block, "pol", [(source, 1 - source)])

    where = jnp.stack([me, pol]).astype(jnp.int32)
    table = call(
        functools.partial(place_table_kernel, most_sets),
        jax.ShapeDtypeStruct((n_owner, beams, width), bf16),
        1,
        1 << 24,
        4 << 20,
        scalars=1,
    )(where, owner_table.reshape(1, -1))
    keep = keep_flags.reshape(1, -1)

    def regroup(mine, target):
        other = swap(mine, 1 - target)
        rows = mine.shape[0]
        shape = jax.ShapeDtypeStruct((rows, width), bf16)
        blocks = call(place_kernel, [shape] * n_owner, 4, 2 * rows * beams * beams * 2, 6 << 20)(
            mine, other, keep, table
        )
        got = [blocks[0]]
        for k in range(1, n_owner):
            route = [(i * 2 + target, (i + k) % n_owner * 2 + target) for i in range(n_owner)]
            got.append(lax.ppermute(blocks[k], ("freq", "pol"), route))
        return got

    late_powers = powers(functools.partial(local_kernel, kept // BLOCK, kept), kept, filt, x, gain, beam_table)
    late = regroup(late_powers, 1)
    near_powers = powers(near_kernel, BLOCK, filt, near, x, gain, beam_table)
    early_near = regroup(near_powers, 0)
    far_powers = powers(far_kernel, BLOCK, filt, edge, far, near, x, gain, beam_table)
    early_far = regroup(far_powers, 0)
    out_shape = jax.ShapeDtypeStruct((kept, n_owner * UPCH, width), bf16)
    return call(functools.partial(gather_kernel, n_owner), out_shape, 3 * n_owner, 0, 3 << 20, scalars=1)(
        where, *late, *early_near, *early_far
    )


def solution(mesh):
    return jax.shard_map(
        per_device,
        mesh=mesh,
        in_specs=(
            P("pol", ("grp", "freq"), "tm", None, None, None),
            P(("grp", "freq"), "pol", None, None, None),
            P(),
            P(),
        ),
        out_specs=P(("grp", "tm", "pol"), None, "freq"),
        check_vma=False,
    )
```

```python
import functools

import jax
import jax.numpy as jnp
import numpy as np
from jax import lax
from jax.experimental import pallas as pl
from jax.experimental.pallas import tpu as pltpu
from jax.sharding import PartitionSpec as P


NS = 256
CYL = 4
UPCH = 16
TAPS = 16
SET_BEAMS = 16
BLOCK = 8
LANES = 128
ROWS = 2 * UPCH


def window_taps():
    span = TAPS * UPCH
    steps = np.arange(span, dtype=np.float64)
    weights = np.sinc((steps - (span - 1) / 2.0) / UPCH) * np.sin(np.pi * (steps + 0.5) / span) ** 2
    return weights / np.sqrt(np.sum(weights * weights))


def filter_matrix():
    weights = window_taps()
    fine = np.arange(UPCH)
    sample = np.arange(TAPS * UPCH)
    phase = 2.0 * np.pi * ((fine[:, None] * sample[None, :]) % UPCH) / UPCH
    cosine = np.cos(phase) * weights
    sine = np.sin(phase) * weights
    table = np.zeros((2, BLOCK, UPCH, TAPS + BLOCK, UPCH, 2))
    for frame in range(BLOCK):
        taps = slice(frame + 1, frame + 1 + TAPS)
        cos_part = cosine.reshape(UPCH, TAPS, UPCH)
        sin_part = sine.reshape(UPCH, TAPS, UPCH)
        table[0, frame, :, taps, :, 0] = cos_part
        table[0, frame, :, taps, :, 1] = sin_part
        table[1, frame, :, taps, :, 0] = -sin_part
        table[1, frame, :, taps, :, 1] = cos_part
    table = table.reshape(2 * BLOCK * UPCH, (TAPS + BLOCK) * ROWS).astype(np.float32)
    high = table.astype(jnp.bfloat16)
    low = (table - high.astype(np.float32)).astype(jnp.bfloat16)
    return np.concatenate([high, low], axis=0)


def beam_matrix():
    rows = np.arange(NS)
    angle = 2.0 * np.pi * (rows[:, None] * rows[None, :] % NS) / NS
    scale = 1.0 / np.sqrt(NS)
    cosine = (np.cos(angle) * scale).astype(np.float32)
    sine = (np.sin(angle) * scale).astype(np.float32)
    upper = np.concatenate([cosine, -sine], axis=1)
    lower = np.concatenate([sine, cosine], axis=1)
    table = np.concatenate([upper, lower], axis=0).astype(jnp.bfloat16)
    table = table.reshape(2 * NS, 2, NS // LANES, LANES).transpose(0, 2, 1, 3).reshape(2 * NS, 2 * NS)
    return (table.astype(np.float32) * 0.5).astype(jnp.bfloat16)


def form_powers(parts, gain_ref, beam_ref, out_ref, cal_ref, out_start):
    half = BLOCK * UPCH
    for cyl in range(CYL):
        total = None
        for table, samples in parts(cyl):
            term = jnp.dot(table, samples, preferred_element_type=jnp.float32)
            total = term if total is None else total + term
        spec = total[: 2 * half] + total[2 * half :]
        real, imag = spec[:half], spec[half:]
        gain_real = gain_ref[cyl, 0:1, :]
        gain_imag = gain_ref[cyl, 1:2, :]
        rows = slice(cyl * half, (cyl + 1) * half)
        cal_ref[rows, :NS] = (real * gain_real - imag * gain_imag).astype(jnp.bfloat16)
        cal_ref[rows, NS:] = (real * gain_imag + imag * gain_real).astype(jnp.bfloat16)
    for strip in range(NS // LANES):
        beam = jnp.dot(
            cal_ref[...],
            beam_ref[:, strip * 2 * LANES : (strip + 1) * 2 * LANES],
            preferred_element_type=jnp.float32,
        )
        beams = [beam[cyl * half : (cyl + 1) * half] for cyl in range(CYL)]
        (r0, i0), (r1, i1), (r2, i2), (r3, i3) = [(b[:, :LANES], b[:, LANES:]) for b in beams]
        pr, pi, mr, mi = r0 + r2, i0 + i2, r0 - r2, i0 - i2
        sr, si, dr, di = r1 + r3, i1 + i3, r1 - r3, i1 - i3
        formed = [(pr + sr, pi + si), (mr + di, mi - dr), (pr - sr, pi - si), (mr - di, mi + dr)]
        for element, (fr, fi) in enumerate(formed):
            power = (fr * fr + fi * fi).astype(jnp.bfloat16)
            at = element * NS + strip * LANES
            out_ref[pl.ds(out_start, half), at : at + LANES] = power


def columns(cyl):
    return slice(cyl * NS, (cyl + 1) * NS)


def local_kernel(blocks, first, filt_ref, x_ref, gain_ref, beam_ref, out_ref, cal_ref):
    depth = (TAPS + BLOCK) * ROWS

    def step(block, carry):
        start = pl.multiple_of((first - TAPS + block * BLOCK) * ROWS, 256)

        def parts(cyl):
            return [(filt_ref[...], x_ref[pl.ds(start, depth), columns(cyl)])]

        form_powers(parts, gain_ref, beam_ref, out_ref, cal_ref, pl.multiple_of(block * BLOCK * UPCH, 128))
        return carry

    lax.fori_loop(0, blocks, step, 0)


def near_kernel(filt_ref, near_ref, x_ref, gain_ref, beam_ref, out_ref, cal_ref):
    reach = BLOCK * ROWS

    def parts(cyl):
        return [
            (filt_ref[:, :reach], near_ref[:, columns(cyl)]),
            (filt_ref[:, reach:], x_ref[: 2 * reach, columns(cyl)]),
        ]

    form_powers(parts, gain_ref, beam_ref, out_ref, cal_ref, 0)


def far_kernel(filt_ref, edge_ref, far_ref, near_ref, x_ref, gain_ref, beam_ref, out_ref, cal_ref):
    reach = BLOCK * ROWS

    def parts(cyl):
        return [
            (filt_ref[:, reach : 2 * reach], near_ref[:, columns(cyl)]),
            (filt_ref[:, 2 * reach :], x_ref[:reach, columns(cyl)]),
            (edge_ref[...], far_ref[:, columns(cyl)]),
        ]

    form_powers(parts, gain_ref, beam_ref, out_ref, cal_ref, 0)


def place_table_kernel(most_sets, me_ref, owner_ref, out_ref):
    n_owner, beams, width = out_ref.shape
    sets = owner_ref.shape[1]
    owner = owner_ref[...].astype(jnp.float32)
    set_of = lax.broadcasted_iota(jnp.int32, (beams, sets), 0) // SET_BEAMS
    lane = lax.broadcasted_iota(jnp.int32, (beams, sets), 1)
    own = jnp.sum(jnp.where(set_of == lane, owner, 0.0), axis=1, keepdims=True)
    same = jnp.logical_and(owner == own, lane < set_of)
    rank = jnp.sum(jnp.where(same, 1.0, 0.0), axis=1, keepdims=True)
    within = lax.broadcasted_iota(jnp.int32, (beams, 1), 0) % SET_BEAMS
    column = (own * most_sets + rank).astype(jnp.int32) * SET_BEAMS + within
    place = lax.broadcasted_iota(jnp.int32, (beams, width), 1)
    for k in range(n_owner):
        owner_k = me_ref[0] ^ k
        hit = (column - owner_k * width) == place
        out_ref[k] = jnp.where(hit, 1.0, 0.0).astype(jnp.bfloat16)


def place_kernel(mine_ref, other_ref, keep_ref, table_ref, *out_refs):
    total = mine_ref[...].astype(jnp.float32) + other_ref[...].astype(jnp.float32)
    total = (total * keep_ref[...].astype(jnp.float32)).astype(jnp.bfloat16)
    for k, out_ref in enumerate(out_refs):
        placed = jnp.dot(total, table_ref[k], preferred_element_type=jnp.float32)
        out_ref[...] = placed.astype(jnp.bfloat16)


def gather_kernel(n_owner, where_ref, *refs):
    late, near, far, out_ref = refs[:n_owner], refs[n_owner : 2 * n_owner], refs[2 * n_owner : -1], refs[-1]
    me = where_ref[0]

    def copy(block, frame, k):
        source = me ^ k
        rows = pl.ds(pl.multiple_of(source * UPCH, UPCH), UPCH)
        count = block.shape[0] // UPCH
        out_ref[frame : frame + count, rows, :] = block[...].reshape(count, UPCH, block.shape[1])

    @pl.when(where_ref[1] == 1)
    def _():
        for k in range(n_owner):
            copy(late[k], 0, k)

    @pl.when(where_ref[1] == 0)
    def _():
        for k in range(n_owner):
            copy(far[k], 0, k)
            copy(near[k], BLOCK, k)


VMEM = pl.BlockSpec(memory_space=pltpu.VMEM)
SMEM = pl.BlockSpec(memory_space=pltpu.SMEM)
ANY = pl.BlockSpec(memory_space=pl.ANY)


def call(body, out_shape, n_in, flops, nbytes, scalars=0, after=0, scratch=()):
    many = isinstance(out_shape, (list, tuple))

    def kernel(*refs):
        seen = scalars + n_in
        body(*refs[:seen], *refs[seen + after :])

    return pl.pallas_call(
        kernel,
        out_shape=out_shape,
        in_specs=[SMEM] * scalars + [VMEM] * n_in + [ANY] * after,
        out_specs=[VMEM] * len(out_shape) if many else VMEM,
        scratch_shapes=list(scratch),
        cost_estimate=pl.CostEstimate(flops=flops, bytes_accessed=nbytes, transcendentals=0),
        compiler_params=pltpu.CompilerParams(vmem_limit_bytes=40 << 20),
    )


def per_device(voltages, feed_gains, owner_table, keep_flags):
    samples = voltages[0, 0]
    gain = feed_gains[0, 0]
    frame_count = samples.shape[0] // UPCH
    kept = frame_count // 2
    n_owner = lax.axis_size("freq")
    assert voltages.shape[1] == 1 and kept == 2 * BLOCK and kept >= TAPS
    assert n_owner & (n_owner - 1) == 0
    n_tm = lax.axis_size("tm")
    me = lax.axis_index("freq")
    pol = lax.axis_index("pol")
    most_sets = 2 * owner_table.shape[0] // n_owner
    beams = keep_flags.shape[0]
    width = most_sets * SET_BEAMS
    bf16 = jnp.bfloat16
    filt = jnp.asarray(filter_matrix())
    edge = jnp.asarray(filter_matrix()[:, ROWS : BLOCK * ROWS])
    beam_table = jnp.asarray(beam_matrix())

    def ahead(part):
        return lax.ppermute(part, "tm", [(i, i + 1) for i in range(n_tm - 1)])

    def powers(body, frames, *args, after=()):
        rows = frames * UPCH
        flops = frames // BLOCK * 2 * 512 * 1024 * 1024
        shape = jax.ShapeDtypeStruct((rows, CYL * NS), bf16)
        scratch = [pltpu.VMEM((CYL * BLOCK * UPCH, 2 * NS), bf16)]
        return call(body, shape, len(args), flops, 3 << 20, after=len(after), scratch=scratch)(*args, *after)

    def swap(block, source):
        return lax.ppermute(block, "pol", [(source, 1 - source)])

    def regroup(mine, target, table):
        other = swap(mine, 1 - target)
        rows = mine.shape[0]
        shape = jax.ShapeDtypeStruct((rows, width), bf16)
        blocks = call(place_kernel, [shape] * n_owner, 4, 2 * rows * beams * beams * 2, 6 << 20)(
            mine, other, keep, table
        )
        got = [blocks[0]]
        for k in range(1, n_owner):
            route = [(i * 2 + target, (i ^ k) * 2 + target) for i in range(n_owner)]
            got.append(lax.ppermute(blocks[k], ("freq", "pol"), route))
        return got

    where = jnp.stack([me, pol]).astype(jnp.int32)
    keep = keep_flags.reshape(1, -1)
    x = samples.transpose(0, 2, 1, 3).reshape(samples.shape[0] * 2, CYL * NS)
    x = lax.optimization_barrier(x)
    length = x.shape[0]
    near_at = length - BLOCK * ROWS
    far_at = length - (TAPS - 1) * ROWS
    near = ahead(x[near_at:])
    far = ahead(x[far_at:near_at])

    late_powers = powers(
        functools.partial(local_kernel, kept // BLOCK, kept), kept, filt, x, gain, beam_table
    )
    table = call(
        functools.partial(place_table_kernel, most_sets),
        jax.ShapeDtypeStruct((n_owner, beams, width), bf16),
        1,
        1 << 24,
        4 << 20,
        scalars=1,
        after=1,
    )(where, owner_table.reshape(1, -1), late_powers)
    late = regroup(late_powers, 1, table)
    near_powers = powers(near_kernel, BLOCK, filt, near, x, gain, beam_table, after=late[:1])
    early_near = regroup(near_powers, 0, table)
    far_powers = powers(
        far_kernel, BLOCK, filt, edge, far, near, x, gain, beam_table, after=early_near[:1]
    )
    early_far = regroup(far_powers, 0, table)
    out_shape = jax.ShapeDtypeStruct((kept, n_owner * UPCH, width), bf16)
    return call(functools.partial(gather_kernel, n_owner), out_shape, 3 * n_owner, 0, 3 << 20, scalars=1)(
        where, *late, *early_near, *early_far
    )


def solution(mesh):
    return jax.shard_map(
        per_device,
        mesh=mesh,
        in_specs=(
            P("pol", ("grp", "freq"), "tm", None, None, None),
            P(("grp", "freq"), "pol", None, None, None),
            P(),
            P(),
        ),
        out_specs=P(("grp", "tm", "pol"), None, "freq"),
        check_vma=False,
    )
```

```python
import functools

import jax
import jax.numpy as jnp
import numpy as np
from jax import lax
from jax.experimental import pallas as pl
from jax.experimental.pallas import tpu as pltpu
from jax.sharding import PartitionSpec as P


NS = 256
CYL = 4
UPCH = 16
TAPS = 16
SET_BEAMS = 16
BLOCK = 8
LANES = 128
ROWS = 2 * UPCH


def window_taps():
    span = TAPS * UPCH
    steps = np.arange(span, dtype=np.float64)
    weights = np.sinc((steps - (span - 1) / 2.0) / UPCH) * np.sin(np.pi * (steps + 0.5) / span) ** 2
    return weights / np.sqrt(np.sum(weights * weights))


def filter_matrix():
    weights = window_taps()
    fine = np.arange(UPCH)
    sample = np.arange(TAPS * UPCH)
    phase = 2.0 * np.pi * ((fine[:, None] * sample[None, :]) % UPCH) / UPCH
    cosine = np.cos(phase) * weights
    sine = np.sin(phase) * weights
    table = np.zeros((2, BLOCK, UPCH, TAPS + BLOCK, UPCH, 2))
    for frame in range(BLOCK):
        taps = slice(frame + 1, frame + 1 + TAPS)
        cos_part = cosine.reshape(UPCH, TAPS, UPCH)
        sin_part = sine.reshape(UPCH, TAPS, UPCH)
        table[0, frame, :, taps, :, 0] = cos_part
        table[0, frame, :, taps, :, 1] = sin_part
        table[1, frame, :, taps, :, 0] = -sin_part
        table[1, frame, :, taps, :, 1] = cos_part
    table = table.reshape(2 * BLOCK * UPCH, (TAPS + BLOCK) * ROWS).astype(np.float32)
    high = table.astype(jnp.bfloat16)
    low = (table - high.astype(np.float32)).astype(jnp.bfloat16)
    return np.concatenate([high, low], axis=0)


def beam_matrix():
    rows = np.arange(NS)
    angle = 2.0 * np.pi * (rows[:, None] * rows[None, :] % NS) / NS
    scale = 1.0 / np.sqrt(NS)
    cosine = (np.cos(angle) * scale).astype(np.float32)
    sine = (np.sin(angle) * scale).astype(np.float32)
    upper = np.concatenate([cosine, -sine], axis=1)
    lower = np.concatenate([sine, cosine], axis=1)
    table = np.concatenate([upper, lower], axis=0).astype(jnp.bfloat16)
    table = table.reshape(2 * NS, 2, NS // LANES, LANES).transpose(0, 2, 1, 3).reshape(2 * NS, 2 * NS)
    return (table.astype(np.float32) * 0.5).astype(jnp.bfloat16)


def columns(cyl):
    return slice(cyl * NS, (cyl + 1) * NS)


def form_powers(parts, gain_ref, beam_ref, cal_ref, emit):
    half = BLOCK * UPCH
    for cyl in range(CYL):
        total = None
        for table, samples in parts(cyl):
            term = jnp.dot(table, samples, preferred_element_type=jnp.float32)
            total = term if total is None else total + term
        spec = total[: 2 * half] + total[2 * half :]
        real, imag = spec[:half], spec[half:]
        gain_real = gain_ref[cyl, 0:1, :]
        gain_imag = gain_ref[cyl, 1:2, :]
        rows = slice(cyl * half, (cyl + 1) * half)
        cal_ref[rows, :NS] = (real * gain_real - imag * gain_imag).astype(jnp.bfloat16)
        cal_ref[rows, NS:] = (real * gain_imag + imag * gain_real).astype(jnp.bfloat16)
    for strip in range(NS // LANES):
        beam = jnp.dot(
            cal_ref[...],
            beam_ref[:, strip * 2 * LANES : (strip + 1) * 2 * LANES],
            preferred_element_type=jnp.float32,
        )
        beams = [beam[cyl * half : (cyl + 1) * half] for cyl in range(CYL)]
        (r0, i0), (r1, i1), (r2, i2), (r3, i3) = [(b[:, :LANES], b[:, LANES:]) for b in beams]
        pr, pi, mr, mi = r0 + r2, i0 + i2, r0 - r2, i0 - i2
        sr, si, dr, di = r1 + r3, i1 + i3, r1 - r3, i1 - i3
        formed = [(pr + sr, pi + si), (mr + di, mi - dr), (pr - sr, pi - si), (mr - di, mi + dr)]
        for element, (fr, fi) in enumerate(formed):
            emit(element * NS + strip * LANES, fr * fr + fi * fi)


def sum_block(parts_of, gains, beam_ref, keep_ref, cal_ref, sum_ref, at):
    rows = pl.ds(at, BLOCK * UPCH)

    def first(column, power):
        sum_ref[rows, column : column + LANES] = power.astype(jnp.bfloat16)

    def second(column, power):
        lanes = slice(column, column + LANES)
        total = sum_ref[rows, lanes].astype(jnp.float32) + power.astype(jnp.bfloat16).astype(jnp.float32)
        sum_ref[rows, lanes] = (total * keep_ref[:, lanes].astype(jnp.float32)).astype(jnp.bfloat16)

    form_powers(parts_of(0), gains[0], beam_ref, cal_ref, first)
    form_powers(parts_of(1), gains[1], beam_ref, cal_ref, second)


def place(sum_ref, table_ref, out_refs, rows):
    for k, out_ref in enumerate(out_refs):
        placed = jnp.dot(sum_ref[...], table_ref[k], preferred_element_type=jnp.float32)
        out_ref[rows, :] = placed.astype(jnp.bfloat16)


def late_kernel(blocks, n_owner, where_ref, filt_ref, x0, x1, g0, g1, beam_ref, keep_ref, table_ref, *refs):
    out_refs, (cal_ref, sum_ref) = refs[:n_owner], refs[n_owner:]
    depth = (TAPS + BLOCK) * ROWS

    @pl.when(where_ref[1] == 1)
    def _():
        def step(block, carry):
            start = pl.multiple_of(block * BLOCK * ROWS, BLOCK * ROWS)

            def parts_of(pol):
                return lambda cyl: [(filt_ref[...], (x0, x1)[pol][pl.ds(start, depth), columns(cyl)])]

            at = pl.multiple_of(block * BLOCK * UPCH, BLOCK * UPCH)
            sum_block(parts_of, (g0, g1), beam_ref, keep_ref, cal_ref, sum_ref, at)
            return carry

        lax.fori_loop(0, blocks, step, 0)
        place(sum_ref, table_ref, out_refs, slice(None))


def near_kernel(n_owner, where_ref, filt_ref, n0, n1, x0, x1, g0, g1, beam_ref, keep_ref, table_ref, *refs):
    out_refs, (cal_ref, sum_ref) = refs[:n_owner], refs[n_owner:]
    reach = BLOCK * ROWS

    @pl.when(where_ref[1] == 0)
    def _():
        def parts_of(pol):
            near, x = (n0, n1)[pol], (x0, x1)[pol]
            return lambda cyl: [
                (filt_ref[:, :reach], near[:, columns(cyl)]),
                (filt_ref[:, reach:], x[: 2 * reach, columns(cyl)]),
            ]

        sum_block(parts_of, (g0, g1), beam_ref, keep_ref, cal_ref, sum_ref, 0)
        place(sum_ref, table_ref, out_refs, slice(None))


def far_kernel(
    n_owner, where_ref, filt_ref, edge_ref, f0, f1, n0, n1, x0, x1, g0, g1, beam_ref, keep_ref, table_ref, *refs
):
    near_refs, out_refs, (cal_ref, sum_ref) = refs[:n_owner], refs[n_owner : 2 * n_owner], refs[2 * n_owner :]
    reach = BLOCK * ROWS
    half = BLOCK * UPCH

    @pl.when(where_ref[1] == 0)
    def _():
        def parts_of(pol):
            far, near, x = (f0, f1)[pol], (n0, n1)[pol], (x0, x1)[pol]
            return lambda cyl: [
                (filt_ref[:, reach : 2 * reach], near[:, columns(cyl)]),
                (filt_ref[:, 2 * reach :], x[:reach, columns(cyl)]),
                (edge_ref[...], far[:, columns(cyl)]),
            ]

        sum_block(parts_of, (g0, g1), beam_ref, keep_ref, cal_ref, sum_ref, 0)
        place(sum_ref, table_ref, out_refs, slice(0, half))
        for near_ref, out_ref in zip(near_refs, out_refs):
            out_ref[half:, :] = near_ref[...]


def place_table_kernel(most_sets, where_ref, owner_ref, out_ref):
    n_owner, beams, width = out_ref.shape
    sets = owner_ref.shape[1]
    owner = owner_ref[...].astype(jnp.float32)
    set_of = lax.broadcasted_iota(jnp.int32, (beams, sets), 0) // SET_BEAMS
    lane = lax.broadcasted_iota(jnp.int32, (beams, sets), 1)
    own = jnp.sum(jnp.where(set_of == lane, owner, 0.0), axis=1, keepdims=True)
    same = jnp.logical_and(owner == own, lane < set_of)
    rank = jnp.sum(jnp.where(same, 1.0, 0.0), axis=1, keepdims=True)
    within = lax.broadcasted_iota(jnp.int32, (beams, 1), 0) % SET_BEAMS
    column = (own * most_sets + rank).astype(jnp.int32) * SET_BEAMS + within
    lane_at = lax.broadcasted_iota(jnp.int32, (beams, width), 1)
    for k in range(n_owner):
        owner_k = where_ref[0] ^ k
        hit = (column - owner_k * width) == lane_at
        out_ref[k] = jnp.where(hit, 1.0, 0.0).astype(jnp.bfloat16)


def gather_kernel(n_owner, where_ref, *refs):
    late, early, out_ref = refs[:n_owner], refs[n_owner : 2 * n_owner], refs[-1]
    for pol, blocks in enumerate((early, late)):

        @pl.when(where_ref[1] == pol)
        def _(blocks=blocks):
            for k, block in enumerate(blocks):
                source = where_ref[0] ^ k
                rows = pl.ds(pl.multiple_of(source * UPCH, UPCH), UPCH)
                count = block.shape[0] // UPCH
                out_ref[:, rows, :] = block[...].reshape(count, UPCH, block.shape[1])


VMEM = pl.BlockSpec(memory_space=pltpu.VMEM)
SMEM = pl.BlockSpec(memory_space=pltpu.SMEM)
ANY = pl.BlockSpec(memory_space=pl.ANY)


def call(body, out_shape, n_in, flops, nbytes, scalars=0, after=0, scratch=()):
    many = isinstance(out_shape, (list, tuple))

    def kernel(*refs):
        seen = scalars + n_in
        body(*refs[:seen], *refs[seen + after :])

    return pl.pallas_call(
        kernel,
        out_shape=out_shape,
        in_specs=[SMEM] * scalars + [VMEM] * n_in + [ANY] * after,
        out_specs=[VMEM] * len(out_shape) if many else VMEM,
        scratch_shapes=list(scratch),
        cost_estimate=pl.CostEstimate(flops=flops, bytes_accessed=nbytes, transcendentals=0),
        compiler_params=pltpu.CompilerParams(vmem_limit_bytes=40 << 20),
    )


def per_device(voltages, feed_gains, owner_table, keep_flags):
    samples = voltages[0, 0]
    gain = feed_gains[0, 0]
    frame_count = samples.shape[0] // UPCH
    kept = frame_count // 2
    n_owner = lax.axis_size("freq")
    assert voltages.shape[1] == 1 and kept == 2 * BLOCK and kept >= TAPS
    assert n_owner & (n_owner - 1) == 0
    n_tm = lax.axis_size("tm")
    me = lax.axis_index("freq")
    pol = lax.axis_index("pol")
    most_sets = 2 * owner_table.shape[0] // n_owner
    beams = keep_flags.shape[0]
    width = most_sets * SET_BEAMS
    bf16 = jnp.bfloat16
    filt = jnp.asarray(filter_matrix())
    edge = jnp.asarray(filter_matrix()[:, ROWS : BLOCK * ROWS])
    beam_table = jnp.asarray(beam_matrix())

    pairs = [(i, i + 1) for i in range(n_tm - 1)]

    def ahead(part, source):
        return lax.ppermute(part, ("tm", "pol"), [(i * 2 + source, j * 2) for i, j in pairs])

    def swap(part):
        return lax.ppermute(part, "pol", [(0, 1), (1, 0)])

    def spread(blocks, target):
        got = [blocks[0]]
        for k in range(1, n_owner):
            route = [(i * 2 + target, (i ^ k) * 2 + target) for i in range(n_owner)]
            got.append(lax.ppermute(blocks[k], ("freq", "pol"), route))
        return got

    def form(body, frames, rows_out, *args, after=()):
        flops = frames // BLOCK * 4 * 512 * 1024 * 1024
        shape = [jax.ShapeDtypeStruct((rows_out, width), bf16)] * n_owner
        scratch = [
            pltpu.VMEM((CYL * BLOCK * UPCH, 2 * NS), bf16),
            pltpu.VMEM((frames * UPCH, beams), bf16),
        ]
        return call(
            body, shape, len(args) - 1, flops, 4 << 20, scalars=1, after=len(after), scratch=scratch
        )(*args, *after)

    where = jnp.stack([me, pol]).astype(jnp.int32)
    keep = keep_flags.reshape(1, -1)
    gain_other = swap(gain)
    x = samples.transpose(0, 2, 1, 3).reshape(samples.shape[0] * 2, CYL * NS)
    x = lax.optimization_barrier(x)
    length = x.shape[0]
    near_at = length - BLOCK * ROWS
    far_at = length - (TAPS - 1) * ROWS
    near0 = ahead(x[near_at:], 0)
    near1 = ahead(x[near_at:], 1)
    x_other = swap(x)
    far0 = ahead(x[far_at:near_at], 0)
    far1 = ahead(x[far_at:near_at], 1)
    table = call(
        functools.partial(place_table_kernel, most_sets),
        jax.ShapeDtypeStruct((n_owner, beams, width), bf16),
        1,
        1 << 24,
        4 << 20,
        scalars=1,
    )(where, owner_table.reshape(1, -1))
    common = (gain, gain_other, beam_table, keep, table)
    body = functools.partial(late_kernel, kept // BLOCK, n_owner)
    late = form(body, kept, kept * UPCH, where, filt, x, x_other, *common)
    late_got = spread(late, 1)
    body = functools.partial(near_kernel, n_owner)
    near = form(body, BLOCK, BLOCK * UPCH, where, filt, near0, near1, x, x_other, *common, after=late[:1])
    body = functools.partial(far_kernel, n_owner)
    early = form(body, BLOCK, kept * UPCH, where, filt, edge, far0, far1, near0, near1, x, x_other, *common, *near)
    early_got = spread(early, 0)
    out_shape = jax.ShapeDtypeStruct((kept, n_owner * UPCH, width), bf16)
    return call(functools.partial(gather_kernel, n_owner), out_shape, 2 * n_owner, 0, 3 << 20, scalars=1)(
        where, *late_got, *early_got
    )


def solution(mesh):
    return jax.shard_map(
        per_device,
        mesh=mesh,
        in_specs=(
            P("pol", ("grp", "freq"), "tm", None, None, None),
            P(("grp", "freq"), "pol", None, None, None),
            P(),
            P(),
        ),
        out_specs=P(("grp", "tm", "pol"), None, "freq"),
        check_vma=False,
    )
```

```python
import functools

import jax
import jax.numpy as jnp
import numpy as np
from jax import lax
from jax.experimental import pallas as pl
from jax.experimental.pallas import tpu as pltpu
from jax.sharding import PartitionSpec as P


NS = 256
CYL = 4
UPCH = 16
TAPS = 16
SET_BEAMS = 16
BLOCK = 8
LANES = 128
ROWS = 2 * UPCH


def window_taps():
    span = TAPS * UPCH
    steps = np.arange(span, dtype=np.float64)
    weights = np.sinc((steps - (span - 1) / 2.0) / UPCH) * np.sin(np.pi * (steps + 0.5) / span) ** 2
    return weights / np.sqrt(np.sum(weights * weights))


def filter_matrix():
    weights = window_taps()
    fine = np.arange(UPCH)
    sample = np.arange(TAPS * UPCH)
    phase = 2.0 * np.pi * ((fine[:, None] * sample[None, :]) % UPCH) / UPCH
    cosine = np.cos(phase) * weights
    sine = np.sin(phase) * weights
    table = np.zeros((2, BLOCK, UPCH, TAPS + BLOCK, UPCH, 2))
    for frame in range(BLOCK):
        taps = slice(frame + 1, frame + 1 + TAPS)
        cos_part = cosine.reshape(UPCH, TAPS, UPCH)
        sin_part = sine.reshape(UPCH, TAPS, UPCH)
        table[0, frame, :, taps, :, 0] = cos_part
        table[0, frame, :, taps, :, 1] = sin_part
        table[1, frame, :, taps, :, 0] = -sin_part
        table[1, frame, :, taps, :, 1] = cos_part
    table = table.reshape(2 * BLOCK * UPCH, (TAPS + BLOCK) * ROWS).astype(np.float32)
    high = table.astype(jnp.bfloat16)
    low = (table - high.astype(np.float32)).astype(jnp.bfloat16)
    return np.concatenate([high, low], axis=0)


def beam_matrix():
    rows = np.arange(NS)
    angle = 2.0 * np.pi * (rows[:, None] * rows[None, :] % NS) / NS
    scale = 1.0 / np.sqrt(NS)
    cosine = (np.cos(angle) * scale).astype(np.float32)
    sine = (np.sin(angle) * scale).astype(np.float32)
    upper = np.concatenate([cosine, -sine], axis=1)
    lower = np.concatenate([sine, cosine], axis=1)
    table = np.concatenate([upper, lower], axis=0).astype(jnp.bfloat16)
    table = table.reshape(2 * NS, 2, NS // LANES, LANES).transpose(0, 2, 1, 3).reshape(2 * NS, 2 * NS)
    return (table.astype(np.float32) * 0.5).astype(jnp.bfloat16)


def form_powers(spectra, gain_ref, beam_ref, cal_ref, emit):
    half = BLOCK * UPCH
    for cyl in range(CYL):
        spec = spectra(cyl)
        real, imag = spec[:half], spec[half:]
        gain_real = gain_ref[cyl, 0:1, :]
        gain_imag = gain_ref[cyl, 1:2, :]
        rows = slice(cyl * half, (cyl + 1) * half)
        cal_ref[rows, :NS] = (real * gain_real - imag * gain_imag).astype(jnp.bfloat16)
        cal_ref[rows, NS:] = (real * gain_imag + imag * gain_real).astype(jnp.bfloat16)
    for strip in range(NS // LANES):
        beam = jnp.dot(
            cal_ref[...],
            beam_ref[:, strip * 2 * LANES : (strip + 1) * 2 * LANES],
            preferred_element_type=jnp.float32,
        )
        beams = [beam[cyl * half : (cyl + 1) * half] for cyl in range(CYL)]
        (r0, i0), (r1, i1), (r2, i2), (r3, i3) = [(b[:, :LANES], b[:, LANES:]) for b in beams]
        pr, pi, mr, mi = r0 + r2, i0 + i2, r0 - r2, i0 - i2
        sr, si, dr, di = r1 + r3, i1 + i3, r1 - r3, i1 - i3
        formed = [(pr + sr, pi + si), (mr + di, mi - dr), (pr - sr, pi - si), (mr - di, mi + dr)]
        for element, (fr, fi) in enumerate(formed):
            emit(element * NS + strip * LANES, fr * fr + fi * fi)


def filtered(table, x_ref, cyl, start, count):
    strips = NS // LANES
    rows = [
        x_ref[cyl * strips + strip, pl.ds(start, count)].reshape(2 * count, LANES) for strip in range(strips)
    ]
    both = jnp.dot(table, jnp.concatenate(rows, axis=1), preferred_element_type=jnp.float32)
    return both[: both.shape[0] // 2] + both[both.shape[0] // 2 :]


def fetches(source_ref, first, count, x_ref, at, sems):
    strips = NS // LANES
    return [
        pltpu.make_async_copy(
            source_ref.at[pl.ds(first, count), j // strips, :, pl.ds(j % strips * LANES, LANES)],
            x_ref.at[j, pl.ds(at, count)],
            sems.at[j],
        )
        for j in range(CYL * strips)
    ]


def start(copies):
    for copy in copies:
        copy.start()


def wait_cylinder(copies, cyl):
    strips = NS // LANES
    for copy in copies[cyl * strips : (cyl + 1) * strips]:
        copy.wait()


def adder(pol, sum_ref, keep_ref, at):
    rows = pl.ds(at, BLOCK * UPCH)

    def first(column, power):
        sum_ref[rows, column : column + LANES] = power.astype(jnp.bfloat16)

    def second(column, power):
        lanes = slice(column, column + LANES)
        total = sum_ref[rows, lanes].astype(jnp.float32) + power.astype(jnp.bfloat16).astype(jnp.float32)
        sum_ref[rows, lanes] = (total * keep_ref[:, lanes].astype(jnp.float32)).astype(jnp.bfloat16)

    return (first, second)[pol]


def place(sum_ref, table_ref, out_refs, rows):
    for k, out_ref in enumerate(out_refs):
        placed = jnp.dot(sum_ref[...], table_ref[k], preferred_element_type=jnp.float32)
        out_ref[rows, :] = placed.astype(jnp.bfloat16)


def late_kernel(blocks, n_owner, where_ref, filt_ref, g0, g1, beam_ref, keep_ref, table_ref, v0, v1, *refs):
    out_refs, (cal_ref, sum_ref, x0, x1, sems) = refs[:n_owner], refs[n_owner:]
    depth = (TAPS + BLOCK) * UPCH
    length = x0.shape[1]

    @pl.when(where_ref[1] == 1)
    def _():
        copies = [fetches(v, 0, length, x, 0, sems.at[pol]) for pol, (v, x) in enumerate(((v0, x0), (v1, x1)))]
        start(copies[0])
        start(copies[1])
        for pol, (x, gain) in enumerate(((x0, g0), (x1, g1))):

            def step(block, carry, pol=pol, x=x, gain=gain):
                at = pl.multiple_of(block * BLOCK * UPCH, BLOCK * UPCH)

                def spectra(cyl):
                    @pl.when(block == 0)
                    def _():
                        wait_cylinder(copies[pol], cyl)

                    return filtered(filt_ref[...], x, cyl, at, depth)

                form_powers(spectra, gain, beam_ref, cal_ref, adder(pol, sum_ref, keep_ref, at))
                return carry

            lax.fori_loop(0, blocks, step, 0)
        place(sum_ref, table_ref, out_refs, slice(None))


def near_kernel(n_owner, where_ref, filt_ref, g0, g1, beam_ref, keep_ref, table_ref, n0, n1, v0, v1, *refs):
    out_refs, pre_ref, (cal_ref, sum_ref, x0, x1, sems) = refs[:n_owner], refs[n_owner], refs[n_owner + 1 :]
    reach = BLOCK * UPCH

    @pl.when(where_ref[1] == 0)
    def _():
        copies = []
        for pol, (v, n, x) in enumerate(((v0, n0, x0), (v1, n1, x1))):
            here = fetches(v, 0, 2 * reach, x, reach, sems.at[pol, 0])
            there = fetches(n, 0, reach, x, 0, sems.at[pol, 1])
            for a, b in zip(here, there):
                a.start()
                b.start()
            copies.append((here, there))
        for pol, (x, gain) in enumerate(((x0, g0), (x1, g1))):

            def spectra(cyl, pol=pol, x=x):
                wait_cylinder(copies[pol][0], cyl)
                wait_cylinder(copies[pol][1], cyl)
                pre_ref[pol * CYL + cyl] = filtered(filt_ref[:, 2 * reach :], x, cyl, 0, 2 * reach)
                return filtered(filt_ref[...], x, cyl, 0, 3 * reach)

            form_powers(spectra, gain, beam_ref, cal_ref, adder(pol, sum_ref, keep_ref, 0))
        place(sum_ref, table_ref, out_refs, slice(None))


def far_kernel(n_owner, where_ref, filt_ref, g0, g1, beam_ref, keep_ref, table_ref, pre_ref, *refs):
    near_refs, (f0, f1), refs = refs[:n_owner], refs[n_owner : n_owner + 2], refs[n_owner + 2 :]
    out_refs, (cal_ref, sum_ref, x0, x1, sems) = refs[:n_owner], refs[n_owner:]
    half = BLOCK * UPCH
    reach = BLOCK * UPCH
    length = f0.shape[0]
    skip = reach - length

    @pl.when(where_ref[1] == 0)
    def _():
        for x in (x0, x1):
            x[:, :skip] = jnp.zeros((x.shape[0], skip, *x.shape[2:]), x.dtype)
        copies = [fetches(f, 0, length, x, skip, sems.at[pol]) for pol, (f, x) in enumerate(((f0, x0), (f1, x1)))]
        start(copies[0])
        start(copies[1])
        for near_ref, out_ref in zip(near_refs, out_refs):
            out_ref[half:, :] = near_ref[...]
        for pol, (x, gain) in enumerate(((x0, g0), (x1, g1))):

            def spectra(cyl, pol=pol, x=x):
                wait_cylinder(copies[pol], cyl)
                return pre_ref[pol * CYL + cyl] + filtered(filt_ref[:, : 2 * reach], x, cyl, 0, reach)

            form_powers(spectra, gain, beam_ref, cal_ref, adder(pol, sum_ref, keep_ref, 0))
        place(sum_ref, table_ref, out_refs, slice(0, half))


def place_table_kernel(most_sets, where_ref, owner_ref, out_ref):
    n_owner, beams, width = out_ref.shape
    sets = owner_ref.shape[1]
    owner = owner_ref[...].astype(jnp.float32)
    set_of = lax.broadcasted_iota(jnp.int32, (beams, sets), 0) // SET_BEAMS
    lane = lax.broadcasted_iota(jnp.int32, (beams, sets), 1)
    own = jnp.sum(jnp.where(set_of == lane, owner, 0.0), axis=1, keepdims=True)
    same = jnp.logical_and(owner == own, lane < set_of)
    rank = jnp.sum(jnp.where(same, 1.0, 0.0), axis=1, keepdims=True)
    within = lax.broadcasted_iota(jnp.int32, (beams, 1), 0) % SET_BEAMS
    column = (own * most_sets + rank).astype(jnp.int32) * SET_BEAMS + within
    lane_at = lax.broadcasted_iota(jnp.int32, (beams, width), 1)
    for k in range(n_owner):
        owner_k = where_ref[0] ^ k
        hit = (column - owner_k * width) == lane_at
        out_ref[k] = jnp.where(hit, 1.0, 0.0).astype(jnp.bfloat16)


def gather_kernel(n_owner, where_ref, *refs):
    late, early, out_ref = refs[:n_owner], refs[n_owner : 2 * n_owner], refs[-1]
    for pol, blocks in enumerate((early, late)):

        @pl.when(where_ref[1] == pol)
        def _(blocks=blocks):
            for k, block in enumerate(blocks):
                source = where_ref[0] ^ k
                rows = pl.ds(pl.multiple_of(source * UPCH, UPCH), UPCH)
                count = block.shape[0] // UPCH
                out_ref[:, rows, :] = block[...].reshape(count, UPCH, block.shape[1])


VMEM = pl.BlockSpec(memory_space=pltpu.VMEM)
SMEM = pl.BlockSpec(memory_space=pltpu.SMEM)
ANY = pl.BlockSpec(memory_space=pl.ANY)


def call(body, out_shape, n_in, flops, nbytes, scalars=0, whole=0, after=0, scratch=()):
    many = isinstance(out_shape, (list, tuple))

    def kernel(*refs):
        seen = scalars + n_in + whole
        body(*refs[:seen], *refs[seen + after :])

    return pl.pallas_call(
        kernel,
        out_shape=out_shape,
        in_specs=[SMEM] * scalars + [VMEM] * n_in + [ANY] * (whole + after),
        out_specs=[VMEM] * len(out_shape) if many else VMEM,
        scratch_shapes=list(scratch),
        cost_estimate=pl.CostEstimate(flops=flops, bytes_accessed=nbytes, transcendentals=0),
        compiler_params=pltpu.CompilerParams(vmem_limit_bytes=40 << 20),
    )


def per_device(voltages, feed_gains, owner_table, keep_flags):
    samples = voltages[0, 0]
    gain = feed_gains[0, 0]
    frame_count = samples.shape[0] // UPCH
    kept = frame_count // 2
    n_owner = lax.axis_size("freq")
    assert voltages.shape[1] == 1 and kept == 2 * BLOCK and kept >= TAPS
    assert n_owner & (n_owner - 1) == 0
    n_tm = lax.axis_size("tm")
    me = lax.axis_index("freq")
    pol = lax.axis_index("pol")
    most_sets = 2 * owner_table.shape[0] // n_owner
    beams = keep_flags.shape[0]
    width = most_sets * SET_BEAMS
    bf16 = jnp.bfloat16
    filt = jnp.asarray(filter_matrix())
    beam_table = jnp.asarray(beam_matrix())

    pairs = [(i, i + 1) for i in range(n_tm - 1)]

    def ahead(part, source):
        return lax.ppermute(part, ("tm", "pol"), [(i * 2 + source, j * 2) for i, j in pairs])

    def swap(part):
        return lax.ppermute(part, "pol", [(0, 1), (1, 0)])

    def spread(blocks, target):
        got = [blocks[0]]
        for k in range(1, n_owner):
            route = [(i * 2 + target, (i ^ k) * 2 + target) for i in range(n_owner)]
            got.append(lax.ppermute(blocks[k], ("freq", "pol"), route))
        return got

    def form(body, frames, rows_out, held, sem_shape, arrays, raw, after=(), more=()):
        flops = frames // BLOCK * 4 * 512 * 1024 * 1024
        shape = [jax.ShapeDtypeStruct((rows_out, width), bf16)] * n_owner
        strips = CYL * NS // LANES
        scratch = [
            pltpu.VMEM((CYL * BLOCK * UPCH, 2 * NS), bf16),
            pltpu.VMEM((frames * UPCH, beams), bf16),
            pltpu.VMEM((strips, held, 2, LANES), bf16),
            pltpu.VMEM((strips, held, 2, LANES), bf16),
            pltpu.SemaphoreType.DMA(sem_shape + (strips,)),
        ]
        return call(
            body,
            shape + list(more),
            len(arrays),
            flops,
            4 << 20,
            scalars=1,
            whole=len(raw),
            after=len(after),
            scratch=scratch,
        )(where, *arrays, *raw, *after)

    where = jnp.stack([me, pol]).astype(jnp.int32)
    keep = keep_flags.reshape(1, -1)
    length = samples.shape[0]
    near_at = length - BLOCK * UPCH
    far_at = length - (TAPS - 1) * UPCH
    near0 = ahead(samples[near_at:], 0)
    near1 = ahead(samples[near_at:], 1)
    other = swap(samples)
    gain_other = swap(gain)
    far0 = ahead(samples[far_at:near_at], 0)
    far1 = ahead(samples[far_at:near_at], 1)
    table = call(
        functools.partial(place_table_kernel, most_sets),
        jax.ShapeDtypeStruct((n_owner, beams, width), bf16),
        1,
        1 << 24,
        4 << 20,
        scalars=1,
    )(where, owner_table.reshape(1, -1))
    common = (gain, gain_other, beam_table, keep, table)
    late = form(
        functools.partial(late_kernel, kept // BLOCK, n_owner),
        kept,
        kept * UPCH,
        length,
        (2,),
        (filt, *common),
        (samples, other),
    )
    late_got = spread(late, 1)
    reach = BLOCK * UPCH
    *near, pre = form(
        functools.partial(near_kernel, n_owner),
        BLOCK,
        reach,
        3 * reach,
        (2, 2),
        (filt, *common),
        (near0, near1, samples, other),
        after=late[:1],
        more=[jax.ShapeDtypeStruct((2 * CYL, 2 * reach, NS), jnp.float32)],
    )
    early = form(
        functools.partial(far_kernel, n_owner),
        BLOCK,
        kept * UPCH,
        reach,
        (2,),
        (filt, *common, pre, *near),
        (far0, far1),
    )
    early_got = spread(early, 0)
    out_shape = jax.ShapeDtypeStruct((kept, n_owner * UPCH, width), bf16)
    return call(functools.partial(gather_kernel, n_owner), out_shape, 2 * n_owner, 0, 3 << 20, scalars=1)(
        where, *late_got, *early_got
    )


def solution(mesh):
    return jax.shard_map(
        per_device,
        mesh=mesh,
        in_specs=(
            P("pol", ("grp", "freq"), "tm", None, None, None),
            P(("grp", "freq"), "pol", None, None, None),
            P(),
            P(),
        ),
        out_specs=P(("grp", "tm", "pol"), None, "freq"),
        check_vma=False,
    )
```

```python
import functools

import jax
import jax.numpy as jnp
import numpy as np
from jax import lax
from jax.experimental import pallas as pl
from jax.experimental.pallas import tpu as pltpu
from jax.sharding import PartitionSpec as P


NS = 256
CYL = 4
UPCH = 16
TAPS = 16
SET_BEAMS = 16
BLOCK = 8
LANES = 128
ROWS = 2 * UPCH


def window_taps():
    span = TAPS * UPCH
    steps = np.arange(span, dtype=np.float64)
    weights = np.sinc((steps - (span - 1) / 2.0) / UPCH) * np.sin(np.pi * (steps + 0.5) / span) ** 2
    return weights / np.sqrt(np.sum(weights * weights))


def filter_matrix():
    weights = window_taps()
    fine = np.arange(UPCH)
    sample = np.arange(TAPS * UPCH)
    phase = 2.0 * np.pi * ((fine[:, None] * sample[None, :]) % UPCH) / UPCH
    cosine = np.cos(phase) * weights
    sine = np.sin(phase) * weights
    table = np.zeros((2, BLOCK, UPCH, TAPS + BLOCK, UPCH, 2))
    for frame in range(BLOCK):
        taps = slice(frame + 1, frame + 1 + TAPS)
        cos_part = cosine.reshape(UPCH, TAPS, UPCH)
        sin_part = sine.reshape(UPCH, TAPS, UPCH)
        table[0, frame, :, taps, :, 0] = cos_part
        table[0, frame, :, taps, :, 1] = sin_part
        table[1, frame, :, taps, :, 0] = -sin_part
        table[1, frame, :, taps, :, 1] = cos_part
    table = table.reshape(2 * BLOCK * UPCH, (TAPS + BLOCK) * ROWS).astype(np.float32)
    high = table.astype(jnp.bfloat16)
    low = (table - high.astype(np.float32)).astype(jnp.bfloat16)
    return np.concatenate([high, low], axis=0)


def beam_matrix():
    rows = np.arange(NS)
    angle = 2.0 * np.pi * (rows[:, None] * rows[None, :] % NS) / NS
    scale = 1.0 / np.sqrt(NS)
    cosine = (np.cos(angle) * scale).astype(np.float32)
    sine = (np.sin(angle) * scale).astype(np.float32)
    upper = np.concatenate([cosine, -sine], axis=1)
    lower = np.concatenate([sine, cosine], axis=1)
    table = np.concatenate([upper, lower], axis=0).astype(jnp.bfloat16)
    table = table.reshape(2 * NS, 2, NS // LANES, LANES).transpose(0, 2, 1, 3).reshape(2 * NS, 2 * NS)
    return (table.astype(np.float32) * 0.5).astype(jnp.bfloat16)


def columns(cyl):
    return slice(cyl * NS, (cyl + 1) * NS)


def form_powers(spectra, gain_ref, beam_ref, cal_ref, emit):
    half = BLOCK * UPCH
    for cyl in range(CYL):
        spec = spectra(cyl)
        real, imag = spec[:half], spec[half:]
        gain_real = gain_ref[cyl, 0:1, :]
        gain_imag = gain_ref[cyl, 1:2, :]
        rows = slice(cyl * half, (cyl + 1) * half)
        cal_ref[rows, :NS] = (real * gain_real - imag * gain_imag).astype(jnp.bfloat16)
        cal_ref[rows, NS:] = (real * gain_imag + imag * gain_real).astype(jnp.bfloat16)
    for strip in range(NS // LANES):
        beam = jnp.dot(
            cal_ref[...],
            beam_ref[:, strip * 2 * LANES : (strip + 1) * 2 * LANES],
            preferred_element_type=jnp.float32,
        )
        beams = [beam[cyl * half : (cyl + 1) * half] for cyl in range(CYL)]
        (r0, i0), (r1, i1), (r2, i2), (r3, i3) = [(b[:, :LANES], b[:, LANES:]) for b in beams]
        pr, pi, mr, mi = r0 + r2, i0 + i2, r0 - r2, i0 - i2
        sr, si, dr, di = r1 + r3, i1 + i3, r1 - r3, i1 - i3
        formed = [(pr + sr, pi + si), (mr + di, mi - dr), (pr - sr, pi - si), (mr - di, mi + dr)]
        for element, (fr, fi) in enumerate(formed):
            emit(element * NS + strip * LANES, fr * fr + fi * fi)


def filtered(terms):
    both = None
    for table, rows in terms:
        term = jnp.dot(table, rows, preferred_element_type=jnp.float32)
        both = term if both is None else both + term
    return both[: both.shape[0] // 2] + both[both.shape[0] // 2 :]


def adder(pol, sum_ref, keep_ref):
    def first(column, power):
        sum_ref[:, column : column + LANES] = power.astype(jnp.bfloat16)

    def second(column, power):
        lanes = slice(column, column + LANES)
        total = sum_ref[:, lanes].astype(jnp.float32) + power.astype(jnp.bfloat16).astype(jnp.float32)
        sum_ref[:, lanes] = (total * keep_ref[:, lanes].astype(jnp.float32)).astype(jnp.bfloat16)

    return (first, second)[pol]


def place(sum_ref, table_ref, out_refs):
    for k, out_ref in enumerate(out_refs):
        placed = jnp.dot(sum_ref[...], table_ref[k], preferred_element_type=jnp.float32)
        out_ref[...] = placed.astype(jnp.bfloat16)


def rows_kernel(first, v_ref, out_ref, held_ref, sems):
    count = held_ref.shape[1]
    strips = NS // LANES
    copies = [
        pltpu.make_async_copy(
            v_ref.at[pl.ds(first, count), j // strips, :, pl.ds(j % strips * LANES, LANES)],
            held_ref.at[j],
            sems.at[j],
        )
        for j in range(CYL * strips)
    ]
    for copy in copies:
        copy.start()
    for j, copy in enumerate(copies):
        copy.wait()
        out_ref[:, j * LANES : (j + 1) * LANES] = held_ref[j].reshape(2 * count, LANES)


def late_kernel(block, n_owner, where_ref, filt_ref, x0, x1, g0, g1, beam_ref, keep_ref, table_ref, *refs):
    out_refs, (cal_ref, sum_ref) = refs[:n_owner], refs[n_owner:]
    rows = slice(block * BLOCK * ROWS, (block * BLOCK + TAPS + BLOCK) * ROWS)

    @pl.when(where_ref[1] == 0)
    def _():
        for pol, (x, gain) in enumerate(((x0, g0), (x1, g1))):

            def spectra(cyl, x=x):
                return filtered([(filt_ref[...], x[rows, columns(cyl)])])

            form_powers(spectra, gain, beam_ref, cal_ref, adder(pol, sum_ref, keep_ref))
        place(sum_ref, table_ref, out_refs)


def near_kernel(n_owner, where_ref, filt_ref, n0, n1, x0, x1, g0, g1, beam_ref, keep_ref, table_ref, *refs):
    out_refs, pre_ref, (cal_ref, sum_ref) = refs[:n_owner], refs[n_owner], refs[n_owner + 1 :]
    reach = BLOCK * ROWS

    @pl.when(where_ref[1] == 1)
    def _():
        for pol, (n, x, gain) in enumerate(((n0, x0, g0), (n1, x1, g1))):

            def spectra(cyl, pol=pol, n=n, x=x):
                there = n[:, columns(cyl)]
                pre_ref[pol * CYL + cyl] = filtered(
                    [(filt_ref[:, reach : 2 * reach], there), (filt_ref[:, 2 * reach :], x[:reach, columns(cyl)])]
                )
                return filtered([(filt_ref[:, :reach], there), (filt_ref[:, reach:], x[: 2 * reach, columns(cyl)])])

            form_powers(spectra, gain, beam_ref, cal_ref, adder(pol, sum_ref, keep_ref))
        place(sum_ref, table_ref, out_refs)


def far_kernel(n_owner, where_ref, edge_ref, f0, f1, g0, g1, beam_ref, keep_ref, table_ref, pre_ref, *refs):
    own_refs, out_refs, own_ref, (cal_ref, sum_ref) = refs[:3], refs[3 : 3 + n_owner], refs[3 + n_owner], refs[-2:]
    half = BLOCK * UPCH

    @pl.when(where_ref[1] == 1)
    def _():
        for pol, (f, gain) in enumerate(((f0, g0), (f1, g1))):

            def spectra(cyl, pol=pol, f=f):
                return pre_ref[pol * CYL + cyl] + filtered([(edge_ref[...], f[:, columns(cyl)])])

            form_powers(spectra, gain, beam_ref, cal_ref, adder(pol, sum_ref, keep_ref))
        place(sum_ref, table_ref, out_refs)
        own_ref[:half, :] = out_refs[0][...]
        own_ref[half:, :] = own_refs[0][...]

    @pl.when(where_ref[1] == 0)
    def _():
        own_ref[:half, :] = own_refs[1][...]
        own_ref[half:, :] = own_refs[2][...]


def place_table_kernel(most_sets, where_ref, owner_ref, out_ref):
    n_owner, beams, width = out_ref.shape
    sets = owner_ref.shape[1]
    owner = owner_ref[...].astype(jnp.float32)
    set_of = lax.broadcasted_iota(jnp.int32, (beams, sets), 0) // SET_BEAMS
    lane = lax.broadcasted_iota(jnp.int32, (beams, sets), 1)
    own = jnp.sum(jnp.where(set_of == lane, owner, 0.0), axis=1, keepdims=True)
    same = jnp.logical_and(owner == own, lane < set_of)
    rank = jnp.sum(jnp.where(same, 1.0, 0.0), axis=1, keepdims=True)
    within = lax.broadcasted_iota(jnp.int32, (beams, 1), 0) % SET_BEAMS
    column = (own * most_sets + rank).astype(jnp.int32) * SET_BEAMS + within
    lane_at = lax.broadcasted_iota(jnp.int32, (beams, width), 1)
    for k in range(n_owner):
        owner_k = where_ref[0] ^ k
        hit = (column - owner_k * width) == lane_at
        out_ref[k] = jnp.where(hit, 1.0, 0.0).astype(jnp.bfloat16)


def gather_kernel(n_owner, where_ref, *refs):
    own_ref, got, out_ref = refs[0], refs[1:-1], refs[-1]
    chunks = [got[i * (n_owner - 1) : (i + 1) * (n_owner - 1)] for i in range(4)]

    def copy(block, frame, k):
        rows = pl.ds(pl.multiple_of((where_ref[0] ^ k) * UPCH, UPCH), UPCH)
        count = block.shape[0] // UPCH
        out_ref[frame : frame + count, rows, :] = block[...].reshape(count, UPCH, block.shape[1])

    copy(own_ref, 0, 0)
    for pol in range(2):

        @pl.when(where_ref[1] == pol)
        def _(pol=pol):
            for part in range(2):
                for k in range(1, n_owner):
                    copy(chunks[2 * pol + part][k - 1], part * BLOCK, k)


VMEM = pl.BlockSpec(memory_space=pltpu.VMEM)
SMEM = pl.BlockSpec(memory_space=pltpu.SMEM)
ANY = pl.BlockSpec(memory_space=pl.ANY)


def call(body, out_shape, n_in, flops, nbytes, scalars=0, whole=0, after=0, scratch=()):
    many = isinstance(out_shape, (list, tuple))

    def kernel(*refs):
        seen = scalars + n_in + whole
        body(*refs[:seen], *refs[seen + after :])

    return pl.pallas_call(
        kernel,
        out_shape=out_shape,
        in_specs=[SMEM] * scalars + [VMEM] * n_in + [ANY] * (whole + after),
        out_specs=[VMEM] * len(out_shape) if many else VMEM,
        scratch_shapes=list(scratch),
        cost_estimate=pl.CostEstimate(flops=flops, bytes_accessed=nbytes, transcendentals=0),
        compiler_params=pltpu.CompilerParams(vmem_limit_bytes=40 << 20),
    )


def per_device(voltages, feed_gains, owner_table, keep_flags):
    samples = voltages[0, 0]
    gain = feed_gains[0, 0]
    frame_count = samples.shape[0] // UPCH
    kept = frame_count // 2
    n_owner = lax.axis_size("freq")
    assert voltages.shape[1] == 1 and kept == 2 * BLOCK and kept >= TAPS
    assert n_owner & (n_owner - 1) == 0
    n_tm = lax.axis_size("tm")
    me = lax.axis_index("freq")
    pol = lax.axis_index("pol")
    most_sets = 2 * owner_table.shape[0] // n_owner
    beams = keep_flags.shape[0]
    width = most_sets * SET_BEAMS
    bf16 = jnp.bfloat16
    filt = jnp.asarray(filter_matrix())
    edge = jnp.asarray(filter_matrix()[:, ROWS : BLOCK * ROWS])
    beam_table = jnp.asarray(beam_matrix())

    pairs = [(i, i + 1) for i in range(n_tm - 1)]

    def ahead(part, source):
        return lax.ppermute(part, ("tm", "pol"), [(i * 2 + source, j * 2 + 1) for i, j in pairs])

    def swap(part):
        return lax.ppermute(part, "pol", [(0, 1), (1, 0)])

    def spread(blocks, source):
        got = []
        for k in range(1, n_owner):
            route = [(i * 2 + source, (i ^ k) * 2 + 1 - source) for i in range(n_owner)]
            got.append(lax.ppermute(blocks[k], ("freq", "pol"), route))
        return got

    def form(body, *arrays, after=(), more=()):
        shape = [jax.ShapeDtypeStruct((BLOCK * UPCH, width), bf16)] * n_owner
        scratch = [pltpu.VMEM((CYL * BLOCK * UPCH, 2 * NS), bf16), pltpu.VMEM((BLOCK * UPCH, beams), bf16)]
        return call(
            body,
            shape + list(more),
            len(arrays),
            4 * 512 * 1024 * 1024,
            4 << 20,
            scalars=1,
            after=len(after),
            scratch=scratch,
        )(where, *arrays, *after)

    where = jnp.stack([me, pol]).astype(jnp.int32)
    keep = keep_flags.reshape(1, -1)
    count = BLOCK * UPCH
    near_rows = call(
        functools.partial(rows_kernel, samples.shape[0] - count),
        jax.ShapeDtypeStruct((BLOCK * ROWS, CYL * NS), bf16),
        0,
        0,
        1 << 20,
        whole=1,
        scratch=[pltpu.VMEM((CYL * NS // LANES, count, 2, LANES), bf16), pltpu.SemaphoreType.DMA((CYL * NS // LANES,))],
    )(samples)
    near0 = ahead(near_rows, 0)
    near1 = ahead(near_rows, 1)
    x = samples.transpose(0, 2, 1, 3).reshape(samples.shape[0] * 2, CYL * NS)
    x = lax.optimization_barrier(x)
    other = swap(x)
    gain_other = swap(gain)
    far_rows = x[x.shape[0] - (TAPS - 1) * ROWS : x.shape[0] - BLOCK * ROWS]
    far0 = ahead(far_rows, 0)
    far1 = ahead(far_rows, 1)
    table = call(
        functools.partial(place_table_kernel, most_sets),
        jax.ShapeDtypeStruct((n_owner, beams, width), bf16),
        1,
        1 << 24,
        4 << 20,
        scalars=1,
    )(where, owner_table.reshape(1, -1))
    common = (gain, gain_other, beam_table, keep, table)
    late = []
    got = []
    for block in range(2):
        body = functools.partial(late_kernel, block, n_owner)
        after = [late[0][0]] if block else []
        late.append(form(body, filt, x, other, *common, after=after))
        got.append(spread(late[block], 0))
    *near, pre = form(
        functools.partial(near_kernel, n_owner),
        filt,
        near1,
        near0,
        x,
        other,
        *common,
        after=late[1][:1],
        more=[jax.ShapeDtypeStruct((2 * CYL, BLOCK * ROWS, NS), jnp.float32)],
    )
    near_got = spread(near, 1)
    *far, own = form(
        functools.partial(far_kernel, n_owner),
        edge,
        far1,
        far0,
        *common,
        pre,
        near[0],
        late[0][0],
        late[1][0],
        more=[jax.ShapeDtypeStruct((kept * UPCH, width), bf16)],
    )
    far_got = spread(far, 1)
    own_got = swap(own)
    out_shape = jax.ShapeDtypeStruct((kept, n_owner * UPCH, width), bf16)
    arrays = [own_got, *far_got, *near_got, *got[0], *got[1]]
    return call(functools.partial(gather_kernel, n_owner), out_shape, len(arrays), 0, 3 << 20, scalars=1)(
        where, *arrays
    )


def solution(mesh):
    return jax.shard_map(
        per_device,
        mesh=mesh,
        in_specs=(
            P("pol", ("grp", "freq"), "tm", None, None, None),
            P(("grp", "freq"), "pol", None, None, None),
            P(),
            P(),
        ),
        out_specs=P(("grp", "tm", "pol"), None, "freq"),
        check_vma=False,
    )
```

```python
import functools

import jax
import jax.numpy as jnp
import numpy as np
from jax import lax
from jax.experimental import pallas as pl
from jax.experimental.pallas import tpu as pltpu
from jax.sharding import PartitionSpec as P


NS = 256
CYL = 4
UPCH = 16
TAPS = 16
SET_BEAMS = 16
BLOCK = 8
LANES = 128
ROWS = 2 * UPCH


def window_taps():
    span = TAPS * UPCH
    steps = np.arange(span, dtype=np.float64)
    weights = np.sinc((steps - (span - 1) / 2.0) / UPCH) * np.sin(np.pi * (steps + 0.5) / span) ** 2
    return weights / np.sqrt(np.sum(weights * weights))


def filter_matrix():
    weights = window_taps()
    fine = np.arange(UPCH)
    sample = np.arange(TAPS * UPCH)
    phase = 2.0 * np.pi * ((fine[:, None] * sample[None, :]) % UPCH) / UPCH
    cosine = np.cos(phase) * weights
    sine = np.sin(phase) * weights
    table = np.zeros((2, BLOCK, UPCH, TAPS + BLOCK, UPCH, 2))
    for frame in range(BLOCK):
        taps = slice(frame + 1, frame + 1 + TAPS)
        cos_part = cosine.reshape(UPCH, TAPS, UPCH)
        sin_part = sine.reshape(UPCH, TAPS, UPCH)
        table[0, frame, :, taps, :, 0] = cos_part
        table[0, frame, :, taps, :, 1] = sin_part
        table[1, frame, :, taps, :, 0] = -sin_part
        table[1, frame, :, taps, :, 1] = cos_part
    table = table.reshape(2 * BLOCK * UPCH, (TAPS + BLOCK) * ROWS).astype(np.float32)
    high = table.astype(jnp.bfloat16)
    low = (table - high.astype(np.float32)).astype(jnp.bfloat16)
    return np.concatenate([high, low], axis=0)


def beam_matrix():
    rows = np.arange(NS)
    angle = 2.0 * np.pi * (rows[:, None] * rows[None, :] % NS) / NS
    scale = 1.0 / np.sqrt(NS)
    cosine = (np.cos(angle) * scale).astype(np.float32)
    sine = (np.sin(angle) * scale).astype(np.float32)
    upper = np.concatenate([cosine, -sine], axis=1)
    lower = np.concatenate([sine, cosine], axis=1)
    table = np.concatenate([upper, lower], axis=0).astype(jnp.bfloat16)
    table = table.reshape(2 * NS, 2, NS // LANES, LANES).transpose(0, 2, 1, 3).reshape(2 * NS, 2 * NS)
    return (table.astype(np.float32) * 0.5).astype(jnp.bfloat16)


def columns(cyl):
    return slice(cyl * NS, (cyl + 1) * NS)


def form_powers(spectra, gain_ref, beam_ref, cal_ref, emit):
    half = BLOCK * UPCH
    for cyl in range(CYL):
        spec = spectra(cyl)
        real, imag = spec[:half], spec[half:]
        gain_real = gain_ref[cyl, 0:1, :]
        gain_imag = gain_ref[cyl, 1:2, :]
        rows = slice(cyl * half, (cyl + 1) * half)
        cal_ref[rows, :NS] = (real * gain_real - imag * gain_imag).astype(jnp.bfloat16)
        cal_ref[rows, NS:] = (real * gain_imag + imag * gain_real).astype(jnp.bfloat16)
    for strip in range(NS // LANES):
        beam = jnp.dot(
            cal_ref[...],
            beam_ref[:, strip * 2 * LANES : (strip + 1) * 2 * LANES],
            preferred_element_type=jnp.float32,
        )
        beams = [beam[cyl * half : (cyl + 1) * half] for cyl in range(CYL)]
        (r0, i0), (r1, i1), (r2, i2), (r3, i3) = [(b[:, :LANES], b[:, LANES:]) for b in beams]
        pr, pi, mr, mi = r0 + r2, i0 + i2, r0 - r2, i0 - i2
        sr, si, dr, di = r1 + r3, i1 + i3, r1 - r3, i1 - i3
        formed = [(pr + sr, pi + si), (mr + di, mi - dr), (pr - sr, pi - si), (mr - di, mi + dr)]
        for element, (fr, fi) in enumerate(formed):
            emit(element * NS + strip * LANES, fr * fr + fi * fi)


def filtered(terms):
    both = None
    for table, rows in terms:
        term = jnp.dot(table, rows, preferred_element_type=jnp.float32)
        both = term if both is None else both + term
    return both[: both.shape[0] // 2] + both[both.shape[0] // 2 :]


def adder(pol, sum_ref, keep_ref):
    def first(column, power):
        sum_ref[:, column : column + LANES] = power.astype(jnp.bfloat16)

    def second(column, power):
        lanes = slice(column, column + LANES)
        total = sum_ref[:, lanes].astype(jnp.float32) + power.astype(jnp.bfloat16).astype(jnp.float32)
        sum_ref[:, lanes] = (total * keep_ref[:, lanes].astype(jnp.float32)).astype(jnp.bfloat16)

    return (first, second)[pol]


def place(sum_ref, table_ref, out_refs):
    for k, out_ref in enumerate(out_refs):
        placed = jnp.dot(sum_ref[...], table_ref[k], preferred_element_type=jnp.float32)
        out_ref[...] = placed.astype(jnp.bfloat16)


def halo_rows_kernel(x_ref, near_ref, far_ref):
    near_at = x_ref.shape[0] - near_ref.shape[0]
    near_ref[...] = x_ref[near_at:, :]
    far_ref[...] = x_ref[near_at - far_ref.shape[0] : near_at, :]


def late_kernel(block, n_owner, where_ref, filt_ref, x0, x1, g0, g1, beam_ref, keep_ref, table_ref, *refs):
    out_refs, (cal_ref, sum_ref) = refs[:n_owner], refs[n_owner:]
    rows = slice(block * BLOCK * ROWS, (block * BLOCK + TAPS + BLOCK) * ROWS)

    @pl.when(where_ref[1] == 0)
    def _():
        for pol, (x, gain) in enumerate(((x0, g0), (x1, g1))):

            def spectra(cyl, x=x):
                return filtered([(filt_ref[...], x[rows, columns(cyl)])])

            form_powers(spectra, gain, beam_ref, cal_ref, adder(pol, sum_ref, keep_ref))
        place(sum_ref, table_ref, out_refs)


def near_kernel(n_owner, where_ref, filt_ref, n0, n1, x0, x1, g0, g1, beam_ref, keep_ref, table_ref, *refs):
    out_refs, pre_ref, (cal_ref, sum_ref) = refs[:n_owner], refs[n_owner], refs[n_owner + 1 :]
    reach = BLOCK * ROWS

    @pl.when(where_ref[1] == 1)
    def _():
        for pol, (n, x, gain) in enumerate(((n0, x0, g0), (n1, x1, g1))):

            def spectra(cyl, pol=pol, n=n, x=x):
                there = n[:, columns(cyl)]
                pre_ref[pol * CYL + cyl] = filtered(
                    [(filt_ref[:, reach : 2 * reach], there), (filt_ref[:, 2 * reach :], x[:reach, columns(cyl)])]
                )
                return filtered([(filt_ref[:, :reach], there), (filt_ref[:, reach:], x[: 2 * reach, columns(cyl)])])

            form_powers(spectra, gain, beam_ref, cal_ref, adder(pol, sum_ref, keep_ref))
        place(sum_ref, table_ref, out_refs)


def far_kernel(n_owner, where_ref, edge_ref, f0, f1, g0, g1, beam_ref, keep_ref, table_ref, pre_ref, *refs):
    own_refs, out_refs, own_ref, (cal_ref, sum_ref) = refs[:3], refs[3 : 3 + n_owner], refs[3 + n_owner], refs[-2:]
    half = BLOCK * UPCH

    @pl.when(where_ref[1] == 1)
    def _():
        for pol, (f, gain) in enumerate(((f0, g0), (f1, g1))):

            def spectra(cyl, pol=pol, f=f):
                return pre_ref[pol * CYL + cyl] + filtered([(edge_ref[...], f[:, columns(cyl)])])

            form_powers(spectra, gain, beam_ref, cal_ref, adder(pol, sum_ref, keep_ref))
        place(sum_ref, table_ref, out_refs)
        own_ref[:half, :] = out_refs[0][...]
        own_ref[half:, :] = own_refs[0][...]

    @pl.when(where_ref[1] == 0)
    def _():
        own_ref[:half, :] = own_refs[1][...]
        own_ref[half:, :] = own_refs[2][...]


def place_table_kernel(most_sets, where_ref, owner_ref, out_ref):
    n_owner, beams, width = out_ref.shape
    sets = owner_ref.shape[1]
    owner = owner_ref[...].astype(jnp.float32)
    set_of = lax.broadcasted_iota(jnp.int32, (beams, sets), 0) // SET_BEAMS
    lane = lax.broadcasted_iota(jnp.int32, (beams, sets), 1)
    own = jnp.sum(jnp.where(set_of == lane, owner, 0.0), axis=1, keepdims=True)
    same = jnp.logical_and(owner == own, lane < set_of)
    rank = jnp.sum(jnp.where(same, 1.0, 0.0), axis=1, keepdims=True)
    within = lax.broadcasted_iota(jnp.int32, (beams, 1), 0) % SET_BEAMS
    column = (own * most_sets + rank).astype(jnp.int32) * SET_BEAMS + within
    lane_at = lax.broadcasted_iota(jnp.int32, (beams, width), 1)
    for k in range(n_owner):
        owner_k = where_ref[0] ^ k
        hit = (column - owner_k * width) == lane_at
        out_ref[k] = jnp.where(hit, 1.0, 0.0).astype(jnp.bfloat16)


def gather_kernel(n_owner, where_ref, *refs):
    own_ref, got, out_ref = refs[0], refs[1:-1], refs[-1]
    chunks = [got[i * (n_owner - 1) : (i + 1) * (n_owner - 1)] for i in range(4)]

    def copy(block, frame, k):
        rows = pl.ds(pl.multiple_of((where_ref[0] ^ k) * UPCH, UPCH), UPCH)
        count = block.shape[0] // UPCH
        out_ref[frame : frame + count, rows, :] = block[...].reshape(count, UPCH, block.shape[1])

    copy(own_ref, 0, 0)
    for pol in range(2):

        @pl.when(where_ref[1] == pol)
        def _(pol=pol):
            for part in range(2):
                for k in range(1, n_owner):
                    copy(chunks[2 * pol + part][k - 1], part * BLOCK, k)


VMEM = pl.BlockSpec(memory_space=pltpu.VMEM)
SMEM = pl.BlockSpec(memory_space=pltpu.SMEM)
ANY = pl.BlockSpec(memory_space=pl.ANY)


def call(body, out_shape, n_in, flops, nbytes, scalars=0, whole=0, after=0, scratch=()):
    many = isinstance(out_shape, (list, tuple))

    def kernel(*refs):
        seen = scalars + n_in + whole
        body(*refs[:seen], *refs[seen + after :])

    return pl.pallas_call(
        kernel,
        out_shape=out_shape,
        in_specs=[SMEM] * scalars + [VMEM] * n_in + [ANY] * (whole + after),
        out_specs=[VMEM] * len(out_shape) if many else VMEM,
        scratch_shapes=list(scratch),
        cost_estimate=pl.CostEstimate(flops=flops, bytes_accessed=nbytes, transcendentals=0),
        compiler_params=pltpu.CompilerParams(vmem_limit_bytes=24 << 20),
    )


def per_device(voltages, feed_gains, owner_table, keep_flags):
    samples = voltages[0, 0]
    gain = feed_gains[0, 0]
    frame_count = samples.shape[0] // UPCH
    kept = frame_count // 2
    n_owner = lax.axis_size("freq")
    assert voltages.shape[1] == 1 and kept == 2 * BLOCK and kept >= TAPS
    assert n_owner & (n_owner - 1) == 0
    n_tm = lax.axis_size("tm")
    me = lax.axis_index("freq")
    pol = lax.axis_index("pol")
    most_sets = 2 * owner_table.shape[0] // n_owner
    beams = keep_flags.shape[0]
    width = most_sets * SET_BEAMS
    bf16 = jnp.bfloat16
    filt = jnp.asarray(filter_matrix())
    edge = jnp.asarray(filter_matrix()[:, ROWS : BLOCK * ROWS])
    beam_table = jnp.asarray(beam_matrix())

    pairs = [(i, i + 1) for i in range(n_tm - 1)]

    def ahead(part, source):
        return lax.ppermute(part, ("tm", "pol"), [(i * 2 + source, j * 2 + 1) for i, j in pairs])

    def swap(part):
        return lax.ppermute(part, "pol", [(0, 1), (1, 0)])

    def spread(blocks, source):
        got = []
        for k in range(1, n_owner):
            route = [(i * 2 + source, (i ^ k) * 2 + 1 - source) for i in range(n_owner)]
            got.append(lax.ppermute(blocks[k], ("freq", "pol"), route))
        return got

    def form(body, *arrays, after=(), more=()):
        shape = [jax.ShapeDtypeStruct((BLOCK * UPCH, width), bf16)] * n_owner
        scratch = [pltpu.VMEM((CYL * BLOCK * UPCH, 2 * NS), bf16), pltpu.VMEM((BLOCK * UPCH, beams), bf16)]
        return call(
            body,
            shape + list(more),
            len(arrays),
            4 * 512 * 1024 * 1024,
            4 << 20,
            scalars=1,
            after=len(after),
            scratch=scratch,
        )(where, *arrays, *after)

    where = jnp.stack([me, pol]).astype(jnp.int32)
    keep = keep_flags.reshape(1, -1)
    reach, edge_rows = BLOCK * ROWS, (TAPS - 1 - BLOCK) * ROWS
    table = call(
        functools.partial(place_table_kernel, most_sets),
        jax.ShapeDtypeStruct((n_owner, beams, width), bf16),
        1,
        1 << 24,
        4 << 20,
        scalars=1,
    )(where, owner_table.reshape(1, -1))
    samples, table = lax.optimization_barrier((samples, table))
    x = samples.transpose(0, 2, 1, 3).reshape(samples.shape[0] * 2, CYL * NS)
    x = lax.optimization_barrier(x)
    near_rows, far_rows = call(
        halo_rows_kernel,
        [jax.ShapeDtypeStruct((rows, CYL * NS), bf16) for rows in (reach, edge_rows)],
        1,
        0,
        2 << 20,
    )(x)
    near0 = ahead(near_rows, 0)
    near1 = ahead(near_rows, 1)
    other = swap(x)
    gain_other = swap(gain)
    far0 = ahead(far_rows, 0)
    far1 = ahead(far_rows, 1)
    common = (gain, gain_other, beam_table, keep, table)
    late = []
    got = []
    for block in range(2):
        body = functools.partial(late_kernel, block, n_owner)
        after = [late[0][0]] if block else []
        late.append(form(body, filt, x, other, *common, after=after))
        got.append(spread(late[block], 0))
    *near, pre = form(
        functools.partial(near_kernel, n_owner),
        filt,
        near1,
        near0,
        x,
        other,
        *common,
        after=late[1][:1],
        more=[jax.ShapeDtypeStruct((2 * CYL, reach, NS), jnp.float32)],
    )
    near_got = spread(near, 1)
    *far, own = form(
        functools.partial(far_kernel, n_owner),
        edge,
        far1,
        far0,
        *common,
        pre,
        near[0],
        late[0][0],
        late[1][0],
        more=[jax.ShapeDtypeStruct((kept * UPCH, width), bf16)],
    )
    far_got = spread(far, 1)
    own_got = swap(own)
    out_shape = jax.ShapeDtypeStruct((kept, n_owner * UPCH, width), bf16)
    arrays = [own_got, *far_got, *near_got, *got[0], *got[1]]
    return call(functools.partial(gather_kernel, n_owner), out_shape, len(arrays), 0, 3 << 20, scalars=1)(
        where, *arrays
    )


def solution(mesh):
    return jax.shard_map(
        per_device,
        mesh=mesh,
        in_specs=(
            P("pol", ("grp", "freq"), "tm", None, None, None),
            P(("grp", "freq"), "pol", None, None, None),
            P(),
            P(),
        ),
        out_specs=P(("grp", "tm", "pol"), None, "freq"),
        check_vma=False,
    )
```

```python
import functools

import jax
import jax.numpy as jnp
import numpy as np
from jax import lax
from jax.experimental import pallas as pl
from jax.experimental.pallas import tpu as pltpu
from jax.sharding import PartitionSpec as P


NS = 256
CYL = 4
UPCH = 16
TAPS = 16
SET_BEAMS = 16
BLOCK = 8
LANES = 128
ROWS = 2 * UPCH


def window_taps():
    span = TAPS * UPCH
    steps = np.arange(span, dtype=np.float64)
    weights = np.sinc((steps - (span - 1) / 2.0) / UPCH) * np.sin(np.pi * (steps + 0.5) / span) ** 2
    return weights / np.sqrt(np.sum(weights * weights))


def filter_matrix():
    weights = window_taps()
    fine = np.arange(UPCH)
    sample = np.arange(TAPS * UPCH)
    phase = 2.0 * np.pi * ((fine[:, None] * sample[None, :]) % UPCH) / UPCH
    cosine = np.cos(phase) * weights
    sine = np.sin(phase) * weights
    table = np.zeros((2, BLOCK, UPCH, TAPS + BLOCK, UPCH, 2))
    for frame in range(BLOCK):
        taps = slice(frame + 1, frame + 1 + TAPS)
        cos_part = cosine.reshape(UPCH, TAPS, UPCH)
        sin_part = sine.reshape(UPCH, TAPS, UPCH)
        table[0, frame, :, taps, :, 0] = cos_part
        table[0, frame, :, taps, :, 1] = sin_part
        table[1, frame, :, taps, :, 0] = -sin_part
        table[1, frame, :, taps, :, 1] = cos_part
    return table.reshape(2 * BLOCK * UPCH, (TAPS + BLOCK) * ROWS).astype(np.float32).astype(jnp.bfloat16)


def beam_matrix():
    rows = np.arange(NS)
    angle = 2.0 * np.pi * (rows[:, None] * rows[None, :] % NS) / NS
    scale = 1.0 / np.sqrt(NS)
    cosine = (np.cos(angle) * scale).astype(np.float32)
    sine = (np.sin(angle) * scale).astype(np.float32)
    upper = np.concatenate([cosine, -sine], axis=1)
    lower = np.concatenate([sine, cosine], axis=1)
    table = np.concatenate([upper, lower], axis=0).astype(jnp.bfloat16)
    table = table.reshape(2 * NS, 2, NS // LANES, LANES).transpose(0, 2, 1, 3).reshape(2 * NS, 2 * NS)
    return (table.astype(np.float32) * 0.5).astype(jnp.bfloat16)


def columns(cyl):
    return slice(cyl * NS, (cyl + 1) * NS)


def form_powers(spectra, gain_ref, beam_ref, cal_ref, emit):
    half = BLOCK * UPCH
    for cyl in range(CYL):
        spec = spectra(cyl)
        real, imag = spec[:half], spec[half:]
        gain_real = gain_ref[cyl, 0:1, :]
        gain_imag = gain_ref[cyl, 1:2, :]
        rows = slice(cyl * half, (cyl + 1) * half)
        cal_ref[rows, :NS] = (real * gain_real - imag * gain_imag).astype(jnp.bfloat16)
        cal_ref[rows, NS:] = (real * gain_imag + imag * gain_real).astype(jnp.bfloat16)
    for strip in range(NS // LANES):
        beam = jnp.dot(
            cal_ref[...],
            beam_ref[:, strip * 2 * LANES : (strip + 1) * 2 * LANES],
            preferred_element_type=jnp.float32,
        )
        beams = [beam[cyl * half : (cyl + 1) * half] for cyl in range(CYL)]
        (r0, i0), (r1, i1), (r2, i2), (r3, i3) = [(b[:, :LANES], b[:, LANES:]) for b in beams]
        pr, pi, mr, mi = r0 + r2, i0 + i2, r0 - r2, i0 - i2
        sr, si, dr, di = r1 + r3, i1 + i3, r1 - r3, i1 - i3
        formed = [(pr + sr, pi + si), (mr + di, mi - dr), (pr - sr, pi - si), (mr - di, mi + dr)]
        for element, (fr, fi) in enumerate(formed):
            emit(element * NS + strip * LANES, fr * fr + fi * fi)


def filtered(terms):
    total = None
    for table, rows in terms:
        term = jnp.dot(table, rows, preferred_element_type=jnp.float32)
        total = term if total is None else total + term
    return total


def adder(pol, sum_ref, keep_ref):
    def first(column, power):
        sum_ref[:, column : column + LANES] = power.astype(jnp.bfloat16)

    def second(column, power):
        lanes = slice(column, column + LANES)
        total = sum_ref[:, lanes].astype(jnp.float32) + power.astype(jnp.bfloat16).astype(jnp.float32)
        sum_ref[:, lanes] = (total * keep_ref[:, lanes].astype(jnp.float32)).astype(jnp.bfloat16)

    return (first, second)[pol]


def place(sum_ref, table_ref, out_refs):
    for k, out_ref in enumerate(out_refs):
        placed = jnp.dot(sum_ref[...], table_ref[k], preferred_element_type=jnp.float32)
        out_ref[...] = placed.astype(jnp.bfloat16)


def halo_rows_kernel(x_ref, near_ref, far_ref):
    near_at = x_ref.shape[0] - near_ref.shape[0]
    near_ref[...] = x_ref[near_at:, :]
    far_ref[...] = x_ref[near_at - far_ref.shape[0] : near_at, :]


def late_kernel(block, n_owner, where_ref, filt_ref, x0, x1, g0, g1, beam_ref, keep_ref, table_ref, *refs):
    out_refs, (cal_ref, sum_ref) = refs[:n_owner], refs[n_owner:]
    rows = slice(block * BLOCK * ROWS, (block * BLOCK + TAPS + BLOCK) * ROWS)

    @pl.when(where_ref[1] == 0)
    def _():
        for pol, (x, gain) in enumerate(((x0, g0), (x1, g1))):

            def spectra(cyl, x=x):
                return filtered([(filt_ref[...], x[rows, columns(cyl)])])

            form_powers(spectra, gain, beam_ref, cal_ref, adder(pol, sum_ref, keep_ref))
        place(sum_ref, table_ref, out_refs)


def near_kernel(n_owner, where_ref, filt_ref, n0, n1, x0, x1, g0, g1, beam_ref, keep_ref, table_ref, *refs):
    out_refs, pre_ref, (cal_ref, sum_ref) = refs[:n_owner], refs[n_owner], refs[n_owner + 1 :]
    reach = BLOCK * ROWS

    @pl.when(where_ref[1] == 1)
    def _():
        for pol, (n, x, gain) in enumerate(((n0, x0, g0), (n1, x1, g1))):

            def spectra(cyl, pol=pol, n=n, x=x):
                there = n[:, columns(cyl)]
                pre_ref[pol * CYL + cyl] = filtered(
                    [(filt_ref[:, reach : 2 * reach], there), (filt_ref[:, 2 * reach :], x[:reach, columns(cyl)])]
                )
                return filtered([(filt_ref[:, :reach], there), (filt_ref[:, reach:], x[: 2 * reach, columns(cyl)])])

            form_powers(spectra, gain, beam_ref, cal_ref, adder(pol, sum_ref, keep_ref))
        place(sum_ref, table_ref, out_refs)


def far_kernel(n_owner, where_ref, edge_ref, f0, f1, g0, g1, beam_ref, keep_ref, table_ref, pre_ref, *refs):
    own_refs, out_refs, own_ref, (cal_ref, sum_ref) = refs[:3], refs[3 : 3 + n_owner], refs[3 + n_owner], refs[-2:]
    half = BLOCK * UPCH

    @pl.when(where_ref[1] == 1)
    def _():
        for pol, (f, gain) in enumerate(((f0, g0), (f1, g1))):

            def spectra(cyl, pol=pol, f=f):
                return pre_ref[pol * CYL + cyl] + filtered([(edge_ref[...], f[:, columns(cyl)])])

            form_powers(spectra, gain, beam_ref, cal_ref, adder(pol, sum_ref, keep_ref))
        place(sum_ref, table_ref, out_refs)
        own_ref[:half, :] = out_refs[0][...]
        own_ref[half:, :] = own_refs[0][...]

    @pl.when(where_ref[1] == 0)
    def _():
        own_ref[:half, :] = own_refs[1][...]
        own_ref[half:, :] = own_refs[2][...]


def place_table_kernel(most_sets, where_ref, owner_ref, out_ref):
    n_owner, beams, width = out_ref.shape
    sets = owner_ref.shape[1]
    owner = owner_ref[...].astype(jnp.float32)
    set_of = lax.broadcasted_iota(jnp.int32, (beams, sets), 0) // SET_BEAMS
    lane = lax.broadcasted_iota(jnp.int32, (beams, sets), 1)
    own = jnp.sum(jnp.where(set_of == lane, owner, 0.0), axis=1, keepdims=True)
    same = jnp.logical_and(owner == own, lane < set_of)
    rank = jnp.sum(jnp.where(same, 1.0, 0.0), axis=1, keepdims=True)
    within = lax.broadcasted_iota(jnp.int32, (beams, 1), 0) % SET_BEAMS
    column = (own * most_sets + rank).astype(jnp.int32) * SET_BEAMS + within
    lane_at = lax.broadcasted_iota(jnp.int32, (beams, width), 1)
    for k in range(n_owner):
        owner_k = where_ref[0] ^ k
        hit = (column - owner_k * width) == lane_at
        out_ref[k] = jnp.where(hit, 1.0, 0.0).astype(jnp.bfloat16)


def gather_kernel(n_owner, where_ref, *refs):
    own_ref, got, out_ref = refs[0], refs[1:-1], refs[-1]
    chunks = [got[i * (n_owner - 1) : (i + 1) * (n_owner - 1)] for i in range(4)]

    def copy(block, frame, k):
        rows = pl.ds(pl.multiple_of((where_ref[0] ^ k) * UPCH, UPCH), UPCH)
        count = block.shape[0] // UPCH
        out_ref[frame : frame + count, rows, :] = block[...].reshape(count, UPCH, block.shape[1])

    copy(own_ref, 0, 0)
    for pol in range(2):

        @pl.when(where_ref[1] == pol)
        def _(pol=pol):
            for part in range(2):
                for k in range(1, n_owner):
                    copy(chunks[2 * pol + part][k - 1], part * BLOCK, k)


VMEM = pl.BlockSpec(memory_space=pltpu.VMEM)
SMEM = pl.BlockSpec(memory_space=pltpu.SMEM)
ANY = pl.BlockSpec(memory_space=pl.ANY)


def call(body, out_shape, n_in, flops, nbytes, scalars=0, whole=0, after=0, scratch=()):
    many = isinstance(out_shape, (list, tuple))

    def kernel(*refs):
        seen = scalars + n_in + whole
        body(*refs[:seen], *refs[seen + after :])

    return pl.pallas_call(
        kernel,
        out_shape=out_shape,
        in_specs=[SMEM] * scalars + [VMEM] * n_in + [ANY] * (whole + after),
        out_specs=[VMEM] * len(out_shape) if many else VMEM,
        scratch_shapes=list(scratch),
        cost_estimate=pl.CostEstimate(flops=flops, bytes_accessed=nbytes, transcendentals=0),
        compiler_params=pltpu.CompilerParams(vmem_limit_bytes=24 << 20),
    )


def per_device(voltages, feed_gains, owner_table, keep_flags):
    samples = voltages[0, 0]
    gain = feed_gains[0, 0]
    frame_count = samples.shape[0] // UPCH
    kept = frame_count // 2
    n_owner = lax.axis_size("freq")
    assert voltages.shape[1] == 1 and kept == 2 * BLOCK and kept >= TAPS
    assert n_owner & (n_owner - 1) == 0
    n_tm = lax.axis_size("tm")
    me = lax.axis_index("freq")
    pol = lax.axis_index("pol")
    most_sets = 2 * owner_table.shape[0] // n_owner
    beams = keep_flags.shape[0]
    width = most_sets * SET_BEAMS
    bf16 = jnp.bfloat16
    filt = jnp.asarray(filter_matrix())
    edge = jnp.asarray(filter_matrix()[:, ROWS : BLOCK * ROWS])
    beam_table = jnp.asarray(beam_matrix())

    pairs = [(i, i + 1) for i in range(n_tm - 1)]

    def ahead(part, source):
        return lax.ppermute(part, ("tm", "pol"), [(i * 2 + source, j * 2 + 1) for i, j in pairs])

    def swap(part):
        return lax.ppermute(part, "pol", [(0, 1), (1, 0)])

    def spread(blocks, source):
        got = []
        for k in range(1, n_owner):
            route = [(i * 2 + source, (i ^ k) * 2 + 1 - source) for i in range(n_owner)]
            got.append(lax.ppermute(blocks[k], ("freq", "pol"), route))
        return got

    def form(body, *arrays, after=(), more=()):
        shape = [jax.ShapeDtypeStruct((BLOCK * UPCH, width), bf16)] * n_owner
        scratch = [pltpu.VMEM((CYL * BLOCK * UPCH, 2 * NS), bf16), pltpu.VMEM((BLOCK * UPCH, beams), bf16)]
        return call(
            body,
            shape + list(more),
            len(arrays),
            4 * 512 * 1024 * 1024,
            4 << 20,
            scalars=1,
            after=len(after),
            scratch=scratch,
        )(where, *arrays, *after)

    where = jnp.stack([me, pol]).astype(jnp.int32)
    keep = keep_flags.reshape(1, -1)
    reach, edge_rows = BLOCK * ROWS, (TAPS - 1 - BLOCK) * ROWS
    table = call(
        functools.partial(place_table_kernel, most_sets),
        jax.ShapeDtypeStruct((n_owner, beams, width), bf16),
        1,
        1 << 24,
        4 << 20,
        scalars=1,
    )(where, owner_table.reshape(1, -1))
    samples, table = lax.optimization_barrier((samples, table))
    x = samples.transpose(0, 2, 1, 3).reshape(samples.shape[0] * 2, CYL * NS)
    x = lax.optimization_barrier(x)
    near_rows, far_rows = call(
        halo_rows_kernel,
        [jax.ShapeDtypeStruct((rows, CYL * NS), bf16) for rows in (reach, edge_rows)],
        1,
        0,
        2 << 20,
    )(x)
    near0 = ahead(near_rows, 0)
    near1 = ahead(near_rows, 1)
    other = swap(x)
    gain_other = swap(gain)
    far0 = ahead(far_rows, 0)
    far1 = ahead(far_rows, 1)
    common = (gain, gain_other, beam_table, keep, table)
    late = []
    got = []
    for block in range(2):
        body = functools.partial(late_kernel, block, n_owner)
        after = [late[0][0]] if block else []
        late.append(form(body, filt, x, other, *common, after=after))
        got.append(spread(late[block], 0))
    *near, pre = form(
        functools.partial(near_kernel, n_owner),
        filt,
        near1,
        near0,
        x,
        other,
        *common,
        after=late[1][:1],
        more=[jax.ShapeDtypeStruct((2 * CYL, reach, NS), jnp.float32)],
    )
    near_got = spread(near, 1)
    *far, own = form(
        functools.partial(far_kernel, n_owner),
        edge,
        far1,
        far0,
        *common,
        pre,
        near[0],
        late[0][0],
        late[1][0],
        more=[jax.ShapeDtypeStruct((kept * UPCH, width), bf16)],
    )
    far_got = spread(far, 1)
    own_got = swap(own)
    out_shape = jax.ShapeDtypeStruct((kept, n_owner * UPCH, width), bf16)
    arrays = [own_got, *far_got, *near_got, *got[0], *got[1]]
    return call(functools.partial(gather_kernel, n_owner), out_shape, len(arrays), 0, 3 << 20, scalars=1)(
        where, *arrays
    )


def solution(mesh):
    return jax.shard_map(
        per_device,
        mesh=mesh,
        in_specs=(
            P("pol", ("grp", "freq"), "tm", None, None, None),
            P(("grp", "freq"), "pol", None, None, None),
            P(),
            P(),
        ),
        out_specs=P(("grp", "tm", "pol"), None, "freq"),
        check_vma=False,
    )
```

```python
import functools

import jax
import jax.numpy as jnp
import numpy as np
from jax import lax
from jax.experimental import pallas as pl
from jax.experimental.pallas import tpu as pltpu
from jax.sharding import PartitionSpec as P


NS = 256
CYL = 4
UPCH = 16
TAPS = 16
SET_BEAMS = 16
BLOCK = 8
LANES = 128
ROWS = 2 * UPCH


def window_taps():
    span = TAPS * UPCH
    steps = np.arange(span, dtype=np.float64)
    weights = np.sinc((steps - (span - 1) / 2.0) / UPCH) * np.sin(np.pi * (steps + 0.5) / span) ** 2
    return weights / np.sqrt(np.sum(weights * weights))


def filter_matrix():
    weights = window_taps()
    fine = np.arange(UPCH)
    sample = np.arange(TAPS * UPCH)
    phase = 2.0 * np.pi * ((fine[:, None] * sample[None, :]) % UPCH) / UPCH
    cosine = np.cos(phase) * weights
    sine = np.sin(phase) * weights
    table = np.zeros((2, BLOCK, UPCH, TAPS + BLOCK, UPCH, 2))
    for frame in range(BLOCK):
        taps = slice(frame + 1, frame + 1 + TAPS)
        cos_part = cosine.reshape(UPCH, TAPS, UPCH)
        sin_part = sine.reshape(UPCH, TAPS, UPCH)
        table[0, frame, :, taps, :, 0] = cos_part
        table[0, frame, :, taps, :, 1] = sin_part
        table[1, frame, :, taps, :, 0] = -sin_part
        table[1, frame, :, taps, :, 1] = cos_part
    return table.reshape(2 * BLOCK * UPCH, (TAPS + BLOCK) * ROWS).astype(np.float32).astype(jnp.bfloat16)


def beam_matrix():
    rows = np.arange(NS)
    angle = 2.0 * np.pi * (rows[:, None] * rows[None, :] % NS) / NS
    scale = 1.0 / np.sqrt(NS)
    cosine = (np.cos(angle) * scale).astype(np.float32)
    sine = (np.sin(angle) * scale).astype(np.float32)
    upper = np.concatenate([cosine, -sine], axis=1)
    lower = np.concatenate([sine, cosine], axis=1)
    table = np.concatenate([upper, lower], axis=0).astype(jnp.bfloat16)
    table = table.reshape(2 * NS, 2, NS // LANES, LANES).transpose(0, 2, 1, 3).reshape(2 * NS, 2 * NS)
    return (table.astype(np.float32) * 0.5).astype(jnp.bfloat16)


def columns(cyl):
    return slice(cyl * NS, (cyl + 1) * NS)


def form_powers(spectra, gain_ref, beam_ref, cal_ref, emit):
    half = BLOCK * UPCH
    for cyl in range(CYL):
        spec = spectra(cyl)
        real, imag = spec[:half], spec[half:]
        gain_real = gain_ref[cyl, 0:1, :]
        gain_imag = gain_ref[cyl, 1:2, :]
        rows = slice(cyl * half, (cyl + 1) * half)
        cal_ref[rows, :NS] = (real * gain_real - imag * gain_imag).astype(jnp.bfloat16)
        cal_ref[rows, NS:] = (real * gain_imag + imag * gain_real).astype(jnp.bfloat16)
    for strip in range(NS // LANES):
        beam = jnp.dot(
            cal_ref[...],
            beam_ref[:, strip * 2 * LANES : (strip + 1) * 2 * LANES],
            preferred_element_type=jnp.float32,
        )
        beams = [beam[cyl * half : (cyl + 1) * half] for cyl in range(CYL)]
        (r0, i0), (r1, i1), (r2, i2), (r3, i3) = [(b[:, :LANES], b[:, LANES:]) for b in beams]
        pr, pi, mr, mi = r0 + r2, i0 + i2, r0 - r2, i0 - i2
        sr, si, dr, di = r1 + r3, i1 + i3, r1 - r3, i1 - i3
        formed = [(pr + sr, pi + si), (mr + di, mi - dr), (pr - sr, pi - si), (mr - di, mi + dr)]
        for element, (fr, fi) in enumerate(formed):
            emit(element * NS + strip * LANES, fr * fr + fi * fi)


def filtered(terms):
    total = None
    for table, rows in terms:
        term = jnp.dot(table, rows, preferred_element_type=jnp.float32)
        total = term if total is None else total + term
    return total


def keeper(power_ref, at=0):
    rows = pl.ds(at, BLOCK * UPCH)

    def emit(column, power):
        power_ref[rows, column : column + LANES] = power.astype(jnp.bfloat16)

    return emit


def adder(power_ref, keep_ref, sum_ref, at=0):
    rows = pl.ds(at, BLOCK * UPCH)

    def emit(column, power):
        lanes = slice(column, column + LANES)
        total = power_ref[rows, lanes].astype(jnp.float32) + power.astype(jnp.bfloat16).astype(jnp.float32)
        sum_ref[rows, lanes] = (total * keep_ref[:, lanes].astype(jnp.float32)).astype(jnp.bfloat16)

    return emit


def place(sum_ref, table_ref, out_refs):
    for k, out_ref in enumerate(out_refs):
        placed = jnp.dot(sum_ref[...], table_ref[k], preferred_element_type=jnp.float32)
        out_ref[...] = placed.astype(jnp.bfloat16)


def halo_rows_kernel(x_ref, near_ref, far_ref):
    near_at = x_ref.shape[0] - near_ref.shape[0]
    near_ref[...] = x_ref[near_at:, :]
    far_ref[...] = x_ref[near_at - far_ref.shape[0] : near_at, :]


def each_late_block(blocks, filt_ref, x_ref, gain_ref, beam_ref, cal_ref, emitter):
    def step(block, carry):
        first = pl.multiple_of(block * BLOCK * ROWS, BLOCK * ROWS)
        rows = pl.ds(first, (TAPS + BLOCK) * ROWS)

        def spectra(cyl):
            return filtered([(filt_ref[...], x_ref[rows, columns(cyl)])])

        at = pl.multiple_of(block * BLOCK * UPCH, BLOCK * UPCH)
        form_powers(spectra, gain_ref, beam_ref, cal_ref, emitter(at))
        return carry

    lax.fori_loop(0, blocks, step, 0)


def late_own_kernel(blocks, where_ref, filt_ref, x_ref, gain_ref, beam_ref, out_ref, cal_ref):
    @pl.when(where_ref[1] == 0)
    def _():
        each_late_block(blocks, filt_ref, x_ref, gain_ref, beam_ref, cal_ref, lambda at: keeper(out_ref, at))


def late_kernel(
    blocks, where_ref, filt_ref, x_ref, gain_ref, beam_ref, keep_ref, table_ref, power_ref, *refs
):
    out_refs, (cal_ref, sum_ref) = refs[:-2], refs[-2:]

    @pl.when(where_ref[1] == 0)
    def _():
        def emitter(at):
            return adder(power_ref, keep_ref, sum_ref, at)

        each_late_block(blocks, filt_ref, x_ref, gain_ref, beam_ref, cal_ref, emitter)
        place(sum_ref, table_ref, out_refs)


def near_kernel(n_owner, where_ref, filt_ref, n0, n1, x0, x1, g0, g1, beam_ref, keep_ref, table_ref, *refs):
    out_refs, pre_ref, (cal_ref, sum_ref) = refs[:n_owner], refs[n_owner], refs[n_owner + 1 :]
    reach = BLOCK * ROWS

    @pl.when(where_ref[1] == 1)
    def _():
        for pol, (n, x, gain) in enumerate(((n0, x0, g0), (n1, x1, g1))):

            def spectra(cyl, pol=pol, n=n, x=x):
                there = n[:, columns(cyl)]
                pre_ref[pol * CYL + cyl] = filtered(
                    [(filt_ref[:, reach : 2 * reach], there), (filt_ref[:, 2 * reach :], x[:reach, columns(cyl)])]
                )
                return filtered([(filt_ref[:, :reach], there), (filt_ref[:, reach:], x[: 2 * reach, columns(cyl)])])

            emit = adder(sum_ref, keep_ref, sum_ref) if pol else keeper(sum_ref)
            form_powers(spectra, gain, beam_ref, cal_ref, emit)
        place(sum_ref, table_ref, out_refs)


def far_kernel(n_owner, where_ref, edge_ref, f0, f1, g0, g1, beam_ref, keep_ref, table_ref, pre_ref, *refs):
    own_refs, out_refs, own_ref, (cal_ref, sum_ref) = refs[:2], refs[2 : 2 + n_owner], refs[2 + n_owner], refs[-2:]
    half = BLOCK * UPCH

    @pl.when(where_ref[1] == 1)
    def _():
        for pol, (f, gain) in enumerate(((f0, g0), (f1, g1))):

            def spectra(cyl, pol=pol, f=f):
                return pre_ref[pol * CYL + cyl] + filtered([(edge_ref[...], f[:, columns(cyl)])])

            emit = adder(sum_ref, keep_ref, sum_ref) if pol else keeper(sum_ref)
            form_powers(spectra, gain, beam_ref, cal_ref, emit)
        place(sum_ref, table_ref, out_refs)
        own_ref[:half, :] = out_refs[0][...]
        own_ref[half:, :] = own_refs[0][...]

    @pl.when(where_ref[1] == 0)
    def _():
        own_ref[...] = own_refs[1][...]


def place_table_kernel(most_sets, where_ref, owner_ref, out_ref):
    n_owner, beams, width = out_ref.shape
    sets = owner_ref.shape[1]
    owner = owner_ref[...].astype(jnp.float32)
    set_of = lax.broadcasted_iota(jnp.int32, (beams, sets), 0) // SET_BEAMS
    lane = lax.broadcasted_iota(jnp.int32, (beams, sets), 1)
    own = jnp.sum(jnp.where(set_of == lane, owner, 0.0), axis=1, keepdims=True)
    same = jnp.logical_and(owner == own, lane < set_of)
    rank = jnp.sum(jnp.where(same, 1.0, 0.0), axis=1, keepdims=True)
    within = lax.broadcasted_iota(jnp.int32, (beams, 1), 0) % SET_BEAMS
    column = (own * most_sets + rank).astype(jnp.int32) * SET_BEAMS + within
    lane_at = lax.broadcasted_iota(jnp.int32, (beams, width), 1)
    for k in range(n_owner):
        owner_k = where_ref[0] ^ k
        hit = (column - owner_k * width) == lane_at
        out_ref[k] = jnp.where(hit, 1.0, 0.0).astype(jnp.bfloat16)


def gather_kernel(n_owner, where_ref, *refs):
    own_ref, got, out_ref = refs[0], refs[1:-1], refs[-1]
    far, near, late = (got[i * (n_owner - 1) : (i + 1) * (n_owner - 1)] for i in range(3))

    def copy(block, frame, k):
        rows = pl.ds(pl.multiple_of((where_ref[0] ^ k) * UPCH, UPCH), UPCH)
        count = block.shape[0] // UPCH
        out_ref[frame : frame + count, rows, :] = block[...].reshape(count, UPCH, block.shape[1])

    copy(own_ref, 0, 0)

    @pl.when(where_ref[1] == 0)
    def _():
        for k in range(1, n_owner):
            copy(far[k - 1], 0, k)
            copy(near[k - 1], BLOCK, k)

    @pl.when(where_ref[1] == 1)
    def _():
        for k in range(1, n_owner):
            copy(late[k - 1], 0, k)


VMEM = pl.BlockSpec(memory_space=pltpu.VMEM)
SMEM = pl.BlockSpec(memory_space=pltpu.SMEM)
ANY = pl.BlockSpec(memory_space=pl.ANY)


def call(body, out_shape, n_in, flops, nbytes, scalars=0, whole=0, after=0, scratch=()):
    many = isinstance(out_shape, (list, tuple))

    def kernel(*refs):
        seen = scalars + n_in + whole
        body(*refs[:seen], *refs[seen + after :])

    return pl.pallas_call(
        kernel,
        out_shape=out_shape,
        in_specs=[SMEM] * scalars + [VMEM] * n_in + [ANY] * (whole + after),
        out_specs=[VMEM] * len(out_shape) if many else VMEM,
        scratch_shapes=list(scratch),
        cost_estimate=pl.CostEstimate(flops=flops, bytes_accessed=nbytes, transcendentals=0),
        compiler_params=pltpu.CompilerParams(vmem_limit_bytes=24 << 20),
    )


def per_device(voltages, feed_gains, owner_table, keep_flags):
    samples = voltages[0, 0]
    gain = feed_gains[0, 0]
    frame_count = samples.shape[0] // UPCH
    kept = frame_count // 2
    n_owner = lax.axis_size("freq")
    assert voltages.shape[1] == 1 and kept == 2 * BLOCK and kept >= TAPS
    assert n_owner & (n_owner - 1) == 0
    n_tm = lax.axis_size("tm")
    me = lax.axis_index("freq")
    pol = lax.axis_index("pol")
    most_sets = 2 * owner_table.shape[0] // n_owner
    beams = keep_flags.shape[0]
    width = most_sets * SET_BEAMS
    bf16 = jnp.bfloat16
    filt = jnp.asarray(filter_matrix())
    edge = jnp.asarray(filter_matrix()[:, ROWS : BLOCK * ROWS])
    beam_table = jnp.asarray(beam_matrix())

    pairs = [(i, i + 1) for i in range(n_tm - 1)]

    def ahead(part, source):
        return lax.ppermute(part, ("tm", "pol"), [(i * 2 + source, j * 2 + 1) for i, j in pairs])

    def swap(part):
        return lax.ppermute(part, "pol", [(0, 1), (1, 0)])

    def spread(blocks, source):
        got = []
        for k in range(1, n_owner):
            route = [(i * 2 + source, (i ^ k) * 2 + 1 - source) for i in range(n_owner)]
            got.append(lax.ppermute(blocks[k], ("freq", "pol"), route))
        return got

    def form(body, rows, *arrays, after=(), more=()):
        shape = [jax.ShapeDtypeStruct((rows, width), bf16)] * n_owner
        scratch = [pltpu.VMEM((CYL * BLOCK * UPCH, 2 * NS), bf16), pltpu.VMEM((rows, beams), bf16)]
        return call(
            body,
            shape + list(more),
            len(arrays),
            4 * 512 * 1024 * 1024,
            4 << 20,
            scalars=1,
            after=len(after),
            scratch=scratch,
        )(where, *arrays, *after)

    where = jnp.stack([me, pol]).astype(jnp.int32)
    keep = keep_flags.reshape(1, -1)
    reach, edge_rows = BLOCK * ROWS, (TAPS - 1 - BLOCK) * ROWS
    table = call(
        functools.partial(place_table_kernel, most_sets),
        jax.ShapeDtypeStruct((n_owner, beams, width), bf16),
        1,
        1 << 24,
        4 << 20,
        scalars=1,
    )(where, owner_table.reshape(1, -1))
    samples, table = lax.optimization_barrier((samples, table))
    x = samples.transpose(0, 2, 1, 3).reshape(samples.shape[0] * 2, CYL * NS)
    x = lax.optimization_barrier(x)
    near_rows, far_rows = call(
        halo_rows_kernel,
        [jax.ShapeDtypeStruct((rows, CYL * NS), bf16) for rows in (reach, edge_rows)],
        1,
        0,
        2 << 20,
    )(x)
    near0 = ahead(near_rows, 0)
    near1 = ahead(near_rows, 1)
    other = swap(x)
    gain_other = swap(gain)
    far0 = ahead(far_rows, 0)
    far1 = ahead(far_rows, 1)
    common = (gain, gain_other, beam_table, keep, table)
    blocks = kept // BLOCK
    late_own = call(
        functools.partial(late_own_kernel, blocks),
        jax.ShapeDtypeStruct((kept * UPCH, beams), bf16),
        4,
        4 * 512 * 1024 * 1024,
        4 << 20,
        scalars=1,
        scratch=[pltpu.VMEM((CYL * BLOCK * UPCH, 2 * NS), bf16)],
    )(where, filt, x, gain, beam_table)
    body = functools.partial(late_kernel, blocks)
    rows = kept * UPCH
    late = form(body, rows, filt, other, gain_other, beam_table, keep, table, late_own)
    late_got = spread(late, 0)
    *near, pre = form(
        functools.partial(near_kernel, n_owner),
        BLOCK * UPCH,
        filt,
        near1,
        near0,
        x,
        other,
        *common,
        after=late[:1],
        more=[jax.ShapeDtypeStruct((2 * CYL, reach, NS), jnp.float32)],
    )
    near_got = spread(near, 1)
    *far, own = form(
        functools.partial(far_kernel, n_owner),
        BLOCK * UPCH,
        edge,
        far1,
        far0,
        *common,
        pre,
        near[0],
        late[0],
        more=[jax.ShapeDtypeStruct((kept * UPCH, width), bf16)],
    )
    far_got = spread(far, 1)
    own_got = swap(own)
    out_shape = jax.ShapeDtypeStruct((kept, n_owner * UPCH, width), bf16)
    arrays = [own_got, *far_got, *near_got, *late_got]
    return call(functools.partial(gather_kernel, n_owner), out_shape, len(arrays), 0, 3 << 20, scalars=1)(
        where, *arrays
    )


def solution(mesh):
    return jax.shard_map(
        per_device,
        mesh=mesh,
        in_specs=(
            P("pol", ("grp", "freq"), "tm", None, None, None),
            P(("grp", "freq"), "pol", None, None, None),
            P(),
            P(),
        ),
        out_specs=P(("grp", "tm", "pol"), None, "freq"),
        check_vma=False,
    )
```

```python
import functools

import jax
import jax.numpy as jnp
import numpy as np
from jax import lax
from jax.experimental import pallas as pl
from jax.experimental.pallas import tpu as pltpu
from jax.sharding import PartitionSpec as P


NS = 256
CYL = 4
UPCH = 16
TAPS = 16
SET_BEAMS = 16
BLOCK = 8
LANES = 128
ROWS = 2 * UPCH


def window_taps():
    span = TAPS * UPCH
    steps = np.arange(span, dtype=np.float64)
    weights = np.sinc((steps - (span - 1) / 2.0) / UPCH) * np.sin(np.pi * (steps + 0.5) / span) ** 2
    return weights / np.sqrt(np.sum(weights * weights))


def filter_matrix():
    weights = window_taps()
    fine = np.arange(UPCH)
    sample = np.arange(TAPS * UPCH)
    phase = 2.0 * np.pi * ((fine[:, None] * sample[None, :]) % UPCH) / UPCH
    cosine = np.cos(phase) * weights
    sine = np.sin(phase) * weights
    table = np.zeros((2, BLOCK, UPCH, TAPS + BLOCK, UPCH, 2))
    for frame in range(BLOCK):
        taps = slice(frame + 1, frame + 1 + TAPS)
        cos_part = cosine.reshape(UPCH, TAPS, UPCH)
        sin_part = sine.reshape(UPCH, TAPS, UPCH)
        table[0, frame, :, taps, :, 0] = cos_part
        table[0, frame, :, taps, :, 1] = sin_part
        table[1, frame, :, taps, :, 0] = -sin_part
        table[1, frame, :, taps, :, 1] = cos_part
    return table.reshape(2 * BLOCK * UPCH, (TAPS + BLOCK) * ROWS).astype(np.float32).astype(jnp.bfloat16)


def beam_matrix():
    rows = np.arange(NS)
    angle = 2.0 * np.pi * (rows[:, None] * rows[None, :] % NS) / NS
    scale = 1.0 / np.sqrt(NS)
    cosine = (np.cos(angle) * scale).astype(np.float32)
    sine = (np.sin(angle) * scale).astype(np.float32)
    upper = np.concatenate([cosine, -sine], axis=1)
    lower = np.concatenate([sine, cosine], axis=1)
    table = np.concatenate([upper, lower], axis=0).astype(jnp.bfloat16)
    table = table.reshape(2 * NS, 2, NS // LANES, LANES).transpose(0, 2, 1, 3).reshape(2 * NS, 2 * NS)
    return (table.astype(np.float32) * 0.5).astype(jnp.bfloat16)


def columns(cyl):
    return slice(cyl * NS, (cyl + 1) * NS)


def form_powers(spectra, gain_ref, beam_ref, cal_ref, emit):
    half = BLOCK * UPCH
    for cyl in range(CYL):
        spec = spectra(cyl)
        real, imag = spec[:half], spec[half:]
        gain_real = gain_ref[cyl, 0:1, :]
        gain_imag = gain_ref[cyl, 1:2, :]
        rows = slice(cyl * half, (cyl + 1) * half)
        cal_ref[rows, :NS] = (real * gain_real - imag * gain_imag).astype(jnp.bfloat16)
        cal_ref[rows, NS:] = (real * gain_imag + imag * gain_real).astype(jnp.bfloat16)
    for strip in range(NS // LANES):
        beam = jnp.dot(
            cal_ref[...],
            beam_ref[:, strip * 2 * LANES : (strip + 1) * 2 * LANES],
            preferred_element_type=jnp.float32,
        )
        beams = [beam[cyl * half : (cyl + 1) * half] for cyl in range(CYL)]
        (r0, i0), (r1, i1), (r2, i2), (r3, i3) = [(b[:, :LANES], b[:, LANES:]) for b in beams]
        pr, pi, mr, mi = r0 + r2, i0 + i2, r0 - r2, i0 - i2
        sr, si, dr, di = r1 + r3, i1 + i3, r1 - r3, i1 - i3
        formed = [(pr + sr, pi + si), (mr + di, mi - dr), (pr - sr, pi - si), (mr - di, mi + dr)]
        for element, (fr, fi) in enumerate(formed):
            emit(element * NS + strip * LANES, fr * fr + fi * fi)


def filtered(terms):
    total = None
    for table, rows in terms:
        term = jnp.dot(table, rows, preferred_element_type=jnp.float32)
        total = term if total is None else total + term
    return total


def keeper(power_ref, at=0):
    rows = pl.ds(at, BLOCK * UPCH)

    def emit(column, power):
        power_ref[rows, column : column + LANES] = power.astype(jnp.bfloat16)

    return emit


def adder(power_ref, keep_ref, sum_ref, at=0):
    rows = pl.ds(at, BLOCK * UPCH)

    def emit(column, power):
        lanes = slice(column, column + LANES)
        total = power_ref[rows, lanes].astype(jnp.float32) + power.astype(jnp.bfloat16).astype(jnp.float32)
        sum_ref[rows, lanes] = (total * keep_ref[:, lanes].astype(jnp.float32)).astype(jnp.bfloat16)

    return emit


def place(sum_ref, table_ref, out_refs):
    for k, out_ref in enumerate(out_refs):
        placed = jnp.dot(sum_ref[...], table_ref[k], preferred_element_type=jnp.float32)
        out_ref[...] = placed.astype(jnp.bfloat16)


def halo_rows_kernel(x_ref, near_ref, far_ref):
    near_at = x_ref.shape[0] - near_ref.shape[0]
    near_ref[...] = x_ref[near_at:, :]
    far_ref[...] = x_ref[near_at - far_ref.shape[0] : near_at, :]


def each_late_block(blocks, filt_ref, x_ref, gain_ref, beam_ref, cal_ref, emitter):
    def step(block, carry):
        first = pl.multiple_of(block * BLOCK * ROWS, BLOCK * ROWS)
        rows = pl.ds(first, (TAPS + BLOCK) * ROWS)

        def spectra(cyl):
            return filtered([(filt_ref[...], x_ref[rows, columns(cyl)])])

        at = pl.multiple_of(block * BLOCK * UPCH, BLOCK * UPCH)
        form_powers(spectra, gain_ref, beam_ref, cal_ref, emitter(at))
        return carry

    lax.fori_loop(0, blocks, step, 0)


def late_own_kernel(blocks, where_ref, filt_ref, x_ref, gain_ref, beam_ref, out_ref, cal_ref):
    @pl.when(where_ref[1] == 0)
    def _():
        each_late_block(blocks, filt_ref, x_ref, gain_ref, beam_ref, cal_ref, lambda at: keeper(out_ref, at))


def late_kernel(block, where_ref, filt_ref, x_ref, gain_ref, beam_ref, keep_ref, table_ref, power_ref, *refs):
    out_refs, (cal_ref, sum_ref) = refs[:-2], refs[-2:]
    rows = slice(block * BLOCK * ROWS, (block * BLOCK + TAPS + BLOCK) * ROWS)
    mine = power_ref.at[block * BLOCK * UPCH : (block + 1) * BLOCK * UPCH]

    @pl.when(where_ref[1] == 0)
    def _():
        def spectra(cyl):
            return filtered([(filt_ref[...], x_ref[rows, columns(cyl)])])

        form_powers(spectra, gain_ref, beam_ref, cal_ref.at[0], adder(mine, keep_ref, sum_ref))
        place(sum_ref, table_ref, out_refs)


def near_kernel(n_owner, where_ref, filt_ref, n0, n1, x0, x1, g0, g1, beam_ref, keep_ref, table_ref, *refs):
    out_refs, pre_ref, (cal_ref, sum_ref) = refs[:n_owner], refs[n_owner], refs[n_owner + 1 :]
    reach = BLOCK * ROWS

    @pl.when(where_ref[1] == 1)
    def _():
        for pol, (n, x, gain) in enumerate(((n0, x0, g0), (n1, x1, g1))):

            def spectra(cyl, pol=pol, n=n, x=x):
                there = n[:, columns(cyl)]
                pre_ref[pol * CYL + cyl] = filtered(
                    [(filt_ref[:, reach : 2 * reach], there), (filt_ref[:, 2 * reach :], x[:reach, columns(cyl)])]
                )
                return filtered([(filt_ref[:, :reach], there), (filt_ref[:, reach:], x[: 2 * reach, columns(cyl)])])

            emit = adder(sum_ref, keep_ref, sum_ref) if pol else keeper(sum_ref)
            form_powers(spectra, gain, beam_ref, cal_ref.at[pol], emit)
        place(sum_ref, table_ref, out_refs)


def far_kernel(n_owner, where_ref, edge_ref, f0, f1, g0, g1, beam_ref, keep_ref, table_ref, pre_ref, *refs):
    own_refs, out_refs, own_ref, (cal_ref, sum_ref) = refs[:3], refs[3 : 3 + n_owner], refs[3 + n_owner], refs[-2:]
    half = BLOCK * UPCH

    @pl.when(where_ref[1] == 1)
    def _():
        for pol, (f, gain) in enumerate(((f0, g0), (f1, g1))):

            def spectra(cyl, pol=pol, f=f):
                return pre_ref[pol * CYL + cyl] + filtered([(edge_ref[...], f[:, columns(cyl)])])

            emit = adder(sum_ref, keep_ref, sum_ref) if pol else keeper(sum_ref)
            form_powers(spectra, gain, beam_ref, cal_ref.at[pol], emit)
        place(sum_ref, table_ref, out_refs)
        own_ref[:half, :] = out_refs[0][...]
        own_ref[half:, :] = own_refs[0][...]

    @pl.when(where_ref[1] == 0)
    def _():
        own_ref[:half, :] = own_refs[1][...]
        own_ref[half:, :] = own_refs[2][...]


def place_table_kernel(most_sets, where_ref, owner_ref, out_ref):
    n_owner, beams, width = out_ref.shape
    sets = owner_ref.shape[1]
    owner = owner_ref[...].astype(jnp.float32)
    set_of = lax.broadcasted_iota(jnp.int32, (sets, sets), 0)
    lane = lax.broadcasted_iota(jnp.int32, (sets, sets), 1)
    own = jnp.sum(jnp.where(set_of == lane, owner, 0.0), axis=1, keepdims=True)
    same = jnp.logical_and(owner == own, lane < set_of)
    rank = jnp.sum(jnp.where(same, 1.0, 0.0), axis=1, keepdims=True)
    first = (own * most_sets + rank).astype(jnp.int32) * SET_BEAMS
    within = lax.broadcasted_iota(jnp.int32, (sets, SET_BEAMS, 1), 1)
    column = (first.reshape(sets, 1, 1) + within).reshape(beams, 1)
    lane_at = lax.broadcasted_iota(jnp.int32, (beams, width), 1)
    for k in range(n_owner):
        owner_k = where_ref[0] ^ k
        hit = (column - owner_k * width) == lane_at
        out_ref[k] = jnp.where(hit, 1.0, 0.0).astype(jnp.bfloat16)


def gather_kernel(n_owner, where_ref, *refs):
    own_ref, got, out_ref = refs[0], refs[1:-1], refs[-1]
    chunks = [got[i * (n_owner - 1) : (i + 1) * (n_owner - 1)] for i in range(4)]

    def copy(block, frame, k):
        rows = pl.ds(pl.multiple_of((where_ref[0] ^ k) * UPCH, UPCH), UPCH)
        count = block.shape[0] // UPCH
        out_ref[frame : frame + count, rows, :] = block[...].reshape(count, UPCH, block.shape[1])

    copy(own_ref, 0, 0)
    for pol in range(2):

        @pl.when(where_ref[1] == pol)
        def _(pol=pol):
            for part in range(2):
                for k in range(1, n_owner):
                    copy(chunks[2 * pol + part][k - 1], part * BLOCK, k)


VMEM = pl.BlockSpec(memory_space=pltpu.VMEM)
SMEM = pl.BlockSpec(memory_space=pltpu.SMEM)
ANY = pl.BlockSpec(memory_space=pl.ANY)


def call(body, out_shape, n_in, flops, nbytes, scalars=0, whole=0, after=0, scratch=()):
    many = isinstance(out_shape, (list, tuple))

    def kernel(*refs):
        seen = scalars + n_in + whole
        body(*refs[:seen], *refs[seen + after :])

    return pl.pallas_call(
        kernel,
        out_shape=out_shape,
        in_specs=[SMEM] * scalars + [VMEM] * n_in + [ANY] * (whole + after),
        out_specs=[VMEM] * len(out_shape) if many else VMEM,
        scratch_shapes=list(scratch),
        cost_estimate=pl.CostEstimate(flops=flops, bytes_accessed=nbytes, transcendentals=0),
        compiler_params=pltpu.CompilerParams(vmem_limit_bytes=24 << 20),
    )


def per_device(voltages, feed_gains, owner_table, keep_flags):
    samples = voltages[0, 0]
    gain = feed_gains[0, 0]
    frame_count = samples.shape[0] // UPCH
    kept = frame_count // 2
    n_owner = lax.axis_size("freq")
    assert voltages.shape[1] == 1 and kept == 2 * BLOCK and kept >= TAPS
    assert n_owner & (n_owner - 1) == 0
    n_tm = lax.axis_size("tm")
    me = lax.axis_index("freq")
    pol = lax.axis_index("pol")
    most_sets = 2 * owner_table.shape[0] // n_owner
    beams = keep_flags.shape[0]
    width = most_sets * SET_BEAMS
    bf16 = jnp.bfloat16
    filt = jnp.asarray(filter_matrix())
    edge = jnp.asarray(filter_matrix()[:, ROWS : BLOCK * ROWS])
    beam_table = jnp.asarray(beam_matrix())

    pairs = [(i, i + 1) for i in range(n_tm - 1)]

    def ahead(part, source):
        return lax.ppermute(part, ("tm", "pol"), [(i * 2 + source, j * 2 + 1) for i, j in pairs])

    def swap(part):
        return lax.ppermute(part, "pol", [(0, 1), (1, 0)])

    def spread(blocks, source):
        got = []
        for k in range(1, n_owner):
            route = [(i * 2 + source, (i ^ k) * 2 + 1 - source) for i in range(n_owner)]
            got.append(lax.ppermute(blocks[k], ("freq", "pol"), route))
        return got

    def form(body, rows, *arrays, after=(), more=()):
        shape = [jax.ShapeDtypeStruct((rows, width), bf16)] * n_owner
        scratch = [pltpu.VMEM((2, CYL * BLOCK * UPCH, 2 * NS), bf16), pltpu.VMEM((rows, beams), bf16)]
        return call(
            body,
            shape + list(more),
            len(arrays),
            4 * 512 * 1024 * 1024,
            4 << 20,
            scalars=1,
            after=len(after),
            scratch=scratch,
        )(where, *arrays, *after)

    where = jnp.stack([me, pol]).astype(jnp.int32)
    keep = keep_flags.reshape(1, -1)
    reach, edge_rows = BLOCK * ROWS, (TAPS - 1 - BLOCK) * ROWS
    table = call(
        functools.partial(place_table_kernel, most_sets),
        jax.ShapeDtypeStruct((n_owner, beams, width), bf16),
        1,
        1 << 24,
        4 << 20,
        scalars=1,
    )(where, owner_table.reshape(1, -1))
    samples, table = lax.optimization_barrier((samples, table))
    x = samples.transpose(0, 2, 1, 3).reshape(samples.shape[0] * 2, CYL * NS)
    x = lax.optimization_barrier(x)
    near_rows, far_rows = call(
        halo_rows_kernel,
        [jax.ShapeDtypeStruct((rows, CYL * NS), bf16) for rows in (reach, edge_rows)],
        1,
        0,
        2 << 20,
    )(x)
    near0 = ahead(near_rows, 0)
    near1 = ahead(near_rows, 1)
    other = swap(x)
    gain_other = swap(gain)
    far0 = ahead(far_rows, 0)
    far1 = ahead(far_rows, 1)
    common = (gain, gain_other, beam_table, keep, table)
    blocks = kept // BLOCK
    late_own = call(
        functools.partial(late_own_kernel, blocks),
        jax.ShapeDtypeStruct((kept * UPCH, beams), bf16),
        4,
        4 * 512 * 1024 * 1024,
        4 << 20,
        scalars=1,
        scratch=[pltpu.VMEM((CYL * BLOCK * UPCH, 2 * NS), bf16)],
    )(where, filt, x, gain, beam_table)
    late, got = [], []
    for block in range(blocks):
        body = functools.partial(late_kernel, block)
        arrays = (filt, other, gain_other, beam_table, keep, table, late_own)
        after = [late[-1][0]] if late else []
        late.append(form(body, BLOCK * UPCH, *arrays, after=after))
        got += spread(late[-1], 0)
    *near, pre = form(
        functools.partial(near_kernel, n_owner),
        BLOCK * UPCH,
        filt,
        near1,
        near0,
        x,
        other,
        *common,
        after=late[1][:1],
        more=[jax.ShapeDtypeStruct((2 * CYL, reach, NS), jnp.float32)],
    )
    near_got = spread(near, 1)
    *far, own = form(
        functools.partial(far_kernel, n_owner),
        BLOCK * UPCH,
        edge,
        far1,
        far0,
        *common,
        pre,
        near[0],
        late[0][0],
        late[1][0],
        more=[jax.ShapeDtypeStruct((kept * UPCH, width), bf16)],
    )
    far_got = spread(far, 1)
    own_got = swap(own)
    out_shape = jax.ShapeDtypeStruct((kept, n_owner * UPCH, width), bf16)
    arrays = [own_got, *far_got, *near_got, *got]
    return call(functools.partial(gather_kernel, n_owner), out_shape, len(arrays), 0, 3 << 20, scalars=1)(
        where, *arrays
    )


def solution(mesh):
    return jax.shard_map(
        per_device,
        mesh=mesh,
        in_specs=(
            P("pol", ("grp", "freq"), "tm", None, None, None),
            P(("grp", "freq"), "pol", None, None, None),
            P(),
            P(),
        ),
        out_specs=P(("grp", "tm", "pol"), None, "freq"),
        check_vma=False,
    )
```

```python
import functools

import jax
import jax.numpy as jnp
import numpy as np
from jax import lax
from jax.experimental import pallas as pl
from jax.experimental.pallas import tpu as pltpu
from jax.sharding import PartitionSpec as P


NS = 256
CYL = 4
UPCH = 16
TAPS = 16
SET_BEAMS = 16
BLOCK = 8
LANES = 128
ROWS = 2 * UPCH


def window_taps():
    span = TAPS * UPCH
    steps = np.arange(span, dtype=np.float64)
    weights = np.sinc((steps - (span - 1) / 2.0) / UPCH) * np.sin(np.pi * (steps + 0.5) / span) ** 2
    return weights / np.sqrt(np.sum(weights * weights))


def filter_matrix():
    weights = window_taps()
    fine = np.arange(UPCH)
    sample = np.arange(TAPS * UPCH)
    phase = 2.0 * np.pi * ((fine[:, None] * sample[None, :]) % UPCH) / UPCH
    cosine = np.cos(phase) * weights
    sine = np.sin(phase) * weights
    table = np.zeros((2, BLOCK, UPCH, TAPS + BLOCK, UPCH, 2))
    for frame in range(BLOCK):
        taps = slice(frame + 1, frame + 1 + TAPS)
        cos_part = cosine.reshape(UPCH, TAPS, UPCH)
        sin_part = sine.reshape(UPCH, TAPS, UPCH)
        table[0, frame, :, taps, :, 0] = cos_part
        table[0, frame, :, taps, :, 1] = sin_part
        table[1, frame, :, taps, :, 0] = -sin_part
        table[1, frame, :, taps, :, 1] = cos_part
    return table.reshape(2 * BLOCK * UPCH, (TAPS + BLOCK) * ROWS).astype(np.float32).astype(jnp.bfloat16)


def beam_matrix():
    rows = np.arange(NS)
    angle = 2.0 * np.pi * (rows[:, None] * rows[None, :] % NS) / NS
    scale = 1.0 / np.sqrt(NS)
    cosine = (np.cos(angle) * scale).astype(np.float32)
    sine = (np.sin(angle) * scale).astype(np.float32)
    upper = np.concatenate([cosine, -sine], axis=1)
    lower = np.concatenate([sine, cosine], axis=1)
    table = np.concatenate([upper, lower], axis=0).astype(jnp.bfloat16)
    table = table.reshape(2 * NS, 2, NS // LANES, LANES).transpose(0, 2, 1, 3).reshape(2 * NS, 2 * NS)
    return (table.astype(np.float32) * 0.5).astype(jnp.bfloat16)


def columns(cyl):
    return slice(cyl * NS, (cyl + 1) * NS)


def form_powers(spectra, gain_ref, beam_ref, cal_ref, emit):
    half = BLOCK * UPCH
    for cyl in range(CYL):
        spec = spectra(cyl)
        real, imag = spec[:half], spec[half:]
        gain_real = gain_ref[cyl, 0:1, :]
        gain_imag = gain_ref[cyl, 1:2, :]
        rows = slice(cyl * half, (cyl + 1) * half)
        cal_ref[rows, :NS] = (real * gain_real - imag * gain_imag).astype(jnp.bfloat16)
        cal_ref[rows, NS:] = (real * gain_imag + imag * gain_real).astype(jnp.bfloat16)
    for strip in range(NS // LANES):
        beam = jnp.dot(
            cal_ref[...],
            beam_ref[:, strip * 2 * LANES : (strip + 1) * 2 * LANES],
            preferred_element_type=jnp.float32,
        )
        beams = [beam[cyl * half : (cyl + 1) * half] for cyl in range(CYL)]
        (r0, i0), (r1, i1), (r2, i2), (r3, i3) = [(b[:, :LANES], b[:, LANES:]) for b in beams]
        pr, pi, mr, mi = r0 + r2, i0 + i2, r0 - r2, i0 - i2
        sr, si, dr, di = r1 + r3, i1 + i3, r1 - r3, i1 - i3
        formed = [(pr + sr, pi + si), (mr + di, mi - dr), (pr - sr, pi - si), (mr - di, mi + dr)]
        for element, (fr, fi) in enumerate(formed):
            emit(element * NS + strip * LANES, fr * fr + fi * fi)


def filtered(terms):
    total = None
    for table, rows in terms:
        term = jnp.dot(table, rows, preferred_element_type=jnp.float32)
        total = term if total is None else total + term
    return total


def keeper(power_ref, at=0):
    rows = pl.ds(at, BLOCK * UPCH)

    def emit(column, power):
        power_ref[rows, column : column + LANES] = power.astype(jnp.bfloat16)

    return emit


def adder(power_ref, keep_ref, sum_ref, at=0):
    rows = pl.ds(at, BLOCK * UPCH)

    def emit(column, power):
        lanes = slice(column, column + LANES)
        total = power_ref[rows, lanes].astype(jnp.float32) + power.astype(jnp.bfloat16).astype(jnp.float32)
        sum_ref[rows, lanes] = (total * keep_ref[:, lanes].astype(jnp.float32)).astype(jnp.bfloat16)

    return emit


def place(sum_ref, table_ref, out_refs):
    for k, out_ref in enumerate(out_refs):
        placed = jnp.dot(sum_ref[...], table_ref[k], preferred_element_type=jnp.float32)
        out_ref[...] = placed.astype(jnp.bfloat16).reshape(out_ref.shape)


def halo_rows_kernel(x_ref, near_ref, far_ref):
    near_at = x_ref.shape[0] - near_ref.shape[0]
    near_ref[...] = x_ref[near_at:, :]
    far_ref[...] = x_ref[near_at - far_ref.shape[0] : near_at, :]


def each_late_block(blocks, filt_ref, x_ref, gain_ref, beam_ref, cal_ref, emitter):
    def step(block, carry):
        first = pl.multiple_of(block * BLOCK * ROWS, BLOCK * ROWS)
        rows = pl.ds(first, (TAPS + BLOCK) * ROWS)

        def spectra(cyl):
            return filtered([(filt_ref[...], x_ref[rows, columns(cyl)])])

        at = pl.multiple_of(block * BLOCK * UPCH, BLOCK * UPCH)
        form_powers(spectra, gain_ref, beam_ref, cal_ref, emitter(at))
        return carry

    lax.fori_loop(0, blocks, step, 0)


def late_own_kernel(blocks, where_ref, filt_ref, x_ref, gain_ref, beam_ref, out_ref, cal_ref):
    @pl.when(where_ref[1] == 0)
    def _():
        each_late_block(blocks, filt_ref, x_ref, gain_ref, beam_ref, cal_ref, lambda at: keeper(out_ref, at))


def late_kernel(
    blocks, where_ref, filt_ref, x_ref, gain_ref, beam_ref, keep_ref, table_ref, power_ref, *refs
):
    out_refs, (cal_ref, sum_ref) = refs[:-2], refs[-2:]

    @pl.when(where_ref[1] == 0)
    def _():
        def emitter(at):
            return adder(power_ref, keep_ref, sum_ref, at)

        each_late_block(blocks, filt_ref, x_ref, gain_ref, beam_ref, cal_ref, emitter)
        place(sum_ref, table_ref, out_refs)


def near_kernel(n_owner, where_ref, filt_ref, n0, n1, x0, x1, g0, g1, beam_ref, keep_ref, table_ref, *refs):
    out_refs, pre_ref, (cal_ref, sum_ref) = refs[:n_owner], refs[n_owner], refs[n_owner + 1 :]
    reach = BLOCK * ROWS

    @pl.when(where_ref[1] == 1)
    def _():
        for pol, (n, x, gain) in enumerate(((n0, x0, g0), (n1, x1, g1))):

            def spectra(cyl, pol=pol, n=n, x=x):
                there = n[:, columns(cyl)]
                pre_ref[pol * CYL + cyl] = filtered(
                    [(filt_ref[:, reach : 2 * reach], there), (filt_ref[:, 2 * reach :], x[:reach, columns(cyl)])]
                )
                return filtered([(filt_ref[:, :reach], there), (filt_ref[:, reach:], x[: 2 * reach, columns(cyl)])])

            emit = adder(sum_ref, keep_ref, sum_ref) if pol else keeper(sum_ref)
            form_powers(spectra, gain, beam_ref, cal_ref, emit)
        place(sum_ref, table_ref, out_refs)


def far_kernel(n_owner, where_ref, edge_ref, f0, f1, g0, g1, beam_ref, keep_ref, table_ref, pre_ref, *refs):
    own_refs, out_refs, own_ref, (cal_ref, sum_ref) = refs[:2], refs[2 : 2 + n_owner], refs[2 + n_owner], refs[-2:]
    half = BLOCK

    @pl.when(where_ref[1] == 1)
    def _():
        for pol, (f, gain) in enumerate(((f0, g0), (f1, g1))):

            def spectra(cyl, pol=pol, f=f):
                return pre_ref[pol * CYL + cyl] + filtered([(edge_ref[...], f[:, columns(cyl)])])

            emit = adder(sum_ref, keep_ref, sum_ref) if pol else keeper(sum_ref)
            form_powers(spectra, gain, beam_ref, cal_ref, emit)
        place(sum_ref, table_ref, out_refs)
        own_ref[:half] = out_refs[0][...]
        own_ref[half:] = own_refs[0][...]

    @pl.when(where_ref[1] == 0)
    def _():
        own_ref[...] = own_refs[1][...]


def place_table_kernel(where_ref, owner_ref, out_ref, rank_ref):
    n_owner = out_ref.shape[0]
    for owner in range(n_owner):
        rank_ref[owner] = 0
    out_ref[...] = jnp.zeros_like(out_ref)
    row = lax.broadcasted_iota(jnp.int32, (SET_BEAMS, LANES), 0)
    lane = lax.broadcasted_iota(jnp.int32, (SET_BEAMS, LANES), 1)

    def step(index, carry):
        owner = owner_ref[index]
        rank = rank_ref[owner]
        rank_ref[owner] = rank + 1
        column = rank * SET_BEAMS
        tile = column // LANES * LANES
        hit = lane - row == column - tile
        rows = pl.ds(pl.multiple_of(index * SET_BEAMS, SET_BEAMS), SET_BEAMS)
        lanes = pl.ds(pl.multiple_of(tile, LANES), LANES)
        out_ref[where_ref[0] ^ owner, rows, lanes] = jnp.where(hit, 1.0, 0.0).astype(jnp.bfloat16)
        return carry

    lax.fori_loop(0, owner_ref.shape[0], step, 0, unroll=4)


def put(where_ref, out_ref, sems, blocks):
    copies = []
    for index, (block, frame, k) in enumerate(blocks):
        rows = pl.ds(pl.multiple_of((where_ref[0] ^ k) * UPCH, UPCH), UPCH)
        at = out_ref.at[pl.ds(frame, block.shape[0]), rows]
        copies.append(pltpu.make_async_copy(block, at, sems.at[index]))
    for copy in copies:
        copy.start()
    for copy in copies:
        copy.wait()


def early_gather_kernel(n_owner, where_ref, *refs):
    near, late, out_ref, sems = refs[: n_owner - 1], refs[n_owner - 1 : -2], refs[-2], refs[-1]

    @pl.when(where_ref[1] == 0)
    def _():
        put(where_ref, out_ref, sems, [(block, BLOCK, k + 1) for k, block in enumerate(near)])

    @pl.when(where_ref[1] == 1)
    def _():
        put(where_ref, out_ref, sems, [(block, 0, k + 1) for k, block in enumerate(late)])


def last_gather_kernel(n_owner, where_ref, own_ref, *refs):
    far, out_ref, sems = refs[: n_owner - 1], refs[-2], refs[-1]

    @pl.when(where_ref[1] == 0)
    def _():
        put(where_ref, out_ref, sems, [(own_ref, 0, 0)] + [(block, 0, k + 1) for k, block in enumerate(far)])

    @pl.when(where_ref[1] == 1)
    def _():
        put(where_ref, out_ref, sems, [(own_ref, 0, 0)])


VMEM = pl.BlockSpec(memory_space=pltpu.VMEM)
SMEM = pl.BlockSpec(memory_space=pltpu.SMEM)
ANY = pl.BlockSpec(memory_space=pl.ANY)


def call(body, out_shape, n_in, flops, nbytes, scalars=0, whole=0, after=0, scratch=()):
    many = isinstance(out_shape, (list, tuple))

    def kernel(*refs):
        seen = scalars + n_in + whole
        body(*refs[:seen], *refs[seen + after :])

    return pl.pallas_call(
        kernel,
        out_shape=out_shape,
        in_specs=[SMEM] * scalars + [VMEM] * n_in + [ANY] * (whole + after),
        out_specs=[VMEM] * len(out_shape) if many else VMEM,
        scratch_shapes=list(scratch),
        cost_estimate=pl.CostEstimate(flops=flops, bytes_accessed=nbytes, transcendentals=0),
        compiler_params=pltpu.CompilerParams(vmem_limit_bytes=24 << 20),
    )


def per_device(voltages, feed_gains, owner_table, keep_flags):
    samples = voltages[0, 0]
    gain = feed_gains[0, 0]
    frame_count = samples.shape[0] // UPCH
    kept = frame_count // 2
    n_owner = lax.axis_size("freq")
    assert voltages.shape[1] == 1 and kept == 2 * BLOCK and kept >= TAPS
    assert n_owner & (n_owner - 1) == 0
    n_tm = lax.axis_size("tm")
    me = lax.axis_index("freq")
    pol = lax.axis_index("pol")
    most_sets = 2 * owner_table.shape[0] // n_owner
    beams = keep_flags.shape[0]
    width = most_sets * SET_BEAMS
    bf16 = jnp.bfloat16
    filt = jnp.asarray(filter_matrix())
    edge = jnp.asarray(filter_matrix()[:, ROWS : BLOCK * ROWS])
    beam_table = jnp.asarray(beam_matrix())

    pairs = [(i, i + 1) for i in range(n_tm - 1)]

    def ahead(part, source):
        return lax.ppermute(part, ("tm", "pol"), [(i * 2 + source, j * 2 + 1) for i, j in pairs])

    def swap(part):
        return lax.ppermute(part, "pol", [(0, 1), (1, 0)])

    def spread(blocks, source):
        got = []
        for k in range(1, n_owner):
            route = [(i * 2 + source, (i ^ k) * 2 + 1 - source) for i in range(n_owner)]
            got.append(lax.ppermute(blocks[k], ("freq", "pol"), route))
        return got

    def form(body, rows, *arrays, after=(), more=()):
        shape = [jax.ShapeDtypeStruct((rows // UPCH, UPCH, width), bf16)] * n_owner
        scratch = [pltpu.VMEM((CYL * BLOCK * UPCH, 2 * NS), bf16), pltpu.VMEM((rows, beams), bf16)]
        return call(
            body,
            shape + list(more),
            len(arrays),
            4 * 512 * 1024 * 1024,
            4 << 20,
            scalars=1,
            after=len(after),
            scratch=scratch,
        )(where, *arrays, *after)

    where = jnp.stack([me, pol]).astype(jnp.int32)
    keep = keep_flags.reshape(1, -1)
    reach, edge_rows = BLOCK * ROWS, (TAPS - 1 - BLOCK) * ROWS
    table = call(
        place_table_kernel,
        jax.ShapeDtypeStruct((n_owner, beams, width), bf16),
        0,
        1 << 20,
        4 << 20,
        scalars=2,
        scratch=[pltpu.SMEM((n_owner,), jnp.int32)],
    )(where, owner_table)
    samples, table = lax.optimization_barrier((samples, table))
    x = samples.transpose(0, 2, 1, 3).reshape(samples.shape[0] * 2, CYL * NS)
    x = lax.optimization_barrier(x)
    near_rows, far_rows = call(
        halo_rows_kernel,
        [jax.ShapeDtypeStruct((rows, CYL * NS), bf16) for rows in (reach, edge_rows)],
        1,
        0,
        2 << 20,
    )(x)
    near0 = ahead(near_rows, 0)
    near1 = ahead(near_rows, 1)
    other = swap(x)
    gain_other = swap(gain)
    far0 = ahead(far_rows, 0)
    far1 = ahead(far_rows, 1)
    common = (gain, gain_other, beam_table, keep, table)
    blocks = kept // BLOCK
    late_own = call(
        functools.partial(late_own_kernel, blocks),
        jax.ShapeDtypeStruct((kept * UPCH, beams), bf16),
        4,
        4 * 512 * 1024 * 1024,
        4 << 20,
        scalars=1,
        scratch=[pltpu.VMEM((CYL * BLOCK * UPCH, 2 * NS), bf16)],
    )(where, filt, x, gain, beam_table)
    body = functools.partial(late_kernel, blocks)
    rows = kept * UPCH
    late = form(body, rows, filt, other, gain_other, beam_table, keep, table, late_own)
    late_got = spread(late, 0)
    *near, pre = form(
        functools.partial(near_kernel, n_owner),
        BLOCK * UPCH,
        filt,
        near1,
        near0,
        x,
        other,
        *common,
        after=late[:1],
        more=[jax.ShapeDtypeStruct((2 * CYL, reach, NS), jnp.float32)],
    )
    near_got = spread(near, 1)
    *far, own = form(
        functools.partial(far_kernel, n_owner),
        BLOCK * UPCH,
        edge,
        far1,
        far0,
        *common,
        pre,
        near[0],
        late[0],
        more=[jax.ShapeDtypeStruct((kept, UPCH, width), bf16)],
    )
    far_got = spread(far, 1)
    own_got = swap(own)
    out_shape = jax.ShapeDtypeStruct((kept, n_owner * UPCH, width), bf16)

    def gather(body, arrays, base=()):
        return pl.pallas_call(
            functools.partial(body, n_owner),
            out_shape=out_shape,
            in_specs=[SMEM] + [VMEM] * len(arrays) + [ANY] * len(base),
            out_specs=ANY,
            scratch_shapes=[pltpu.SemaphoreType.DMA((n_owner,))],
            input_output_aliases={1 + len(arrays): 0} if base else {},
            cost_estimate=pl.CostEstimate(flops=0, bytes_accessed=2 << 20, transcendentals=0),
            compiler_params=pltpu.CompilerParams(vmem_limit_bytes=24 << 20),
        )(where, *arrays, *base)

    out = gather(early_gather_kernel, [*near_got, *late_got])
    return gather(last_gather_kernel, [own_got, *far_got], base=[out])


def solution(mesh):
    return jax.shard_map(
        per_device,
        mesh=mesh,
        in_specs=(
            P("pol", ("grp", "freq"), "tm", None, None, None),
            P(("grp", "freq"), "pol", None, None, None),
            P(),
            P(),
        ),
        out_specs=P(("grp", "tm", "pol"), None, "freq"),
        check_vma=False,
    )
```

```python
import functools

import jax
import jax.numpy as jnp
import numpy as np
from jax import lax
from jax.experimental import pallas as pl
from jax.experimental.pallas import tpu as pltpu
from jax.sharding import PartitionSpec as P


NS = 256
CYL = 4
UPCH = 16
TAPS = 16
SET_BEAMS = 16
BLOCK = 8
LANES = 128
ROWS = 2 * UPCH


def window_taps():
    span = TAPS * UPCH
    steps = np.arange(span, dtype=np.float64)
    weights = np.sinc((steps - (span - 1) / 2.0) / UPCH) * np.sin(np.pi * (steps + 0.5) / span) ** 2
    return weights / np.sqrt(np.sum(weights * weights))


def filter_matrix():
    weights = window_taps()
    fine = np.arange(UPCH)
    sample = np.arange(TAPS * UPCH)
    phase = 2.0 * np.pi * ((fine[:, None] * sample[None, :]) % UPCH) / UPCH
    cosine = np.cos(phase) * weights
    sine = np.sin(phase) * weights
    table = np.zeros((2, BLOCK, UPCH, TAPS + BLOCK, UPCH, 2))
    for frame in range(BLOCK):
        taps = slice(frame + 1, frame + 1 + TAPS)
        cos_part = cosine.reshape(UPCH, TAPS, UPCH)
        sin_part = sine.reshape(UPCH, TAPS, UPCH)
        table[0, frame, :, taps, :, 0] = cos_part
        table[0, frame, :, taps, :, 1] = sin_part
        table[1, frame, :, taps, :, 0] = -sin_part
        table[1, frame, :, taps, :, 1] = cos_part
    return table.reshape(2 * BLOCK * UPCH, (TAPS + BLOCK) * ROWS).astype(np.float32).astype(jnp.bfloat16)


def beam_matrix():
    rows = np.arange(NS)
    angle = 2.0 * np.pi * (rows[:, None] * rows[None, :] % NS) / NS
    scale = 1.0 / np.sqrt(NS)
    cosine = (np.cos(angle) * scale).astype(np.float32)
    sine = (np.sin(angle) * scale).astype(np.float32)
    upper = np.concatenate([cosine, -sine], axis=1)
    lower = np.concatenate([sine, cosine], axis=1)
    table = np.concatenate([upper, lower], axis=0).astype(jnp.bfloat16)
    table = table.reshape(2 * NS, 2, NS // LANES, LANES).transpose(0, 2, 1, 3).reshape(2 * NS, 2 * NS)
    return (table.astype(np.float32) * 0.5).astype(jnp.bfloat16)


def columns(cyl):
    return slice(cyl * NS, (cyl + 1) * NS)


def form_powers(spectra, gain_ref, beam_ref, cal_ref, emit):
    half = BLOCK * UPCH
    for cyl in range(CYL):
        spec = spectra(cyl)
        real, imag = spec[:half], spec[half:]
        gain_real = gain_ref[cyl, 0:1, :]
        gain_imag = gain_ref[cyl, 1:2, :]
        rows = slice(cyl * half, (cyl + 1) * half)
        cal_ref[rows, :NS] = (real * gain_real - imag * gain_imag).astype(jnp.bfloat16)
        cal_ref[rows, NS:] = (real * gain_imag + imag * gain_real).astype(jnp.bfloat16)
    for strip in range(NS // LANES):
        beam = jnp.dot(
            cal_ref[...],
            beam_ref[:, strip * 2 * LANES : (strip + 1) * 2 * LANES],
            preferred_element_type=jnp.float32,
        )
        beams = [beam[cyl * half : (cyl + 1) * half] for cyl in range(CYL)]
        (r0, i0), (r1, i1), (r2, i2), (r3, i3) = [(b[:, :LANES], b[:, LANES:]) for b in beams]
        pr, pi, mr, mi = r0 + r2, i0 + i2, r0 - r2, i0 - i2
        sr, si, dr, di = r1 + r3, i1 + i3, r1 - r3, i1 - i3
        formed = [(pr + sr, pi + si), (mr + di, mi - dr), (pr - sr, pi - si), (mr - di, mi + dr)]
        for element, (fr, fi) in enumerate(formed):
            emit(element * NS + strip * LANES, fr * fr + fi * fi)


def filtered(terms):
    total = None
    for table, rows in terms:
        term = jnp.dot(table, rows, preferred_element_type=jnp.float32)
        total = term if total is None else total + term
    return total


def keeper(power_ref, at=0):
    rows = pl.ds(at, BLOCK * UPCH)

    def emit(column, power):
        power_ref[rows, column : column + LANES] = power.astype(jnp.bfloat16)

    return emit


def adder(power_ref, keep_ref, sum_ref, at=0):
    rows = pl.ds(at, BLOCK * UPCH)

    def emit(column, power):
        lanes = slice(column, column + LANES)
        total = power_ref[rows, lanes].astype(jnp.float32) + power.astype(jnp.bfloat16).astype(jnp.float32)
        sum_ref[rows, lanes] = (total * keep_ref[:, lanes].astype(jnp.float32)).astype(jnp.bfloat16)

    return emit


def place(sum_ref, table, out_ref):
    placed = jnp.dot(sum_ref[...], table, preferred_element_type=jnp.float32)
    out_ref[...] = placed.astype(jnp.bfloat16).reshape(out_ref.shape)


def place_kernel(pol, where_ref, sum_ref, table_ref, *out_refs):
    @pl.when(where_ref[1] == pol)
    def _():
        for k, out_ref in enumerate(out_refs):
            place(sum_ref, table_ref[k], out_ref)


def near_rows_kernel(x_ref, out_ref):
    out_ref[...] = x_ref[x_ref.shape[0] - out_ref.shape[0] :, :]


def far_rows_kernel(reach, where_ref, x_ref, other_ref, out_ref):
    count = out_ref.shape[0] // 2
    at = x_ref.shape[0] - reach - count

    @pl.when(where_ref[1] == 1)
    def _():
        out_ref[:count, :] = x_ref[at : at + count, :]
        out_ref[count:, :] = other_ref[at : at + count, :]


def each_late_block(blocks, filt_ref, x_ref, gain_ref, beam_ref, cal_ref, emitter):
    def step(block, carry):
        first = pl.multiple_of(block * BLOCK * ROWS, BLOCK * ROWS)
        rows = pl.ds(first, (TAPS + BLOCK) * ROWS)

        def spectra(cyl):
            return filtered([(filt_ref[...], x_ref[rows, columns(cyl)])])

        at = pl.multiple_of(block * BLOCK * UPCH, BLOCK * UPCH)
        form_powers(spectra, gain_ref, beam_ref, cal_ref, emitter(at))
        return carry

    lax.fori_loop(0, blocks, step, 0)


def late_own_kernel(blocks, where_ref, filt_ref, x_ref, gain_ref, beam_ref, out_ref, cal_ref):
    @pl.when(where_ref[1] == 0)
    def _():
        each_late_block(blocks, filt_ref, x_ref, gain_ref, beam_ref, cal_ref, lambda at: keeper(out_ref, at))


def late_kernel(
    blocks, where_ref, filt_ref, x_ref, gain_ref, beam_ref, keep_ref, table_ref, power_ref, sum_ref, out_ref, cal_ref
):
    @pl.when(where_ref[1] == 0)
    def _():
        def emitter(at):
            return adder(power_ref, keep_ref, sum_ref, at)

        each_late_block(blocks, filt_ref, x_ref, gain_ref, beam_ref, cal_ref, emitter)
        place(sum_ref, table_ref[table_ref.shape[0] - 1], out_ref)


def near_kernel(
    where_ref, filt_ref, n0, n1, x0, x1, g0, g1, beam_ref, keep_ref, table_ref, sum_ref, out_ref, pre_ref, cal_ref
):
    reach = BLOCK * ROWS

    @pl.when(where_ref[1] == 1)
    def _():
        for pol, (n, x, gain) in enumerate(((n0, x0, g0), (n1, x1, g1))):

            def spectra(cyl, pol=pol, n=n, x=x):
                there = n[:, columns(cyl)]
                pre_ref[pol * CYL + cyl] = filtered(
                    [(filt_ref[:, reach : 2 * reach], there), (filt_ref[:, 2 * reach :], x[:reach, columns(cyl)])]
                )
                return filtered([(filt_ref[:, :reach], there), (filt_ref[:, reach:], x[: 2 * reach, columns(cyl)])])

            emit = adder(sum_ref, keep_ref, sum_ref) if pol else keeper(sum_ref)
            form_powers(spectra, gain, beam_ref, cal_ref, emit)
        place(sum_ref, table_ref[table_ref.shape[0] - 1], out_ref)


def far_kernel(
    where_ref, edge_ref, far_ref, g0, g1, beam_ref, keep_ref, table_ref, pre_ref, sum_ref, out_ref, cal_ref
):
    count = far_ref.shape[0] // 2

    @pl.when(where_ref[1] == 1)
    def _():
        for pol, gain in enumerate((g0, g1)):

            def spectra(cyl, pol=pol):
                rows = far_ref[pol * count : (pol + 1) * count, columns(cyl)]
                return pre_ref[pol * CYL + cyl] + filtered([(edge_ref[...], rows)])

            emit = adder(sum_ref, keep_ref, sum_ref) if pol else keeper(sum_ref)
            form_powers(spectra, gain, beam_ref, cal_ref, emit)
        place(sum_ref, table_ref[table_ref.shape[0] - 1], out_ref)


def far_place_kernel(where_ref, sum_ref, table_ref, near_ref, late_ref, own_ref, *out_refs):
    @pl.when(where_ref[1] == 1)
    def _():
        for k, out_ref in enumerate(out_refs, 1):
            place(sum_ref, table_ref[k], out_ref)
        place(sum_ref, table_ref[0], own_ref.at[:BLOCK])
        own_ref[BLOCK:] = near_ref[...]

    @pl.when(where_ref[1] == 0)
    def _():
        own_ref[...] = late_ref[...]


def place_table_kernel(where_ref, owner_ref, out_ref, rank_ref):
    n_owner = out_ref.shape[0]
    for owner in range(n_owner):
        rank_ref[owner] = 0
    out_ref[...] = jnp.zeros_like(out_ref)
    row = lax.broadcasted_iota(jnp.int32, (SET_BEAMS, LANES), 0)
    lane = lax.broadcasted_iota(jnp.int32, (SET_BEAMS, LANES), 1)

    def step(index, carry):
        owner = owner_ref[index]
        rank = rank_ref[owner]
        rank_ref[owner] = rank + 1
        column = rank * SET_BEAMS
        tile = column // LANES * LANES
        hit = lane - row == column - tile
        rows = pl.ds(pl.multiple_of(index * SET_BEAMS, SET_BEAMS), SET_BEAMS)
        lanes = pl.ds(pl.multiple_of(tile, LANES), LANES)
        out_ref[where_ref[0] ^ owner, rows, lanes] = jnp.where(hit, 1.0, 0.0).astype(jnp.bfloat16)
        return carry

    lax.fori_loop(0, owner_ref.shape[0], step, 0, unroll=4)


def put(where_ref, out_ref, sems, blocks):
    copies = []
    for index, (block, frame, k) in enumerate(blocks):
        rows = pl.ds(pl.multiple_of((where_ref[0] ^ k) * UPCH, UPCH), UPCH)
        at = out_ref.at[pl.ds(frame, block.shape[0]), rows]
        copies.append(pltpu.make_async_copy(block, at, sems.at[index]))
    for copy in copies:
        copy.start()
    for copy in copies:
        copy.wait()


def early_gather_kernel(n_owner, where_ref, *refs):
    near, late, out_ref, sems = refs[: n_owner - 1], refs[n_owner - 1 : -2], refs[-2], refs[-1]

    @pl.when(where_ref[1] == 0)
    def _():
        put(where_ref, out_ref, sems, [(block, BLOCK, k + 1) for k, block in enumerate(near)])

    @pl.when(where_ref[1] == 1)
    def _():
        put(where_ref, out_ref, sems, [(block, 0, k + 1) for k, block in enumerate(late)])


def last_gather_kernel(n_owner, where_ref, own_ref, *refs):
    far, out_ref, sems = refs[: n_owner - 1], refs[-2], refs[-1]

    @pl.when(where_ref[1] == 0)
    def _():
        put(where_ref, out_ref, sems, [(own_ref, 0, 0)] + [(block, 0, k + 1) for k, block in enumerate(far)])

    @pl.when(where_ref[1] == 1)
    def _():
        put(where_ref, out_ref, sems, [(own_ref, 0, 0)])


VMEM = pl.BlockSpec(memory_space=pltpu.VMEM)
SMEM = pl.BlockSpec(memory_space=pltpu.SMEM)
ANY = pl.BlockSpec(memory_space=pl.ANY)


def call(body, out_shape, n_in, flops, nbytes, scalars=0, whole=0, after=0, scratch=()):
    many = isinstance(out_shape, (list, tuple))

    def kernel(*refs):
        seen = scalars + n_in + whole
        body(*refs[:seen], *refs[seen + after :])

    return pl.pallas_call(
        kernel,
        out_shape=out_shape,
        in_specs=[SMEM] * scalars + [VMEM] * n_in + [ANY] * (whole + after),
        out_specs=[VMEM] * len(out_shape) if many else VMEM,
        scratch_shapes=list(scratch),
        cost_estimate=pl.CostEstimate(flops=flops, bytes_accessed=nbytes, transcendentals=0),
        compiler_params=pltpu.CompilerParams(vmem_limit_bytes=24 << 20),
    )


def per_device(voltages, feed_gains, owner_table, keep_flags):
    samples = voltages[0, 0]
    gain = feed_gains[0, 0]
    frame_count = samples.shape[0] // UPCH
    kept = frame_count // 2
    n_owner = lax.axis_size("freq")
    assert voltages.shape[1] == 1 and kept == 2 * BLOCK and kept >= TAPS
    assert n_owner & (n_owner - 1) == 0
    n_tm = lax.axis_size("tm")
    me = lax.axis_index("freq")
    pol = lax.axis_index("pol")
    most_sets = 2 * owner_table.shape[0] // n_owner
    beams = keep_flags.shape[0]
    width = most_sets * SET_BEAMS
    bf16 = jnp.bfloat16
    filt = jnp.asarray(filter_matrix())
    edge = jnp.asarray(filter_matrix()[:, ROWS : BLOCK * ROWS])
    beam_table = jnp.asarray(beam_matrix())

    pairs = [(i, i + 1) for i in range(n_tm - 1)]

    def ahead(part, source):
        return lax.ppermute(part, ("tm", "pol"), [(i * 2 + source, j * 2 + 1) for i, j in pairs])

    def swap(part):
        return lax.ppermute(part, "pol", [(0, 1), (1, 0)])

    def spread(blocks, source):
        got = []
        for k in range(1, n_owner):
            route = [(i * 2 + source, (i ^ k) * 2 + 1 - source) for i in range(n_owner)]
            got.append(lax.ppermute(blocks[k], ("freq", "pol"), route))
        return got

    def form(body, frames, *arrays, more=()):
        shape = [jax.ShapeDtypeStruct((frames * UPCH, beams), bf16), jax.ShapeDtypeStruct((frames, UPCH, width), bf16)]
        scratch = [pltpu.VMEM((CYL * BLOCK * UPCH, 2 * NS), bf16)]
        return call(
            body, shape + list(more), len(arrays), 4 * 512 * 1024 * 1024, 4 << 20, scalars=1, scratch=scratch
        )(where, *arrays)

    def rest(body, frames, *arrays, more=(), count=n_owner - 1):
        shape = [jax.ShapeDtypeStruct((frames, UPCH, width), bf16)] * count
        return call(body, list(more) + shape, len(arrays), 1 << 29, 4 << 20, scalars=1)(where, *arrays)

    where = jnp.stack([me, pol]).astype(jnp.int32)
    keep = keep_flags.reshape(1, -1)
    reach, edge_rows = BLOCK * ROWS, (TAPS - 1 - BLOCK) * ROWS
    blocks = kept // BLOCK
    x = samples.transpose(0, 2, 1, 3).reshape(samples.shape[0] * 2, CYL * NS)
    x = lax.optimization_barrier(x)
    near_rows = call(near_rows_kernel, jax.ShapeDtypeStruct((reach, CYL * NS), bf16), 1, 0, 1 << 20)(x)
    near0 = ahead(near_rows, 0)
    near1 = ahead(near_rows, 1)
    other = swap(x)
    gain_other = swap(gain)
    late_own = call(
        functools.partial(late_own_kernel, blocks),
        jax.ShapeDtypeStruct((kept * UPCH, beams), bf16),
        4,
        4 * 512 * 1024 * 1024,
        4 << 20,
        scalars=1,
        scratch=[pltpu.VMEM((CYL * BLOCK * UPCH, 2 * NS), bf16)],
    )(where, filt, x, gain, beam_table)
    table = call(
        place_table_kernel,
        jax.ShapeDtypeStruct((n_owner, beams, width), bf16),
        0,
        1 << 20,
        4 << 20,
        scalars=2,
        after=1,
        scratch=[pltpu.SMEM((n_owner,), jnp.int32)],
    )(where, owner_table, late_own)
    late_sum, late_last = form(
        functools.partial(late_kernel, blocks), kept, filt, other, gain_other, beam_table, keep, table, late_own
    )
    far_rows = call(
        functools.partial(far_rows_kernel, reach),
        jax.ShapeDtypeStruct((2 * edge_rows, CYL * NS), bf16),
        2,
        0,
        2 << 20,
        scalars=1,
    )(where, x, other)
    far_halo = ahead(far_rows, 1)
    late = [*rest(functools.partial(place_kernel, 0), kept, late_sum, table), late_last]
    late_got = spread(late, 0)
    common = (gain, gain_other, beam_table, keep, table)
    near_sum, near_last, pre = form(
        near_kernel,
        BLOCK,
        filt,
        near1,
        near0,
        x,
        other,
        *common,
        more=[jax.ShapeDtypeStruct((2 * CYL, reach, NS), jnp.float32)],
    )
    near = [*rest(functools.partial(place_kernel, 1), BLOCK, near_sum, table), near_last]
    near_got = spread(near, 1)
    far_sum, far_last = form(far_kernel, BLOCK, edge, far_halo, *common, pre)
    own, *far = rest(
        far_place_kernel,
        BLOCK,
        far_sum,
        table,
        near[0],
        late[0],
        more=[jax.ShapeDtypeStruct((kept, UPCH, width), bf16)],
        count=n_owner - 2,
    )
    far = [own, *far, far_last]
    far_got = spread(far, 1)
    own_got = swap(own)
    out_shape = jax.ShapeDtypeStruct((kept, n_owner * UPCH, width), bf16)

    def gather(body, arrays, base=()):
        return pl.pallas_call(
            functools.partial(body, n_owner),
            out_shape=out_shape,
            in_specs=[SMEM] + [VMEM] * len(arrays) + [ANY] * len(base),
            out_specs=ANY,
            scratch_shapes=[pltpu.SemaphoreType.DMA((n_owner,))],
            input_output_aliases={1 + len(arrays): 0} if base else {},
            cost_estimate=pl.CostEstimate(flops=0, bytes_accessed=2 << 20, transcendentals=0),
            compiler_params=pltpu.CompilerParams(vmem_limit_bytes=24 << 20),
        )(where, *arrays, *base)

    out = gather(early_gather_kernel, [*near_got, *late_got])
    return gather(last_gather_kernel, [own_got, *far_got], base=[out])


def solution(mesh):
    return jax.shard_map(
        per_device,
        mesh=mesh,
        in_specs=(
            P("pol", ("grp", "freq"), "tm", None, None, None),
            P(("grp", "freq"), "pol", None, None, None),
            P(),
            P(),
        ),
        out_specs=P(("grp", "tm", "pol"), None, "freq"),
        check_vma=False,
    )
```

```python
import functools

import jax
import jax.numpy as jnp
import numpy as np
from jax import lax
from jax.experimental import pallas as pl
from jax.experimental.pallas import tpu as pltpu
from jax.sharding import PartitionSpec as P


NS = 256
CYL = 4
UPCH = 16
TAPS = 16
SET_BEAMS = 16
BLOCK = 8
LANES = 128
ROWS = 2 * UPCH


def window_taps():
    span = TAPS * UPCH
    steps = np.arange(span, dtype=np.float64)
    weights = np.sinc((steps - (span - 1) / 2.0) / UPCH) * np.sin(np.pi * (steps + 0.5) / span) ** 2
    return weights / np.sqrt(np.sum(weights * weights))


def filter_matrix():
    weights = window_taps()
    fine = np.arange(UPCH)
    sample = np.arange(TAPS * UPCH)
    phase = 2.0 * np.pi * ((fine[:, None] * sample[None, :]) % UPCH) / UPCH
    cosine = np.cos(phase) * weights
    sine = np.sin(phase) * weights
    table = np.zeros((2, BLOCK, UPCH, TAPS + BLOCK, UPCH, 2))
    for frame in range(BLOCK):
        taps = slice(frame + 1, frame + 1 + TAPS)
        cos_part = cosine.reshape(UPCH, TAPS, UPCH)
        sin_part = sine.reshape(UPCH, TAPS, UPCH)
        table[0, frame, :, taps, :, 0] = cos_part
        table[0, frame, :, taps, :, 1] = sin_part
        table[1, frame, :, taps, :, 0] = -sin_part
        table[1, frame, :, taps, :, 1] = cos_part
    return table.reshape(2 * BLOCK * UPCH, (TAPS + BLOCK) * ROWS).astype(np.float32).astype(jnp.bfloat16)


def beam_matrix():
    rows = np.arange(NS)
    angle = 2.0 * np.pi * (rows[:, None] * rows[None, :] % NS) / NS
    scale = 1.0 / np.sqrt(NS)
    cosine = (np.cos(angle) * scale).astype(np.float32)
    sine = (np.sin(angle) * scale).astype(np.float32)
    upper = np.concatenate([cosine, -sine], axis=1)
    lower = np.concatenate([sine, cosine], axis=1)
    table = np.concatenate([upper, lower], axis=0).astype(jnp.bfloat16)
    table = table.reshape(2 * NS, 2, NS // LANES, LANES).transpose(0, 2, 1, 3).reshape(2 * NS, 2 * NS)
    return (table.astype(np.float32) * 0.5).astype(jnp.bfloat16)


def columns(cyl):
    return slice(cyl * NS, (cyl + 1) * NS)


def form_powers(spectra, gain_ref, beam_ref, cal_ref, emit):
    half = BLOCK * UPCH
    for cyl in range(CYL):
        spec = spectra(cyl)
        real, imag = spec[:half], spec[half:]
        gain_real = gain_ref[cyl, 0:1, :]
        gain_imag = gain_ref[cyl, 1:2, :]
        rows = slice(cyl * half, (cyl + 1) * half)
        cal_ref[rows, :NS] = (real * gain_real - imag * gain_imag).astype(jnp.bfloat16)
        cal_ref[rows, NS:] = (real * gain_imag + imag * gain_real).astype(jnp.bfloat16)
    for strip in range(NS // LANES):
        beam = jnp.dot(
            cal_ref[...],
            beam_ref[:, strip * 2 * LANES : (strip + 1) * 2 * LANES],
            preferred_element_type=jnp.float32,
        )
        beams = [beam[cyl * half : (cyl + 1) * half] for cyl in range(CYL)]
        (r0, i0), (r1, i1), (r2, i2), (r3, i3) = [(b[:, :LANES], b[:, LANES:]) for b in beams]
        pr, pi, mr, mi = r0 + r2, i0 + i2, r0 - r2, i0 - i2
        sr, si, dr, di = r1 + r3, i1 + i3, r1 - r3, i1 - i3
        formed = [(pr + sr, pi + si), (mr + di, mi - dr), (pr - sr, pi - si), (mr - di, mi + dr)]
        for element, (fr, fi) in enumerate(formed):
            emit(element * NS + strip * LANES, fr * fr + fi * fi)


def filtered(terms):
    total = None
    for table, rows in terms:
        term = jnp.dot(table, rows, preferred_element_type=jnp.float32)
        total = term if total is None else total + term
    return total


def keeper(power_ref, at=0):
    rows = pl.ds(at, BLOCK * UPCH)

    def emit(column, power):
        power_ref[rows, column : column + LANES] = power.astype(jnp.bfloat16)

    return emit


def adder(power_ref, keep_ref, sum_ref, at=0):
    rows = pl.ds(at, BLOCK * UPCH)

    def emit(column, power):
        lanes = slice(column, column + LANES)
        total = power_ref[rows, lanes].astype(jnp.float32) + power.astype(jnp.bfloat16).astype(jnp.float32)
        sum_ref[rows, lanes] = (total * keep_ref[:, lanes].astype(jnp.float32)).astype(jnp.bfloat16)

    return emit


def place(sum_ref, table, out_ref):
    placed = jnp.dot(sum_ref[...], table, preferred_element_type=jnp.float32)
    out_ref[...] = placed.astype(jnp.bfloat16).reshape(out_ref.shape)


def place_kernel(pol, where_ref, sum_ref, table_ref, *out_refs):
    @pl.when(where_ref[1] == pol)
    def _():
        for k, out_ref in enumerate(out_refs):
            place(sum_ref, table_ref[k], out_ref)


def halo_rows_kernel(x_ref, near_ref, far_ref):
    near_at = x_ref.shape[0] - near_ref.shape[0]
    near_ref[...] = x_ref[near_at:, :]
    far_ref[...] = x_ref[near_at - far_ref.shape[0] : near_at, :]


def each_late_block(blocks, filt_ref, x_ref, gain_ref, beam_ref, cal_ref, emitter):
    def step(block, carry):
        first = pl.multiple_of(block * BLOCK * ROWS, BLOCK * ROWS)
        rows = pl.ds(first, (TAPS + BLOCK) * ROWS)

        def spectra(cyl):
            return filtered([(filt_ref[...], x_ref[rows, columns(cyl)])])

        at = pl.multiple_of(block * BLOCK * UPCH, BLOCK * UPCH)
        form_powers(spectra, gain_ref, beam_ref, cal_ref, emitter(at))
        return carry

    lax.fori_loop(0, blocks, step, 0)


def late_own_kernel(blocks, where_ref, filt_ref, x_ref, gain_ref, beam_ref, out_ref, cal_ref):
    @pl.when(where_ref[1] == 0)
    def _():
        each_late_block(blocks, filt_ref, x_ref, gain_ref, beam_ref, cal_ref, lambda at: keeper(out_ref, at))


def late_kernel(
    blocks, where_ref, filt_ref, x_ref, gain_ref, beam_ref, keep_ref, table_ref, power_ref, sum_ref, out_ref, cal_ref
):
    @pl.when(where_ref[1] == 0)
    def _():
        def emitter(at):
            return adder(power_ref, keep_ref, sum_ref, at)

        each_late_block(blocks, filt_ref, x_ref, gain_ref, beam_ref, cal_ref, emitter)
        place(sum_ref, table_ref[table_ref.shape[0] - 1], out_ref)


def near_kernel(
    where_ref, filt_ref, n0, n1, x0, x1, g0, g1, beam_ref, keep_ref, table_ref, sum_ref, out_ref, pre_ref, cal_ref
):
    reach = BLOCK * ROWS

    @pl.when(where_ref[1] == 1)
    def _():
        for pol, (n, x, gain) in enumerate(((n0, x0, g0), (n1, x1, g1))):

            def spectra(cyl, pol=pol, n=n, x=x):
                there = n[:, columns(cyl)]
                pre_ref[pol * CYL + cyl] = filtered(
                    [(filt_ref[:, reach : 2 * reach], there), (filt_ref[:, 2 * reach :], x[:reach, columns(cyl)])]
                )
                return filtered([(filt_ref[:, :reach], there), (filt_ref[:, reach:], x[: 2 * reach, columns(cyl)])])

            emit = adder(sum_ref, keep_ref, sum_ref) if pol else keeper(sum_ref)
            form_powers(spectra, gain, beam_ref, cal_ref, emit)
        place(sum_ref, table_ref[table_ref.shape[0] - 1], out_ref)


def far_kernel(
    where_ref, edge_ref, f0, f1, g0, g1, beam_ref, keep_ref, table_ref, pre_ref, sum_ref, out_ref, cal_ref
):
    @pl.when(where_ref[1] == 1)
    def _():
        for pol, (far_ref, gain) in enumerate(((f0, g0), (f1, g1))):

            def spectra(cyl, pol=pol, far_ref=far_ref):
                return pre_ref[pol * CYL + cyl] + filtered([(edge_ref[...], far_ref[:, columns(cyl)])])

            emit = adder(sum_ref, keep_ref, sum_ref) if pol else keeper(sum_ref)
            form_powers(spectra, gain, beam_ref, cal_ref, emit)
        place(sum_ref, table_ref[table_ref.shape[0] - 1], out_ref)


def far_place_kernel(where_ref, sum_ref, table_ref, near_ref, late_ref, own_ref, *out_refs):
    @pl.when(where_ref[1] == 1)
    def _():
        for k, out_ref in enumerate(out_refs, 1):
            place(sum_ref, table_ref[k], out_ref)
        place(sum_ref, table_ref[0], own_ref.at[:BLOCK])
        own_ref[BLOCK:] = near_ref[...]

    @pl.when(where_ref[1] == 0)
    def _():
        own_ref[...] = late_ref[...]


def place_table_kernel(where_ref, owner_ref, out_ref, rank_ref):
    n_owner = out_ref.shape[0]
    for owner in range(n_owner):
        rank_ref[owner] = 0
    out_ref[...] = jnp.zeros_like(out_ref)
    row = lax.broadcasted_iota(jnp.int32, (SET_BEAMS, LANES), 0)
    lane = lax.broadcasted_iota(jnp.int32, (SET_BEAMS, LANES), 1)

    def step(index, carry):
        owner = owner_ref[index]
        rank = rank_ref[owner]
        rank_ref[owner] = rank + 1
        column = rank * SET_BEAMS
        tile = column // LANES * LANES
        hit = lane - row == column - tile
        rows = pl.ds(pl.multiple_of(index * SET_BEAMS, SET_BEAMS), SET_BEAMS)
        lanes = pl.ds(pl.multiple_of(tile, LANES), LANES)
        out_ref[where_ref[0] ^ owner, rows, lanes] = jnp.where(hit, 1.0, 0.0).astype(jnp.bfloat16)
        return carry

    lax.fori_loop(0, owner_ref.shape[0], step, 0, unroll=4)


def put(where_ref, out_ref, sems, blocks):
    copies = []
    for index, (block, frame, k) in enumerate(blocks):
        rows = pl.ds(pl.multiple_of((where_ref[0] ^ k) * UPCH, UPCH), UPCH)
        at = out_ref.at[pl.ds(frame, block.shape[0]), rows]
        copies.append(pltpu.make_async_copy(block, at, sems.at[index]))
    for copy in copies:
        copy.start()
    for copy in copies:
        copy.wait()


def early_gather_kernel(n_owner, where_ref, *refs):
    near, late, out_ref, sems = refs[: n_owner - 1], refs[n_owner - 1 : -2], refs[-2], refs[-1]

    @pl.when(where_ref[1] == 0)
    def _():
        put(where_ref, out_ref, sems, [(block, BLOCK, k + 1) for k, block in enumerate(near)])

    @pl.when(where_ref[1] == 1)
    def _():
        put(where_ref, out_ref, sems, [(block, 0, k + 1) for k, block in enumerate(late)])


def last_gather_kernel(n_owner, where_ref, own_ref, *refs):
    far, out_ref, sems = refs[: n_owner - 1], refs[-2], refs[-1]

    @pl.when(where_ref[1] == 0)
    def _():
        put(where_ref, out_ref, sems, [(own_ref, 0, 0)] + [(block, 0, k + 1) for k, block in enumerate(far)])

    @pl.when(where_ref[1] == 1)
    def _():
        put(where_ref, out_ref, sems, [(own_ref, 0, 0)])


VMEM = pl.BlockSpec(memory_space=pltpu.VMEM)
SMEM = pl.BlockSpec(memory_space=pltpu.SMEM)
ANY = pl.BlockSpec(memory_space=pl.ANY)


def call(body, out_shape, n_in, flops, nbytes, scalars=0, whole=0, after=0, scratch=()):
    many = isinstance(out_shape, (list, tuple))

    def kernel(*refs):
        seen = scalars + n_in + whole
        body(*refs[:seen], *refs[seen + after :])

    return pl.pallas_call(
        kernel,
        out_shape=out_shape,
        in_specs=[SMEM] * scalars + [VMEM] * n_in + [ANY] * (whole + after),
        out_specs=[VMEM] * len(out_shape) if many else VMEM,
        scratch_shapes=list(scratch),
        cost_estimate=pl.CostEstimate(flops=flops, bytes_accessed=nbytes, transcendentals=0),
        compiler_params=pltpu.CompilerParams(vmem_limit_bytes=24 << 20),
    )


def per_device(voltages, feed_gains, owner_table, keep_flags):
    samples = voltages[0, 0]
    gain = feed_gains[0, 0]
    frame_count = samples.shape[0] // UPCH
    kept = frame_count // 2
    n_owner = lax.axis_size("freq")
    assert voltages.shape[1] == 1 and kept == 2 * BLOCK and kept >= TAPS
    assert n_owner & (n_owner - 1) == 0
    n_tm = lax.axis_size("tm")
    me = lax.axis_index("freq")
    pol = lax.axis_index("pol")
    most_sets = 2 * owner_table.shape[0] // n_owner
    beams = keep_flags.shape[0]
    width = most_sets * SET_BEAMS
    bf16 = jnp.bfloat16
    filt = jnp.asarray(filter_matrix())
    edge = jnp.asarray(filter_matrix()[:, ROWS : BLOCK * ROWS])
    beam_table = jnp.asarray(beam_matrix())

    pairs = [(i, i + 1) for i in range(n_tm - 1)]

    def ahead(part, source):
        return lax.ppermute(part, ("tm", "pol"), [(i * 2 + source, j * 2 + 1) for i, j in pairs])

    def swap(part):
        return lax.ppermute(part, "pol", [(0, 1), (1, 0)])

    def spread(blocks, source):
        got = []
        for k in range(1, n_owner):
            route = [(i * 2 + source, (i ^ k) * 2 + 1 - source) for i in range(n_owner)]
            got.append(lax.ppermute(blocks[k], ("freq", "pol"), route))
        return got

    def form(body, frames, *arrays, more=()):
        shape = [jax.ShapeDtypeStruct((frames * UPCH, beams), bf16), jax.ShapeDtypeStruct((frames, UPCH, width), bf16)]
        scratch = [pltpu.VMEM((CYL * BLOCK * UPCH, 2 * NS), bf16)]
        return call(
            body, shape + list(more), len(arrays), 4 * 512 * 1024 * 1024, 4 << 20, scalars=1, scratch=scratch
        )(where, *arrays)

    def rest(body, frames, *arrays, more=(), count=n_owner - 1):
        shape = [jax.ShapeDtypeStruct((frames, UPCH, width), bf16)] * count
        return call(body, list(more) + shape, len(arrays), 1 << 29, 4 << 20, scalars=1)(where, *arrays)

    where = jnp.stack([me, pol]).astype(jnp.int32)
    keep = keep_flags.reshape(1, -1)
    reach, edge_rows = BLOCK * ROWS, (TAPS - 1 - BLOCK) * ROWS
    blocks = kept // BLOCK
    table = call(
        place_table_kernel,
        jax.ShapeDtypeStruct((n_owner, beams, width), bf16),
        0,
        1 << 20,
        4 << 20,
        scalars=2,
        scratch=[pltpu.SMEM((n_owner,), jnp.int32)],
    )(where, owner_table)
    samples, table = lax.optimization_barrier((samples, table))
    x = samples.transpose(0, 2, 1, 3).reshape(samples.shape[0] * 2, CYL * NS)
    x = lax.optimization_barrier(x)
    near_rows, far_rows = call(
        halo_rows_kernel,
        [jax.ShapeDtypeStruct((rows, CYL * NS), bf16) for rows in (reach, edge_rows)],
        1,
        0,
        2 << 20,
    )(x)
    near0 = ahead(near_rows, 0)
    near1 = ahead(near_rows, 1)
    other = swap(x)
    gain_other = swap(gain)
    far0 = ahead(far_rows, 0)
    far1 = ahead(far_rows, 1)
    late_own = call(
        functools.partial(late_own_kernel, blocks),
        jax.ShapeDtypeStruct((kept * UPCH, beams), bf16),
        4,
        4 * 512 * 1024 * 1024,
        4 << 20,
        scalars=1,
        scratch=[pltpu.VMEM((CYL * BLOCK * UPCH, 2 * NS), bf16)],
    )(where, filt, x, gain, beam_table)
    late_sum, late_last = form(
        functools.partial(late_kernel, blocks), kept, filt, other, gain_other, beam_table, keep, table, late_own
    )
    late = [*rest(functools.partial(place_kernel, 0), kept, late_sum, table), late_last]
    late_got = spread(late, 0)
    common = (gain, gain_other, beam_table, keep, table)
    near_sum, near_last, pre = form(
        near_kernel,
        BLOCK,
        filt,
        near1,
        near0,
        x,
        other,
        *common,
        more=[jax.ShapeDtypeStruct((2 * CYL, reach, NS), jnp.float32)],
    )
    near = [*rest(functools.partial(place_kernel, 1), BLOCK, near_sum, table), near_last]
    near_got = spread(near, 1)
    far_sum, far_last = form(far_kernel, BLOCK, edge, far1, far0, *common, pre)
    own, *far = rest(
        far_place_kernel,
        BLOCK,
        far_sum,
        table,
        near[0],
        late[0],
        more=[jax.ShapeDtypeStruct((kept, UPCH, width), bf16)],
        count=n_owner - 2,
    )
    far = [own, *far, far_last]
    far_got = spread(far, 1)
    own_got = swap(own)
    out_shape = jax.ShapeDtypeStruct((kept, n_owner * UPCH, width), bf16)

    def gather(body, arrays, base=()):
        return pl.pallas_call(
            functools.partial(body, n_owner),
            out_shape=out_shape,
            in_specs=[SMEM] + [VMEM] * len(arrays) + [ANY] * len(base),
            out_specs=ANY,
            scratch_shapes=[pltpu.SemaphoreType.DMA((n_owner,))],
            input_output_aliases={1 + len(arrays): 0} if base else {},
            cost_estimate=pl.CostEstimate(flops=0, bytes_accessed=2 << 20, transcendentals=0),
            compiler_params=pltpu.CompilerParams(vmem_limit_bytes=24 << 20),
        )(where, *arrays, *base)

    out = gather(early_gather_kernel, [*near_got, *late_got])
    return gather(last_gather_kernel, [own_got, *far_got], base=[out])


def solution(mesh):
    return jax.shard_map(
        per_device,
        mesh=mesh,
        in_specs=(
            P("pol", ("grp", "freq"), "tm", None, None, None),
            P(("grp", "freq"), "pol", None, None, None),
            P(),
            P(),
        ),
        out_specs=P(("grp", "tm", "pol"), None, "freq"),
        check_vma=False,
    )
```

```python
import functools

import jax
import jax.numpy as jnp
import numpy as np
from jax import lax
from jax.experimental import pallas as pl
from jax.experimental.pallas import tpu as pltpu
from jax.sharding import PartitionSpec as P


NS = 256
CYL = 4
UPCH = 16
TAPS = 16
SET_BEAMS = 16
BLOCK = 8
LANES = 128
ROWS = 2 * UPCH


def window_taps():
    span = TAPS * UPCH
    steps = np.arange(span, dtype=np.float64)
    weights = np.sinc((steps - (span - 1) / 2.0) / UPCH) * np.sin(np.pi * (steps + 0.5) / span) ** 2
    return weights / np.sqrt(np.sum(weights * weights))


def filter_matrix():
    weights = window_taps()
    fine = np.arange(UPCH)
    sample = np.arange(TAPS * UPCH)
    phase = 2.0 * np.pi * ((fine[:, None] * sample[None, :]) % UPCH) / UPCH
    cosine = np.cos(phase) * weights
    sine = np.sin(phase) * weights
    table = np.zeros((2, BLOCK, UPCH, TAPS + BLOCK, UPCH, 2))
    for frame in range(BLOCK):
        taps = slice(frame + 1, frame + 1 + TAPS)
        cos_part = cosine.reshape(UPCH, TAPS, UPCH)
        sin_part = sine.reshape(UPCH, TAPS, UPCH)
        table[0, frame, :, taps, :, 0] = cos_part
        table[0, frame, :, taps, :, 1] = sin_part
        table[1, frame, :, taps, :, 0] = -sin_part
        table[1, frame, :, taps, :, 1] = cos_part
    return table.reshape(2 * BLOCK * UPCH, (TAPS + BLOCK) * ROWS).astype(np.float32).astype(jnp.bfloat16)


def beam_matrix():
    rows = np.arange(NS)
    angle = 2.0 * np.pi * (rows[:, None] * rows[None, :] % NS) / NS
    scale = 1.0 / np.sqrt(NS)
    cosine = (np.cos(angle) * scale).astype(np.float32)
    sine = (np.sin(angle) * scale).astype(np.float32)
    upper = np.concatenate([cosine, -sine], axis=1)
    lower = np.concatenate([sine, cosine], axis=1)
    table = np.concatenate([upper, lower], axis=0).astype(jnp.bfloat16)
    table = table.reshape(2 * NS, 2, NS // LANES, LANES).transpose(0, 2, 1, 3).reshape(2 * NS, 2 * NS)
    return (table.astype(np.float32) * 0.5).astype(jnp.bfloat16)


def columns(cyl):
    return slice(cyl * NS, (cyl + 1) * NS)


def form_powers(spectra, gain_ref, beam_ref, cal_ref, emit):
    half = BLOCK * UPCH
    for cyl in range(CYL):
        spec = spectra(cyl)
        real, imag = spec[:half], spec[half:]
        gain_real = gain_ref[cyl, 0:1, :]
        gain_imag = gain_ref[cyl, 1:2, :]
        rows = slice(cyl * half, (cyl + 1) * half)
        cal_ref[rows, :NS] = (real * gain_real - imag * gain_imag).astype(jnp.bfloat16)
        cal_ref[rows, NS:] = (real * gain_imag + imag * gain_real).astype(jnp.bfloat16)
    for strip in range(NS // LANES):
        beam = jnp.dot(
            cal_ref[...],
            beam_ref[:, strip * 2 * LANES : (strip + 1) * 2 * LANES],
            preferred_element_type=jnp.float32,
        )
        beams = [beam[cyl * half : (cyl + 1) * half] for cyl in range(CYL)]
        (r0, i0), (r1, i1), (r2, i2), (r3, i3) = [(b[:, :LANES], b[:, LANES:]) for b in beams]
        pr, pi, mr, mi = r0 + r2, i0 + i2, r0 - r2, i0 - i2
        sr, si, dr, di = r1 + r3, i1 + i3, r1 - r3, i1 - i3
        formed = [(pr + sr, pi + si), (mr + di, mi - dr), (pr - sr, pi - si), (mr - di, mi + dr)]
        for element, (fr, fi) in enumerate(formed):
            emit(element * NS + strip * LANES, fr * fr + fi * fi)


def filtered(terms):
    total = None
    for table, rows in terms:
        term = jnp.dot(table, rows, preferred_element_type=jnp.float32)
        total = term if total is None else total + term
    return total


def keeper(power_ref, at=0):
    rows = pl.ds(at, BLOCK * UPCH)

    def emit(column, power):
        power_ref[rows, column : column + LANES] = power.astype(jnp.bfloat16)

    return emit


def adder(power_ref, keep_ref, sum_ref, at=0):
    rows = pl.ds(at, BLOCK * UPCH)

    def emit(column, power):
        lanes = slice(column, column + LANES)
        total = power_ref[rows, lanes].astype(jnp.float32) + power.astype(jnp.bfloat16).astype(jnp.float32)
        sum_ref[rows, lanes] = (total * keep_ref[:, lanes].astype(jnp.float32)).astype(jnp.bfloat16)

    return emit


def place(sum_ref, table, out_ref):
    placed = jnp.dot(sum_ref[...], table, preferred_element_type=jnp.float32)
    out_ref[...] = placed.astype(jnp.bfloat16).reshape(out_ref.shape)


def place_kernel(pol, sum_ref, table_ref, *out_refs):
    @pl.when(lax.axis_index("pol") == pol)
    def _():
        for k, out_ref in enumerate(out_refs):
            place(sum_ref, table_ref[k], out_ref)


def halo_rows_kernel(x_ref, near_ref, far_ref):
    near_at = x_ref.shape[0] - near_ref.shape[0]
    near_ref[...] = x_ref[near_at:, :]
    far_ref[...] = x_ref[near_at - far_ref.shape[0] : near_at, :]


def each_late_block(blocks, filt_ref, x_ref, gain_ref, beam_ref, cal_ref, emitter):
    def step(block, carry):
        first = pl.multiple_of(block * BLOCK * ROWS, BLOCK * ROWS)
        rows = pl.ds(first, (TAPS + BLOCK) * ROWS)

        def spectra(cyl):
            return filtered([(filt_ref[...], x_ref[rows, columns(cyl)])])

        at = pl.multiple_of(block * BLOCK * UPCH, BLOCK * UPCH)
        form_powers(spectra, gain_ref, beam_ref, cal_ref, emitter(at))
        return carry

    lax.fori_loop(0, blocks, step, 0)


def late_own_kernel(blocks, filt_ref, x_ref, gain_ref, beam_ref, out_ref, cal_ref):
    @pl.when(lax.axis_index("pol") == 0)
    def _():
        each_late_block(blocks, filt_ref, x_ref, gain_ref, beam_ref, cal_ref, lambda at: keeper(out_ref, at))


def late_kernel(
    blocks, filt_ref, x_ref, gain_ref, beam_ref, keep_ref, table_ref, power_ref, sum_ref, out_ref, cal_ref
):
    @pl.when(lax.axis_index("pol") == 0)
    def _():
        def emitter(at):
            return adder(power_ref, keep_ref, sum_ref, at)

        each_late_block(blocks, filt_ref, x_ref, gain_ref, beam_ref, cal_ref, emitter)
        place(sum_ref, table_ref[table_ref.shape[0] - 1], out_ref)


def near_kernel(
    filt_ref, n0, n1, x0, x1, g0, g1, beam_ref, keep_ref, table_ref, sum_ref, out_ref, pre_ref, cal_ref
):
    reach = BLOCK * ROWS

    @pl.when(lax.axis_index("pol") == 1)
    def _():
        for pol, (n, x, gain) in enumerate(((n0, x0, g0), (n1, x1, g1))):

            def spectra(cyl, pol=pol, n=n, x=x):
                there = n[:, columns(cyl)]
                pre_ref[pol * CYL + cyl] = filtered(
                    [(filt_ref[:, reach : 2 * reach], there), (filt_ref[:, 2 * reach :], x[:reach, columns(cyl)])]
                )
                return filtered([(filt_ref[:, :reach], there), (filt_ref[:, reach:], x[: 2 * reach, columns(cyl)])])

            emit = adder(sum_ref, keep_ref, sum_ref) if pol else keeper(sum_ref)
            form_powers(spectra, gain, beam_ref, cal_ref, emit)
        place(sum_ref, table_ref[table_ref.shape[0] - 1], out_ref)


def far_kernel(
    edge_ref, f0, f1, g0, g1, beam_ref, keep_ref, table_ref, pre_ref, sum_ref, out_ref, next_ref, cal_ref
):
    @pl.when(lax.axis_index("pol") == 1)
    def _():
        for pol, (far_ref, gain) in enumerate(((f0, g0), (f1, g1))):

            def spectra(cyl, pol=pol, far_ref=far_ref):
                return pre_ref[pol * CYL + cyl] + filtered([(edge_ref[...], far_ref[:, columns(cyl)])])

            emit = adder(sum_ref, keep_ref, sum_ref) if pol else keeper(sum_ref)
            form_powers(spectra, gain, beam_ref, cal_ref, emit)
        place(sum_ref, table_ref[table_ref.shape[0] - 1], out_ref)
        place(sum_ref, table_ref[table_ref.shape[0] - 2], next_ref)


def far_place_kernel(sum_ref, table_ref, near_ref, late_ref, own_ref, *out_refs):
    @pl.when(lax.axis_index("pol") == 1)
    def _():
        for k, out_ref in enumerate(out_refs, 1):
            place(sum_ref, table_ref[k], out_ref)
        place(sum_ref, table_ref[0], own_ref.at[:BLOCK])
        own_ref[BLOCK:] = near_ref[...]

    @pl.when(lax.axis_index("pol") == 0)
    def _():
        own_ref[...] = late_ref[...]


def place_table_kernel(owner_ref, out_ref, rank_ref):
    n_owner = out_ref.shape[0]
    for owner in range(n_owner):
        rank_ref[owner] = 0
    out_ref[...] = jnp.zeros_like(out_ref)
    row = lax.broadcasted_iota(jnp.int32, (SET_BEAMS, LANES), 0)
    lane = lax.broadcasted_iota(jnp.int32, (SET_BEAMS, LANES), 1)

    def step(index, carry):
        owner = owner_ref[index]
        rank = rank_ref[owner]
        rank_ref[owner] = rank + 1
        column = rank * SET_BEAMS
        tile = column // LANES * LANES
        hit = lane - row == column - tile
        rows = pl.ds(pl.multiple_of(index * SET_BEAMS, SET_BEAMS), SET_BEAMS)
        lanes = pl.ds(pl.multiple_of(tile, LANES), LANES)
        out_ref[lax.axis_index("freq") ^ owner, rows, lanes] = jnp.where(hit, 1.0, 0.0).astype(jnp.bfloat16)
        return carry

    lax.fori_loop(0, owner_ref.shape[0], step, 0, unroll=4)


def put(out_ref, sems, blocks):
    copies = []
    for index, (block, frame, k) in enumerate(blocks):
        rows = pl.ds(pl.multiple_of((lax.axis_index("freq") ^ k) * UPCH, UPCH), UPCH)
        at = out_ref.at[pl.ds(frame, block.shape[0]), rows]
        copies.append(pltpu.make_async_copy(block, at, sems.at[index]))
    for copy in copies:
        copy.start()
    for copy in copies:
        copy.wait()


def early_gather_kernel(n_owner, own_ref, *refs):
    near, late, out_ref, sems = refs[: n_owner - 1], refs[n_owner - 1 : -2], refs[-2], refs[-1]
    own = [(own_ref, 0, 0)]

    @pl.when(lax.axis_index("pol") == 0)
    def _():
        put(out_ref, sems, own + [(block, BLOCK, k + 1) for k, block in enumerate(near)])

    @pl.when(lax.axis_index("pol") == 1)
    def _():
        put(out_ref, sems, own + [(block, 0, k + 1) for k, block in enumerate(late)])


def last_gather_kernel(n_owner, *refs):
    far, out_ref, sems = refs[: n_owner - 1], refs[-2], refs[-1]

    @pl.when(lax.axis_index("pol") == 0)
    def _():
        put(out_ref, sems, [(block, 0, k + 1) for k, block in enumerate(far)])


VMEM = pl.BlockSpec(memory_space=pltpu.VMEM)
SMEM = pl.BlockSpec(memory_space=pltpu.SMEM)
ANY = pl.BlockSpec(memory_space=pl.ANY)


def call(body, out_shape, n_in, flops, nbytes, scalars=0, whole=0, after=0, scratch=()):
    many = isinstance(out_shape, (list, tuple))

    def kernel(*refs):
        seen = scalars + n_in + whole
        body(*refs[:seen], *refs[seen + after :])

    return pl.pallas_call(
        kernel,
        out_shape=out_shape,
        in_specs=[SMEM] * scalars + [VMEM] * n_in + [ANY] * (whole + after),
        out_specs=[VMEM] * len(out_shape) if many else VMEM,
        scratch_shapes=list(scratch),
        cost_estimate=pl.CostEstimate(flops=flops, bytes_accessed=nbytes, transcendentals=0),
        compiler_params=pltpu.CompilerParams(vmem_limit_bytes=24 << 20),
    )


def per_device(voltages, feed_gains, owner_table, keep_flags):
    samples = voltages[0, 0]
    gain = feed_gains[0, 0]
    frame_count = samples.shape[0] // UPCH
    kept = frame_count // 2
    n_owner = lax.axis_size("freq")
    assert voltages.shape[1] == 1 and kept == 2 * BLOCK and kept >= TAPS
    assert n_owner & (n_owner - 1) == 0
    n_tm = lax.axis_size("tm")
    most_sets = 2 * owner_table.shape[0] // n_owner
    beams = keep_flags.shape[0]
    width = most_sets * SET_BEAMS
    bf16 = jnp.bfloat16
    filt = jnp.asarray(filter_matrix())
    edge = jnp.asarray(filter_matrix()[:, ROWS : BLOCK * ROWS])
    beam_table = jnp.asarray(beam_matrix())

    pairs = [(i, i + 1) for i in range(n_tm - 1)]

    def ahead(part, source):
        return lax.ppermute(part, ("tm", "pol"), [(i * 2 + source, j * 2 + 1) for i, j in pairs])

    def swap(part):
        return lax.ppermute(part, "pol", [(0, 1), (1, 0)])

    def spread(blocks, source):
        got = []
        for k in range(1, n_owner):
            route = [(i * 2 + source, (i ^ k) * 2 + 1 - source) for i in range(n_owner)]
            got.append(lax.ppermute(blocks[k], ("freq", "pol"), route))
        return got

    def form(body, frames, *arrays, more=()):
        shape = [jax.ShapeDtypeStruct((frames * UPCH, beams), bf16), jax.ShapeDtypeStruct((frames, UPCH, width), bf16)]
        scratch = [pltpu.VMEM((CYL * BLOCK * UPCH, 2 * NS), bf16)]
        return call(
            body, shape + list(more), len(arrays), 4 * 512 * 1024 * 1024, 4 << 20, scratch=scratch
        )(*arrays)

    def rest(body, frames, *arrays, more=(), count=n_owner - 1):
        shape = [jax.ShapeDtypeStruct((frames, UPCH, width), bf16)] * count
        return call(body, list(more) + shape, len(arrays), 1 << 29, 4 << 20)(*arrays)

    keep = keep_flags.reshape(1, -1)
    reach, edge_rows = BLOCK * ROWS, (TAPS - 1 - BLOCK) * ROWS
    blocks = kept // BLOCK
    table = call(
        place_table_kernel,
        jax.ShapeDtypeStruct((n_owner, beams, width), bf16),
        0,
        1 << 20,
        4 << 20,
        scalars=1,
        scratch=[pltpu.SMEM((n_owner,), jnp.int32)],
    )(owner_table)
    samples, table = lax.optimization_barrier((samples, table))
    x = samples.transpose(0, 2, 1, 3).reshape(samples.shape[0] * 2, CYL * NS)
    x = lax.optimization_barrier(x)
    near_rows, far_rows = call(
        halo_rows_kernel,
        [jax.ShapeDtypeStruct((rows, CYL * NS), bf16) for rows in (reach, edge_rows)],
        1,
        0,
        2 << 20,
    )(x)
    near0 = ahead(near_rows, 0)
    near1 = ahead(near_rows, 1)
    other = swap(x)
    gain_other = swap(gain)
    far0 = ahead(far_rows, 0)
    far1 = ahead(far_rows, 1)
    late_own = call(
        functools.partial(late_own_kernel, blocks),
        jax.ShapeDtypeStruct((kept * UPCH, beams), bf16),
        4,
        4 * 512 * 1024 * 1024,
        4 << 20,
        scratch=[pltpu.VMEM((CYL * BLOCK * UPCH, 2 * NS), bf16)],
    )(filt, x, gain, beam_table)
    late_sum, late_last = form(
        functools.partial(late_kernel, blocks), kept, filt, other, gain_other, beam_table, keep, table, late_own
    )
    late = [*rest(functools.partial(place_kernel, 0), kept, late_sum, table), late_last]
    late_got = spread(late, 0)
    common = (gain, gain_other, beam_table, keep, table)
    near_sum, near_last, pre = form(
        near_kernel,
        BLOCK,
        filt,
        near1,
        near0,
        x,
        other,
        *common,
        more=[jax.ShapeDtypeStruct((2 * CYL, reach, NS), jnp.float32)],
    )
    near = [*rest(functools.partial(place_kernel, 1), BLOCK, near_sum, table), near_last]
    near_got = spread(near, 1)
    block_shape = jax.ShapeDtypeStruct((BLOCK, UPCH, width), bf16)
    far_sum, far_last, far_next = form(far_kernel, BLOCK, edge, far1, far0, *common, pre, more=[block_shape])
    own, *far = rest(
        far_place_kernel,
        BLOCK,
        far_sum,
        table,
        near[0],
        late[0],
        more=[jax.ShapeDtypeStruct((kept, UPCH, width), bf16)],
        count=n_owner - 3,
    )
    far = [own, *far, far_next, far_last]
    far_got = spread(far, 1)
    own_got = swap(own)
    out_shape = jax.ShapeDtypeStruct((kept, n_owner * UPCH, width), bf16)

    def gather(body, arrays, base=()):
        return pl.pallas_call(
            functools.partial(body, n_owner),
            out_shape=out_shape,
            in_specs=[VMEM] * len(arrays) + [ANY] * len(base),
            out_specs=ANY,
            scratch_shapes=[pltpu.SemaphoreType.DMA((n_owner,))],
            input_output_aliases={len(arrays): 0} if base else {},
            cost_estimate=pl.CostEstimate(flops=0, bytes_accessed=2 << 20, transcendentals=0),
            compiler_params=pltpu.CompilerParams(vmem_limit_bytes=24 << 20),
        )(*arrays, *base)

    out = gather(early_gather_kernel, [own_got, *near_got, *late_got])
    return gather(last_gather_kernel, far_got, base=[out])


def solution(mesh):
    return jax.shard_map(
        per_device,
        mesh=mesh,
        in_specs=(
            P("pol", ("grp", "freq"), "tm", None, None, None),
            P(("grp", "freq"), "pol", None, None, None),
            P(),
            P(),
        ),
        out_specs=P(("grp", "tm", "pol"), None, "freq"),
        check_vma=False,
    )
```

```python
import functools

import jax
import jax.numpy as jnp
import numpy as np
from jax import lax
from jax.experimental import pallas as pl
from jax.experimental.pallas import tpu as pltpu
from jax.sharding import PartitionSpec as P


NS = 256
CYL = 4
UPCH = 16
TAPS = 16
SET_BEAMS = 16
BLOCK = 8
LANES = 128
ROWS = 2 * UPCH


def window_taps():
    span = TAPS * UPCH
    steps = np.arange(span, dtype=np.float64)
    weights = np.sinc((steps - (span - 1) / 2.0) / UPCH) * np.sin(np.pi * (steps + 0.5) / span) ** 2
    return weights / np.sqrt(np.sum(weights * weights))


def filter_matrix():
    weights = window_taps()
    fine = np.arange(UPCH)
    sample = np.arange(TAPS * UPCH)
    phase = 2.0 * np.pi * ((fine[:, None] * sample[None, :]) % UPCH) / UPCH
    cosine = np.cos(phase) * weights
    sine = np.sin(phase) * weights
    table = np.zeros((2, BLOCK, UPCH, TAPS + BLOCK, UPCH, 2))
    for frame in range(BLOCK):
        taps = slice(frame + 1, frame + 1 + TAPS)
        cos_part = cosine.reshape(UPCH, TAPS, UPCH)
        sin_part = sine.reshape(UPCH, TAPS, UPCH)
        table[0, frame, :, taps, :, 0] = cos_part
        table[0, frame, :, taps, :, 1] = sin_part
        table[1, frame, :, taps, :, 0] = -sin_part
        table[1, frame, :, taps, :, 1] = cos_part
    return table.reshape(2 * BLOCK * UPCH, (TAPS + BLOCK) * ROWS).astype(np.float32).astype(jnp.bfloat16)


def beam_matrix():
    rows = np.arange(NS)
    angle = 2.0 * np.pi * (rows[:, None] * rows[None, :] % NS) / NS
    scale = 1.0 / np.sqrt(NS)
    cosine = (np.cos(angle) * scale).astype(np.float32)
    sine = (np.sin(angle) * scale).astype(np.float32)
    upper = np.concatenate([cosine, -sine], axis=1)
    lower = np.concatenate([sine, cosine], axis=1)
    table = np.concatenate([upper, lower], axis=0).astype(jnp.bfloat16)
    table = table.reshape(2 * NS, 2, NS // LANES, LANES).transpose(0, 2, 1, 3).reshape(2 * NS, 2 * NS)
    return (table.astype(np.float32) * 0.5).astype(jnp.bfloat16)


def columns(cyl):
    return slice(cyl * NS, (cyl + 1) * NS)


def form_powers(spectra, gain_ref, beam_ref, cal_ref, emit):
    half = BLOCK * UPCH
    for cyl in range(CYL):
        spec = spectra(cyl)
        real, imag = spec[:half], spec[half:]
        gain_real = gain_ref[cyl, 0:1, :]
        gain_imag = gain_ref[cyl, 1:2, :]
        rows = slice(cyl * half, (cyl + 1) * half)
        cal_ref[rows, :NS] = (real * gain_real - imag * gain_imag).astype(jnp.bfloat16)
        cal_ref[rows, NS:] = (real * gain_imag + imag * gain_real).astype(jnp.bfloat16)
    for strip in range(NS // LANES):
        beam = jnp.dot(
            cal_ref[...],
            beam_ref[:, strip * 2 * LANES : (strip + 1) * 2 * LANES],
            preferred_element_type=jnp.float32,
        )
        beams = [beam[cyl * half : (cyl + 1) * half] for cyl in range(CYL)]
        (r0, i0), (r1, i1), (r2, i2), (r3, i3) = [(b[:, :LANES], b[:, LANES:]) for b in beams]
        pr, pi, mr, mi = r0 + r2, i0 + i2, r0 - r2, i0 - i2
        sr, si, dr, di = r1 + r3, i1 + i3, r1 - r3, i1 - i3
        formed = [(pr + sr, pi + si), (mr + di, mi - dr), (pr - sr, pi - si), (mr - di, mi + dr)]
        for element, (fr, fi) in enumerate(formed):
            emit(element * NS + strip * LANES, fr * fr + fi * fi)


def filtered(terms):
    total = None
    for table, rows in terms:
        term = jnp.dot(table, rows, preferred_element_type=jnp.float32)
        total = term if total is None else total + term
    return total


def keeper(power_ref, at=0):
    rows = pl.ds(at, BLOCK * UPCH)

    def emit(column, power):
        power_ref[rows, column : column + LANES] = power.astype(jnp.bfloat16)

    return emit


def adder(power_ref, keep_ref, sum_ref, at=0):
    rows = pl.ds(at, BLOCK * UPCH)

    def emit(column, power):
        lanes = slice(column, column + LANES)
        total = power_ref[rows, lanes].astype(jnp.float32) + power.astype(jnp.bfloat16).astype(jnp.float32)
        sum_ref[rows, lanes] = (total * keep_ref[:, lanes].astype(jnp.float32)).astype(jnp.bfloat16)

    return emit


def place(sum_ref, table, out_ref):
    placed = jnp.dot(sum_ref[...], table, preferred_element_type=jnp.float32)
    out_ref[...] = placed.astype(jnp.bfloat16).reshape(out_ref.shape)


def place_kernel(pol, sum_ref, table_ref, *out_refs):
    @pl.when(lax.axis_index("pol") == pol)
    def _():
        for k, out_ref in enumerate(out_refs):
            place(sum_ref, table_ref[k], out_ref)


def halo_rows_kernel(x_ref, near_ref, far_ref):
    near_at = x_ref.shape[0] - near_ref.shape[0]
    near_ref[...] = x_ref[near_at:, :]
    far_ref[...] = x_ref[near_at - far_ref.shape[0] : near_at, :]


def each_late_block(blocks, filt_ref, x_ref, gain_ref, beam_ref, cal_ref, emitter):
    def step(block, carry):
        first = pl.multiple_of(block * BLOCK * ROWS, BLOCK * ROWS)
        rows = pl.ds(first, (TAPS + BLOCK) * ROWS)

        def spectra(cyl):
            return filtered([(filt_ref[...], x_ref[rows, columns(cyl)])])

        at = pl.multiple_of(block * BLOCK * UPCH, BLOCK * UPCH)
        form_powers(spectra, gain_ref, beam_ref, cal_ref, emitter(at))
        return carry

    lax.fori_loop(0, blocks, step, 0)


def late_own_kernel(blocks, filt_ref, x_ref, gain_ref, beam_ref, out_ref, cal_ref):
    @pl.when(lax.axis_index("pol") == 0)
    def _():
        each_late_block(blocks, filt_ref, x_ref, gain_ref, beam_ref, cal_ref, lambda at: keeper(out_ref, at))


def late_kernel(
    blocks, filt_ref, x_ref, gain_ref, beam_ref, keep_ref, table_ref, power_ref, sum_ref, out_ref, cal_ref
):
    @pl.when(lax.axis_index("pol") == 0)
    def _():
        def emitter(at):
            return adder(power_ref, keep_ref, sum_ref, at)

        each_late_block(blocks, filt_ref, x_ref, gain_ref, beam_ref, cal_ref, emitter)
        place(sum_ref, table_ref[table_ref.shape[0] - 1], out_ref)


def near_kernel(
    filt_ref, n0, n1, x0, x1, g0, g1, beam_ref, keep_ref, table_ref, sum_ref, out_ref, cal_ref
):
    reach = BLOCK * ROWS

    @pl.when(lax.axis_index("pol") == 1)
    def _():
        for pol, (n, x, gain) in enumerate(((n0, x0, g0), (n1, x1, g1))):

            def spectra(cyl, n=n, x=x):
                there, here = n[:, columns(cyl)], x[: 2 * reach, columns(cyl)]
                return filtered([(filt_ref[:, :reach], there), (filt_ref[:, reach:], here)])

            emit = adder(sum_ref, keep_ref, sum_ref) if pol else keeper(sum_ref)
            form_powers(spectra, gain, beam_ref, cal_ref, emit)
        place(sum_ref, table_ref[table_ref.shape[0] - 1], out_ref)


def ahead_kernel(filt_ref, n0, n1, x0, x1, pre_ref):
    reach = BLOCK * ROWS

    @pl.when(lax.axis_index("pol") == 1)
    def _():
        for pol, (n, x) in enumerate(((n0, x0), (n1, x1))):
            for cyl in range(CYL):
                there, here = n[:, columns(cyl)], x[:reach, columns(cyl)]
                terms = [(filt_ref[:, reach : 2 * reach], there), (filt_ref[:, 2 * reach :], here)]
                pre_ref[pol * CYL + cyl] = filtered(terms)


def far_kernel(
    edge_ref, f0, f1, g0, g1, beam_ref, keep_ref, table_ref, pre_ref, sum_ref, out_ref, next_ref, cal_ref
):
    @pl.when(lax.axis_index("pol") == 1)
    def _():
        for pol, (far_ref, gain) in enumerate(((f0, g0), (f1, g1))):

            def spectra(cyl, pol=pol, far_ref=far_ref):
                return pre_ref[pol * CYL + cyl] + filtered([(edge_ref[...], far_ref[:, columns(cyl)])])

            emit = adder(sum_ref, keep_ref, sum_ref) if pol else keeper(sum_ref)
            form_powers(spectra, gain, beam_ref, cal_ref, emit)
        place(sum_ref, table_ref[table_ref.shape[0] - 1], out_ref)
        place(sum_ref, table_ref[table_ref.shape[0] - 2], next_ref)


def far_place_kernel(sum_ref, table_ref, near_ref, late_ref, own_ref, *out_refs):
    @pl.when(lax.axis_index("pol") == 1)
    def _():
        for k, out_ref in enumerate(out_refs, 1):
            place(sum_ref, table_ref[k], out_ref)
        place(sum_ref, table_ref[0], own_ref.at[:BLOCK])
        own_ref[BLOCK:] = near_ref[...]

    @pl.when(lax.axis_index("pol") == 0)
    def _():
        own_ref[...] = late_ref[...]


def place_table_kernel(owner_ref, out_ref, rank_ref):
    n_owner = out_ref.shape[0]
    for owner in range(n_owner):
        rank_ref[owner] = 0
    out_ref[...] = jnp.zeros_like(out_ref)
    row = lax.broadcasted_iota(jnp.int32, (SET_BEAMS, LANES), 0)
    lane = lax.broadcasted_iota(jnp.int32, (SET_BEAMS, LANES), 1)

    def step(index, carry):
        owner = owner_ref[index]
        rank = rank_ref[owner]
        rank_ref[owner] = rank + 1
        column = rank * SET_BEAMS
        tile = column // LANES * LANES
        hit = lane - row == column - tile
        rows = pl.ds(pl.multiple_of(index * SET_BEAMS, SET_BEAMS), SET_BEAMS)
        lanes = pl.ds(pl.multiple_of(tile, LANES), LANES)
        out_ref[lax.axis_index("freq") ^ owner, rows, lanes] = jnp.where(hit, 1.0, 0.0).astype(jnp.bfloat16)
        return carry

    lax.fori_loop(0, owner_ref.shape[0], step, 0, unroll=4)


def put(out_ref, sems, blocks):
    copies = []
    for index, (block, frame, k) in enumerate(blocks):
        rows = pl.ds(pl.multiple_of((lax.axis_index("freq") ^ k) * UPCH, UPCH), UPCH)
        at = out_ref.at[pl.ds(frame, block.shape[0]), rows]
        copies.append(pltpu.make_async_copy(block, at, sems.at[index]))
    for copy in copies:
        copy.start()
    for copy in copies:
        copy.wait()


def early_gather_kernel(n_owner, own_ref, *refs):
    near, late, out_ref, sems = refs[: n_owner - 1], refs[n_owner - 1 : -2], refs[-2], refs[-1]
    own = [(own_ref, 0, 0)]

    @pl.when(lax.axis_index("pol") == 0)
    def _():
        put(out_ref, sems, own + [(block, BLOCK, k + 1) for k, block in enumerate(near)])

    @pl.when(lax.axis_index("pol") == 1)
    def _():
        put(out_ref, sems, own + [(block, 0, k + 1) for k, block in enumerate(late)])


def last_gather_kernel(n_owner, *refs):
    far, out_ref, sems = refs[: n_owner - 1], refs[-2], refs[-1]

    @pl.when(lax.axis_index("pol") == 0)
    def _():
        put(out_ref, sems, [(block, 0, k + 1) for k, block in enumerate(far)])


VMEM = pl.BlockSpec(memory_space=pltpu.VMEM)
SMEM = pl.BlockSpec(memory_space=pltpu.SMEM)
ANY = pl.BlockSpec(memory_space=pl.ANY)


def call(body, out_shape, n_in, flops, nbytes, scalars=0, whole=0, after=0, scratch=()):
    many = isinstance(out_shape, (list, tuple))

    def kernel(*refs):
        seen = scalars + n_in + whole
        body(*refs[:seen], *refs[seen + after :])

    return pl.pallas_call(
        kernel,
        out_shape=out_shape,
        in_specs=[SMEM] * scalars + [VMEM] * n_in + [ANY] * (whole + after),
        out_specs=[VMEM] * len(out_shape) if many else VMEM,
        scratch_shapes=list(scratch),
        cost_estimate=pl.CostEstimate(flops=flops, bytes_accessed=nbytes, transcendentals=0),
        compiler_params=pltpu.CompilerParams(vmem_limit_bytes=24 << 20),
    )


def per_device(voltages, feed_gains, owner_table, keep_flags):
    samples = voltages[0, 0]
    gain = feed_gains[0, 0]
    frame_count = samples.shape[0] // UPCH
    kept = frame_count // 2
    n_owner = lax.axis_size("freq")
    assert voltages.shape[1] == 1 and kept == 2 * BLOCK and kept >= TAPS
    assert n_owner & (n_owner - 1) == 0
    n_tm = lax.axis_size("tm")
    most_sets = 2 * owner_table.shape[0] // n_owner
    beams = keep_flags.shape[0]
    width = most_sets * SET_BEAMS
    bf16 = jnp.bfloat16
    filt = jnp.asarray(filter_matrix())
    edge = jnp.asarray(filter_matrix()[:, ROWS : BLOCK * ROWS])
    beam_table = jnp.asarray(beam_matrix())

    pairs = [(i, i + 1) for i in range(n_tm - 1)]

    def ahead(part, source):
        return lax.ppermute(part, ("tm", "pol"), [(i * 2 + source, j * 2 + 1) for i, j in pairs])

    def swap(part):
        return lax.ppermute(part, "pol", [(0, 1), (1, 0)])

    def spread(blocks, source):
        got = []
        for k in range(1, n_owner):
            route = [(i * 2 + source, (i ^ k) * 2 + 1 - source) for i in range(n_owner)]
            got.append(lax.ppermute(blocks[k], ("freq", "pol"), route))
        return got

    def form(body, frames, *arrays, more=()):
        shape = [jax.ShapeDtypeStruct((frames * UPCH, beams), bf16), jax.ShapeDtypeStruct((frames, UPCH, width), bf16)]
        scratch = [pltpu.VMEM((CYL * BLOCK * UPCH, 2 * NS), bf16)]
        return call(
            body, shape + list(more), len(arrays), 4 * 512 * 1024 * 1024, 4 << 20, scratch=scratch
        )(*arrays)

    def rest(body, frames, *arrays, more=(), count=n_owner - 1):
        shape = [jax.ShapeDtypeStruct((frames, UPCH, width), bf16)] * count
        return call(body, list(more) + shape, len(arrays), 1 << 29, 4 << 20)(*arrays)

    keep = keep_flags.reshape(1, -1)
    reach, edge_rows = BLOCK * ROWS, (TAPS - 1 - BLOCK) * ROWS
    blocks = kept // BLOCK
    x = samples.transpose(0, 2, 1, 3).reshape(samples.shape[0] * 2, CYL * NS)
    x = lax.optimization_barrier(x)
    near_rows, far_rows = call(
        halo_rows_kernel,
        [jax.ShapeDtypeStruct((rows, CYL * NS), bf16) for rows in (reach, edge_rows)],
        1,
        0,
        2 << 20,
    )(x)
    near0 = ahead(near_rows, 0)
    near1 = ahead(near_rows, 1)
    other = swap(x)
    gain_other = swap(gain)
    far0 = ahead(far_rows, 0)
    far1 = ahead(far_rows, 1)
    late_own = call(
        functools.partial(late_own_kernel, blocks),
        jax.ShapeDtypeStruct((kept * UPCH, beams), bf16),
        4,
        4 * 512 * 1024 * 1024,
        4 << 20,
        scratch=[pltpu.VMEM((CYL * BLOCK * UPCH, 2 * NS), bf16)],
    )(filt, x, gain, beam_table)
    table = call(
        place_table_kernel,
        jax.ShapeDtypeStruct((n_owner, beams, width), bf16),
        0,
        1 << 20,
        4 << 20,
        scalars=1,
        after=1,
        scratch=[pltpu.SMEM((n_owner,), jnp.int32)],
    )(owner_table, late_own)
    late_sum, late_last = form(
        functools.partial(late_kernel, blocks), kept, filt, other, gain_other, beam_table, keep, table, late_own
    )
    late = [*rest(functools.partial(place_kernel, 0), kept, late_sum, table), late_last]
    late_got = spread(late, 0)
    common = (gain, gain_other, beam_table, keep, table)
    near_sum, near_last = form(near_kernel, BLOCK, filt, near1, near0, x, other, *common)
    near = [*rest(functools.partial(place_kernel, 1), BLOCK, near_sum, table), near_last]
    near_got = spread(near, 1)
    pre = call(
        ahead_kernel,
        jax.ShapeDtypeStruct((2 * CYL, reach, NS), jnp.float32),
        5,
        2 * 512 * 1024 * 1024,
        4 << 20,
        after=1,
    )(filt, near1, near0, x, other, near[0])
    block_shape = jax.ShapeDtypeStruct((BLOCK, UPCH, width), bf16)
    far_sum, far_last, far_next = form(far_kernel, BLOCK, edge, far1, far0, *common, pre, more=[block_shape])
    own, *far = rest(
        far_place_kernel,
        BLOCK,
        far_sum,
        table,
        near[0],
        late[0],
        more=[jax.ShapeDtypeStruct((kept, UPCH, width), bf16)],
        count=n_owner - 3,
    )
    far = [own, *far, far_next, far_last]
    far_got = spread(far, 1)
    own_got = swap(own)
    out_shape = jax.ShapeDtypeStruct((kept, n_owner * UPCH, width), bf16)

    def gather(body, arrays, base=()):
        return pl.pallas_call(
            functools.partial(body, n_owner),
            out_shape=out_shape,
            in_specs=[VMEM] * len(arrays) + [ANY] * len(base),
            out_specs=ANY,
            scratch_shapes=[pltpu.SemaphoreType.DMA((n_owner,))],
            input_output_aliases={len(arrays): 0} if base else {},
            cost_estimate=pl.CostEstimate(flops=0, bytes_accessed=2 << 20, transcendentals=0),
            compiler_params=pltpu.CompilerParams(vmem_limit_bytes=24 << 20),
        )(*arrays, *base)

    out = gather(early_gather_kernel, [own_got, *near_got, *late_got])
    return gather(last_gather_kernel, far_got, base=[out])


def solution(mesh):
    return jax.shard_map(
        per_device,
        mesh=mesh,
        in_specs=(
            P("pol", ("grp", "freq"), "tm", None, None, None),
            P(("grp", "freq"), "pol", None, None, None),
            P(),
            P(),
        ),
        out_specs=P(("grp", "tm", "pol"), None, "freq"),
        check_vma=False,
    )
```

```python
import functools

import jax
import jax.numpy as jnp
import numpy as np
from jax import lax
from jax.experimental import pallas as pl
from jax.experimental.pallas import tpu as pltpu
from jax.sharding import PartitionSpec as P


NS = 256
CYL = 4
UPCH = 16
TAPS = 16
SET_BEAMS = 16
BLOCK = 8
LANES = 128
ROWS = 2 * UPCH


def window_taps():
    span = TAPS * UPCH
    steps = np.arange(span, dtype=np.float64)
    weights = np.sinc((steps - (span - 1) / 2.0) / UPCH) * np.sin(np.pi * (steps + 0.5) / span) ** 2
    return weights / np.sqrt(np.sum(weights * weights))


def filter_matrix():
    weights = window_taps()
    fine = np.arange(UPCH)
    sample = np.arange(TAPS * UPCH)
    phase = 2.0 * np.pi * ((fine[:, None] * sample[None, :]) % UPCH) / UPCH
    cosine = np.cos(phase) * weights
    sine = np.sin(phase) * weights
    table = np.zeros((2, BLOCK, UPCH, TAPS + BLOCK, UPCH, 2))
    for frame in range(BLOCK):
        taps = slice(frame + 1, frame + 1 + TAPS)
        cos_part = cosine.reshape(UPCH, TAPS, UPCH)
        sin_part = sine.reshape(UPCH, TAPS, UPCH)
        table[0, frame, :, taps, :, 0] = cos_part
        table[0, frame, :, taps, :, 1] = sin_part
        table[1, frame, :, taps, :, 0] = -sin_part
        table[1, frame, :, taps, :, 1] = cos_part
    return table.reshape(2 * BLOCK * UPCH, (TAPS + BLOCK) * ROWS).astype(np.float32).astype(jnp.bfloat16)


def beam_matrix():
    rows = np.arange(NS)
    angle = 2.0 * np.pi * (rows[:, None] * rows[None, :] % NS) / NS
    scale = 1.0 / np.sqrt(NS)
    cosine = (np.cos(angle) * scale).astype(np.float32)
    sine = (np.sin(angle) * scale).astype(np.float32)
    upper = np.concatenate([cosine, -sine], axis=1)
    lower = np.concatenate([sine, cosine], axis=1)
    table = np.concatenate([upper, lower], axis=0).astype(jnp.bfloat16)
    table = table.reshape(2 * NS, 2, NS // LANES, LANES).transpose(0, 2, 1, 3).reshape(2 * NS, 2 * NS)
    return (table.astype(np.float32) * 0.5).astype(jnp.bfloat16)


def columns(cyl):
    return slice(cyl * NS, (cyl + 1) * NS)


def form_powers(spectra, gain_ref, beam_ref, cal_ref, emit):
    half = BLOCK * UPCH
    for cyl in range(CYL):
        spec = spectra(cyl)
        real, imag = spec[:half], spec[half:]
        gain_real = gain_ref[cyl, 0:1, :]
        gain_imag = gain_ref[cyl, 1:2, :]
        rows = slice(cyl * half, (cyl + 1) * half)
        cal_ref[rows, :NS] = (real * gain_real - imag * gain_imag).astype(jnp.bfloat16)
        cal_ref[rows, NS:] = (real * gain_imag + imag * gain_real).astype(jnp.bfloat16)
    for strip in range(NS // LANES):
        beam = jnp.dot(
            cal_ref[...],
            beam_ref[:, strip * 2 * LANES : (strip + 1) * 2 * LANES],
            preferred_element_type=jnp.float32,
        )
        beams = [beam[cyl * half : (cyl + 1) * half] for cyl in range(CYL)]
        (r0, i0), (r1, i1), (r2, i2), (r3, i3) = [(b[:, :LANES], b[:, LANES:]) for b in beams]
        pr, pi, mr, mi = r0 + r2, i0 + i2, r0 - r2, i0 - i2
        sr, si, dr, di = r1 + r3, i1 + i3, r1 - r3, i1 - i3
        formed = [(pr + sr, pi + si), (mr + di, mi - dr), (pr - sr, pi - si), (mr - di, mi + dr)]
        for element, (fr, fi) in enumerate(formed):
            emit(element * NS + strip * LANES, fr * fr + fi * fi)


def filtered(terms):
    total = None
    for table, rows in terms:
        term = jnp.dot(table, rows, preferred_element_type=jnp.float32)
        total = term if total is None else total + term
    return total


def keeper(power_ref, at=0):
    rows = pl.ds(at, BLOCK * UPCH)

    def emit(column, power):
        power_ref[rows, column : column + LANES] = power.astype(jnp.bfloat16)

    return emit


def adder(power_ref, keep_ref, sum_ref, at=0):
    rows = pl.ds(at, BLOCK * UPCH)

    def emit(column, power):
        lanes = slice(column, column + LANES)
        total = power_ref[rows, lanes].astype(jnp.float32) + power.astype(jnp.bfloat16).astype(jnp.float32)
        sum_ref[rows, lanes] = (total * keep_ref[:, lanes].astype(jnp.float32)).astype(jnp.bfloat16)

    return emit


def place(sum_ref, table, out_ref):
    placed = jnp.dot(sum_ref[...], table, preferred_element_type=jnp.float32)
    out_ref[...] = placed.astype(jnp.bfloat16).reshape(out_ref.shape)


def place_kernel(pol, sum_ref, table_ref, *out_refs):
    @pl.when(lax.axis_index("pol") == pol)
    def _():
        for k, out_ref in enumerate(out_refs):
            place(sum_ref, table_ref[k], out_ref)


def far_rows_kernel(reach, x_ref, out_ref):
    at = x_ref.shape[0] - reach - out_ref.shape[0]
    out_ref[...] = x_ref[at : at + out_ref.shape[0], :]


def each_late_block(blocks, filt_ref, x_ref, gain_ref, beam_ref, cal_ref, emitter):
    def step(block, carry):
        first = pl.multiple_of(block * BLOCK * ROWS, BLOCK * ROWS)
        rows = pl.ds(first, (TAPS + BLOCK) * ROWS)

        def spectra(cyl):
            return filtered([(filt_ref[...], x_ref[rows, columns(cyl)])])

        at = pl.multiple_of(block * BLOCK * UPCH, BLOCK * UPCH)
        form_powers(spectra, gain_ref, beam_ref, cal_ref, emitter(at))
        return carry

    lax.fori_loop(0, blocks, step, 0)


def late_own_kernel(blocks, filt_ref, x_ref, gain_ref, beam_ref, out_ref, cal_ref):
    @pl.when(lax.axis_index("pol") == 0)
    def _():
        each_late_block(blocks, filt_ref, x_ref, gain_ref, beam_ref, cal_ref, lambda at: keeper(out_ref, at))


def late_kernel(
    blocks, filt_ref, x_ref, gain_ref, beam_ref, keep_ref, table_ref, power_ref, sum_ref, out_ref, cal_ref
):
    @pl.when(lax.axis_index("pol") == 0)
    def _():
        def emitter(at):
            return adder(power_ref, keep_ref, sum_ref, at)

        each_late_block(blocks, filt_ref, x_ref, gain_ref, beam_ref, cal_ref, emitter)
        place(sum_ref, table_ref[table_ref.shape[0] - 1], out_ref)


def near_kernel(
    filt_ref, n0, n1, x0, x1, g0, g1, beam_ref, keep_ref, table_ref, sum_ref, out_ref, cal_ref
):
    reach = BLOCK * ROWS

    @pl.when(lax.axis_index("pol") == 1)
    def _():
        for pol, (n, x, gain) in enumerate(((n0, x0, g0), (n1, x1, g1))):

            def spectra(cyl, n=n, x=x):
                there, here = n[:, columns(cyl)], x[: 2 * reach, columns(cyl)]
                return filtered([(filt_ref[:, :reach], there), (filt_ref[:, reach:], here)])

            emit = adder(sum_ref, keep_ref, sum_ref) if pol else keeper(sum_ref)
            form_powers(spectra, gain, beam_ref, cal_ref, emit)
        place(sum_ref, table_ref[table_ref.shape[0] - 1], out_ref)


def ahead_kernel(filt_ref, n0, n1, x0, x1, pre_ref):
    reach = BLOCK * ROWS

    @pl.when(lax.axis_index("pol") == 1)
    def _():
        for pol, (n, x) in enumerate(((n0, x0), (n1, x1))):
            for cyl in range(CYL):
                there, here = n[:, columns(cyl)], x[:reach, columns(cyl)]
                terms = [(filt_ref[:, reach : 2 * reach], there), (filt_ref[:, 2 * reach :], here)]
                pre_ref[pol * CYL + cyl] = filtered(terms)


def far_kernel(
    edge_ref, f0, f1, g0, g1, beam_ref, keep_ref, table_ref, pre_ref, sum_ref, out_ref, next_ref, cal_ref
):
    @pl.when(lax.axis_index("pol") == 1)
    def _():
        for pol, (far_ref, gain) in enumerate(((f0, g0), (f1, g1))):

            def spectra(cyl, pol=pol, far_ref=far_ref):
                return pre_ref[pol * CYL + cyl] + filtered([(edge_ref[...], far_ref[:, columns(cyl)])])

            emit = adder(sum_ref, keep_ref, sum_ref) if pol else keeper(sum_ref)
            form_powers(spectra, gain, beam_ref, cal_ref, emit)
        place(sum_ref, table_ref[table_ref.shape[0] - 1], out_ref)
        place(sum_ref, table_ref[table_ref.shape[0] - 2], next_ref)


def far_place_kernel(sum_ref, table_ref, near_ref, late_ref, own_ref, *out_refs):
    @pl.when(lax.axis_index("pol") == 1)
    def _():
        for k, out_ref in enumerate(out_refs, 1):
            place(sum_ref, table_ref[k], out_ref)
        place(sum_ref, table_ref[0], own_ref.at[:BLOCK])
        own_ref[BLOCK:] = near_ref[...]

    @pl.when(lax.axis_index("pol") == 0)
    def _():
        own_ref[...] = late_ref[...]


def head_kernel(owner_ref, v_ref, table_ref, near_ref, held_ref, rank_ref, sems):
    count = held_ref.shape[1]
    strips = NS // LANES
    copies = [
        pltpu.make_async_copy(
            v_ref.at[pl.ds(v_ref.shape[0] - count, count), j // strips, :, pl.ds(j % strips * LANES, LANES)],
            held_ref.at[j],
            sems.at[j],
        )
        for j in range(CYL * strips)
    ]
    for copy in copies:
        copy.start()
    for owner in range(table_ref.shape[0]):
        rank_ref[owner] = 0
    table_ref[...] = jnp.zeros_like(table_ref)
    row = lax.broadcasted_iota(jnp.int32, (SET_BEAMS, LANES), 0)
    lane = lax.broadcasted_iota(jnp.int32, (SET_BEAMS, LANES), 1)

    def step(index, carry):
        owner = owner_ref[index]
        rank = rank_ref[owner]
        rank_ref[owner] = rank + 1
        column = rank * SET_BEAMS
        tile = column // LANES * LANES
        hit = lane - row == column - tile
        rows = pl.ds(pl.multiple_of(index * SET_BEAMS, SET_BEAMS), SET_BEAMS)
        lanes = pl.ds(pl.multiple_of(tile, LANES), LANES)
        table_ref[lax.axis_index("freq") ^ owner, rows, lanes] = jnp.where(hit, 1.0, 0.0).astype(jnp.bfloat16)
        return carry

    lax.fori_loop(0, owner_ref.shape[0], step, 0, unroll=4)
    for j, copy in enumerate(copies):
        copy.wait()
        near_ref[:, j * LANES : (j + 1) * LANES] = held_ref[j].reshape(2 * count, LANES)


def put(out_ref, sems, blocks):
    copies = []
    for index, (block, frame, k) in enumerate(blocks):
        rows = pl.ds(pl.multiple_of((lax.axis_index("freq") ^ k) * UPCH, UPCH), UPCH)
        at = out_ref.at[pl.ds(frame, block.shape[0]), rows]
        copies.append(pltpu.make_async_copy(block, at, sems.at[index]))
    for copy in copies:
        copy.start()
    for copy in copies:
        copy.wait()


def early_gather_kernel(n_owner, own_ref, *refs):
    near, late, out_ref, sems = refs[: n_owner - 1], refs[n_owner - 1 : -2], refs[-2], refs[-1]
    own = [(own_ref, 0, 0)]

    @pl.when(lax.axis_index("pol") == 0)
    def _():
        put(out_ref, sems, own + [(block, BLOCK, k + 1) for k, block in enumerate(near)])

    @pl.when(lax.axis_index("pol") == 1)
    def _():
        put(out_ref, sems, own + [(block, 0, k + 1) for k, block in enumerate(late)])


def last_gather_kernel(n_owner, *refs):
    far, out_ref, sems = refs[: n_owner - 1], refs[-2], refs[-1]

    @pl.when(lax.axis_index("pol") == 0)
    def _():
        put(out_ref, sems, [(block, 0, k + 1) for k, block in enumerate(far)])


VMEM = pl.BlockSpec(memory_space=pltpu.VMEM)
SMEM = pl.BlockSpec(memory_space=pltpu.SMEM)
ANY = pl.BlockSpec(memory_space=pl.ANY)


def call(body, out_shape, n_in, flops, nbytes, scalars=0, whole=0, after=0, scratch=()):
    many = isinstance(out_shape, (list, tuple))

    def kernel(*refs):
        seen = scalars + n_in + whole
        body(*refs[:seen], *refs[seen + after :])

    return pl.pallas_call(
        kernel,
        out_shape=out_shape,
        in_specs=[SMEM] * scalars + [VMEM] * n_in + [ANY] * (whole + after),
        out_specs=[VMEM] * len(out_shape) if many else VMEM,
        scratch_shapes=list(scratch),
        cost_estimate=pl.CostEstimate(flops=flops, bytes_accessed=nbytes, transcendentals=0),
        compiler_params=pltpu.CompilerParams(vmem_limit_bytes=24 << 20),
    )


def per_device(voltages, feed_gains, owner_table, keep_flags):
    samples = voltages[0, 0]
    gain = feed_gains[0, 0]
    frame_count = samples.shape[0] // UPCH
    kept = frame_count // 2
    n_owner = lax.axis_size("freq")
    assert voltages.shape[1] == 1 and kept == 2 * BLOCK and kept >= TAPS
    assert n_owner & (n_owner - 1) == 0
    n_tm = lax.axis_size("tm")
    most_sets = 2 * owner_table.shape[0] // n_owner
    beams = keep_flags.shape[0]
    width = most_sets * SET_BEAMS
    bf16 = jnp.bfloat16
    filt = jnp.asarray(filter_matrix())
    edge = jnp.asarray(filter_matrix()[:, ROWS : BLOCK * ROWS])
    beam_table = jnp.asarray(beam_matrix())

    pairs = [(i, i + 1) for i in range(n_tm - 1)]

    def ahead(part, source):
        return lax.ppermute(part, ("tm", "pol"), [(i * 2 + source, j * 2 + 1) for i, j in pairs])

    def swap(part):
        return lax.ppermute(part, "pol", [(0, 1), (1, 0)])

    def spread(blocks, source):
        got = []
        for k in range(1, n_owner):
            route = [(i * 2 + source, (i ^ k) * 2 + 1 - source) for i in range(n_owner)]
            got.append(lax.ppermute(blocks[k], ("freq", "pol"), route))
        return got

    def form(body, frames, *arrays, more=()):
        shape = [jax.ShapeDtypeStruct((frames * UPCH, beams), bf16), jax.ShapeDtypeStruct((frames, UPCH, width), bf16)]
        scratch = [pltpu.VMEM((CYL * BLOCK * UPCH, 2 * NS), bf16)]
        return call(
            body, shape + list(more), len(arrays), 4 * 512 * 1024 * 1024, 4 << 20, scratch=scratch
        )(*arrays)

    def rest(body, frames, *arrays, more=(), count=n_owner - 1):
        shape = [jax.ShapeDtypeStruct((frames, UPCH, width), bf16)] * count
        return call(body, list(more) + shape, len(arrays), 1 << 29, 4 << 20)(*arrays)

    keep = keep_flags.reshape(1, -1)
    reach, edge_rows = BLOCK * ROWS, (TAPS - 1 - BLOCK) * ROWS
    blocks = kept // BLOCK
    strips = CYL * NS // LANES
    table, near_rows = pl.pallas_call(
        head_kernel,
        out_shape=[jax.ShapeDtypeStruct((n_owner, beams, width), bf16), jax.ShapeDtypeStruct((reach, CYL * NS), bf16)],
        in_specs=[SMEM, pl.BlockSpec(memory_space=pltpu.HBM)],
        out_specs=[VMEM, VMEM],
        scratch_shapes=[
            pltpu.VMEM((strips, BLOCK * UPCH, 2, LANES), bf16),
            pltpu.SMEM((n_owner,), jnp.int32),
            pltpu.SemaphoreType.DMA((strips,)),
        ],
        cost_estimate=pl.CostEstimate(flops=1 << 20, bytes_accessed=4 << 20, transcendentals=0),
        compiler_params=pltpu.CompilerParams(vmem_limit_bytes=24 << 20),
    )(owner_table, pltpu.with_memory_space_constraint(samples, pltpu.HBM))
    near0 = ahead(near_rows, 0)
    near1 = ahead(near_rows, 1)
    samples, table = lax.optimization_barrier((samples, table))
    x = samples.transpose(0, 2, 1, 3).reshape(samples.shape[0] * 2, CYL * NS)
    x = lax.optimization_barrier(x)
    far_rows = call(
        functools.partial(far_rows_kernel, reach), jax.ShapeDtypeStruct((edge_rows, CYL * NS), bf16), 1, 0, 1 << 20
    )(x)
    other = swap(x)
    gain_other = swap(gain)
    far0 = ahead(far_rows, 0)
    far1 = ahead(far_rows, 1)
    late_own = call(
        functools.partial(late_own_kernel, blocks),
        jax.ShapeDtypeStruct((kept * UPCH, beams), bf16),
        4,
        4 * 512 * 1024 * 1024,
        4 << 20,
        scratch=[pltpu.VMEM((CYL * BLOCK * UPCH, 2 * NS), bf16)],
    )(filt, x, gain, beam_table)
    late_sum, late_last = form(
        functools.partial(late_kernel, blocks), kept, filt, other, gain_other, beam_table, keep, table, late_own
    )
    late = [*rest(functools.partial(place_kernel, 0), kept, late_sum, table), late_last]
    late_got = spread(late, 0)
    common = (gain, gain_other, beam_table, keep, table)
    near_sum, near_last = form(near_kernel, BLOCK, filt, near1, near0, x, other, *common)
    near = [*rest(functools.partial(place_kernel, 1), BLOCK, near_sum, table), near_last]
    near_got = spread(near, 1)
    pre = call(
        ahead_kernel,
        jax.ShapeDtypeStruct((2 * CYL, reach, NS), jnp.float32),
        5,
        2 * 512 * 1024 * 1024,
        4 << 20,
        after=1,
    )(filt, near1, near0, x, other, near[0])
    block_shape = jax.ShapeDtypeStruct((BLOCK, UPCH, width), bf16)
    far_sum, far_last, far_next = form(far_kernel, BLOCK, edge, far1, far0, *common, pre, more=[block_shape])
    own, *far = rest(
        far_place_kernel,
        BLOCK,
        far_sum,
        table,
        near[0],
        late[0],
        more=[jax.ShapeDtypeStruct((kept, UPCH, width), bf16)],
        count=n_owner - 3,
    )
    far = [own, *far, far_next, far_last]
    far_got = spread(far, 1)
    own_got = swap(own)
    out_shape = jax.ShapeDtypeStruct((kept, n_owner * UPCH, width), bf16)

    def gather(body, arrays, base=()):
        return pl.pallas_call(
            functools.partial(body, n_owner),
            out_shape=out_shape,
            in_specs=[VMEM] * len(arrays) + [ANY] * len(base),
            out_specs=ANY,
            scratch_shapes=[pltpu.SemaphoreType.DMA((n_owner,))],
            input_output_aliases={len(arrays): 0} if base else {},
            cost_estimate=pl.CostEstimate(flops=0, bytes_accessed=2 << 20, transcendentals=0),
            compiler_params=pltpu.CompilerParams(vmem_limit_bytes=24 << 20),
        )(*arrays, *base)

    out = gather(early_gather_kernel, [own_got, *near_got, *late_got])
    return gather(last_gather_kernel, far_got, base=[out])


def solution(mesh):
    return jax.shard_map(
        per_device,
        mesh=mesh,
        in_specs=(
            P("pol", ("grp", "freq"), "tm", None, None, None),
            P(("grp", "freq"), "pol", None, None, None),
            P(),
            P(),
        ),
        out_specs=P(("grp", "tm", "pol"), None, "freq"),
        check_vma=False,
    )
```

```python
import functools

import jax
import jax.numpy as jnp
import numpy as np
from jax import lax
from jax.experimental import pallas as pl
from jax.experimental.pallas import tpu as pltpu
from jax.sharding import PartitionSpec as P


NS = 256
CYL = 4
UPCH = 16
TAPS = 16
SET_BEAMS = 16
BLOCK = 8
LANES = 128
ROWS = 2 * UPCH


def window_taps():
    span = TAPS * UPCH
    steps = np.arange(span, dtype=np.float64)
    weights = np.sinc((steps - (span - 1) / 2.0) / UPCH) * np.sin(np.pi * (steps + 0.5) / span) ** 2
    return weights / np.sqrt(np.sum(weights * weights))


def filter_matrix():
    weights = window_taps()
    fine = np.arange(UPCH)
    sample = np.arange(TAPS * UPCH)
    phase = 2.0 * np.pi * ((fine[:, None] * sample[None, :]) % UPCH) / UPCH
    cosine = np.cos(phase) * weights
    sine = np.sin(phase) * weights
    table = np.zeros((2, BLOCK, UPCH, TAPS + BLOCK, UPCH, 2))
    for frame in range(BLOCK):
        taps = slice(frame + 1, frame + 1 + TAPS)
        cos_part = cosine.reshape(UPCH, TAPS, UPCH)
        sin_part = sine.reshape(UPCH, TAPS, UPCH)
        table[0, frame, :, taps, :, 0] = cos_part
        table[0, frame, :, taps, :, 1] = sin_part
        table[1, frame, :, taps, :, 0] = -sin_part
        table[1, frame, :, taps, :, 1] = cos_part
    return table.reshape(2 * BLOCK * UPCH, (TAPS + BLOCK) * ROWS).astype(np.float32).astype(jnp.bfloat16)


def beam_matrix():
    rows = np.arange(NS)
    angle = 2.0 * np.pi * (rows[:, None] * rows[None, :] % NS) / NS
    scale = 1.0 / np.sqrt(NS)
    cosine = (np.cos(angle) * scale).astype(np.float32)
    sine = (np.sin(angle) * scale).astype(np.float32)
    upper = np.concatenate([cosine, -sine], axis=1)
    lower = np.concatenate([sine, cosine], axis=1)
    table = np.concatenate([upper, lower], axis=0).astype(jnp.bfloat16)
    table = table.reshape(2 * NS, 2, NS // LANES, LANES).transpose(0, 2, 1, 3).reshape(2 * NS, 2 * NS)
    return (table.astype(np.float32) * 0.5).astype(jnp.bfloat16)


def columns(cyl):
    return slice(cyl * NS, (cyl + 1) * NS)


def form_powers(spectra, gain_ref, beam_ref, cal_ref, emit):
    half = BLOCK * UPCH
    for cyl in range(CYL):
        spec = spectra(cyl)
        real, imag = spec[:half], spec[half:]
        gain_real = gain_ref[cyl, 0:1, :]
        gain_imag = gain_ref[cyl, 1:2, :]
        rows = slice(cyl * half, (cyl + 1) * half)
        cal_ref[rows, :NS] = (real * gain_real - imag * gain_imag).astype(jnp.bfloat16)
        cal_ref[rows, NS:] = (real * gain_imag + imag * gain_real).astype(jnp.bfloat16)
    for strip in range(NS // LANES):
        beam = jnp.dot(
            cal_ref[...],
            beam_ref[:, strip * 2 * LANES : (strip + 1) * 2 * LANES],
            preferred_element_type=jnp.float32,
        )
        beams = [beam[cyl * half : (cyl + 1) * half] for cyl in range(CYL)]
        (r0, i0), (r1, i1), (r2, i2), (r3, i3) = [(b[:, :LANES], b[:, LANES:]) for b in beams]
        pr, pi, mr, mi = r0 + r2, i0 + i2, r0 - r2, i0 - i2
        sr, si, dr, di = r1 + r3, i1 + i3, r1 - r3, i1 - i3
        formed = [(pr + sr, pi + si), (mr + di, mi - dr), (pr - sr, pi - si), (mr - di, mi + dr)]
        for element, (fr, fi) in enumerate(formed):
            emit(element * NS + strip * LANES, fr * fr + fi * fi)


def filtered(terms):
    total = None
    for table, rows in terms:
        term = jnp.dot(table, rows, preferred_element_type=jnp.float32)
        total = term if total is None else total + term
    return total


def keeper(power_ref, at=0):
    rows = pl.ds(at, BLOCK * UPCH)

    def emit(column, power):
        power_ref[rows, column : column + LANES] = power.astype(jnp.bfloat16)

    return emit


def adder(power_ref, keep_ref, sum_ref, at=0):
    rows = pl.ds(at, BLOCK * UPCH)

    def emit(column, power):
        lanes = slice(column, column + LANES)
        total = power_ref[rows, lanes].astype(jnp.float32) + power.astype(jnp.bfloat16).astype(jnp.float32)
        sum_ref[rows, lanes] = (total * keep_ref[:, lanes].astype(jnp.float32)).astype(jnp.bfloat16)

    return emit


def place(sum_ref, table, out_ref):
    placed = jnp.dot(sum_ref[...], table, preferred_element_type=jnp.float32)
    out_ref[...] = placed.astype(jnp.bfloat16).reshape(out_ref.shape)


def place_kernel(pol, sum_ref, table_ref, *out_refs):
    @pl.when(lax.axis_index("pol") == pol)
    def _():
        for k, out_ref in enumerate(out_refs):
            place(sum_ref, table_ref[k], out_ref)


def far_rows_kernel(reach, x_ref, other_ref, out_ref):
    count = out_ref.shape[0] // 2
    at = x_ref.shape[0] - reach - count

    @pl.when(lax.axis_index("pol") == 1)
    def _():
        out_ref[:count, :] = x_ref[at : at + count, :]
        out_ref[count:, :] = other_ref[at : at + count, :]


def each_late_block(blocks, filt_ref, x_ref, gain_ref, beam_ref, cal_ref, emitter):
    def step(block, carry):
        first = pl.multiple_of(block * BLOCK * ROWS, BLOCK * ROWS)
        rows = pl.ds(first, (TAPS + BLOCK) * ROWS)

        def spectra(cyl):
            return filtered([(filt_ref[...], x_ref[rows, columns(cyl)])])

        at = pl.multiple_of(block * BLOCK * UPCH, BLOCK * UPCH)
        form_powers(spectra, gain_ref, beam_ref, cal_ref, emitter(at))
        return carry

    lax.fori_loop(0, blocks, step, 0)


def late_own_kernel(blocks, filt_ref, x_ref, gain_ref, beam_ref, out_ref, cal_ref):
    @pl.when(lax.axis_index("pol") == 0)
    def _():
        each_late_block(blocks, filt_ref, x_ref, gain_ref, beam_ref, cal_ref, lambda at: keeper(out_ref, at))


def late_kernel(
    blocks, filt_ref, x_ref, gain_ref, beam_ref, keep_ref, table_ref, power_ref, sum_ref, out_ref, cal_ref
):
    @pl.when(lax.axis_index("pol") == 0)
    def _():
        def emitter(at):
            return adder(power_ref, keep_ref, sum_ref, at)

        each_late_block(blocks, filt_ref, x_ref, gain_ref, beam_ref, cal_ref, emitter)
        place(sum_ref, table_ref[table_ref.shape[0] - 1], out_ref)


def near_kernel(
    filt_ref, n0, n1, x0, x1, g0, g1, beam_ref, keep_ref, table_ref, sum_ref, out_ref, cal_ref
):
    reach = BLOCK * ROWS

    @pl.when(lax.axis_index("pol") == 1)
    def _():
        for pol, (n, x, gain) in enumerate(((n0, x0, g0), (n1, x1, g1))):

            def spectra(cyl, n=n, x=x):
                there, here = n[:, columns(cyl)], x[: 2 * reach, columns(cyl)]
                return filtered([(filt_ref[:, :reach], there), (filt_ref[:, reach:], here)])

            emit = adder(sum_ref, keep_ref, sum_ref) if pol else keeper(sum_ref)
            form_powers(spectra, gain, beam_ref, cal_ref, emit)
        place(sum_ref, table_ref[table_ref.shape[0] - 1], out_ref)


def ahead_kernel(filt_ref, n0, n1, x0, x1, pre_ref):
    reach = BLOCK * ROWS

    @pl.when(lax.axis_index("pol") == 1)
    def _():
        for pol, (n, x) in enumerate(((n0, x0), (n1, x1))):
            for cyl in range(CYL):
                there, here = n[:, columns(cyl)], x[:reach, columns(cyl)]
                terms = [(filt_ref[:, reach : 2 * reach], there), (filt_ref[:, 2 * reach :], here)]
                pre_ref[pol * CYL + cyl] = filtered(terms)


def far_kernel(
    edge_ref, far_ref, g0, g1, beam_ref, keep_ref, table_ref, pre_ref, sum_ref, out_ref, next_ref, cal_ref
):
    @pl.when(lax.axis_index("pol") == 1)
    def _():
        count = far_ref.shape[0] // 2
        for pol, gain in enumerate((g0, g1)):

            def spectra(cyl, pol=pol):
                rows = far_ref[pol * count : (pol + 1) * count, columns(cyl)]
                return pre_ref[pol * CYL + cyl] + filtered([(edge_ref[...], rows)])

            emit = adder(sum_ref, keep_ref, sum_ref) if pol else keeper(sum_ref)
            form_powers(spectra, gain, beam_ref, cal_ref, emit)
        place(sum_ref, table_ref[table_ref.shape[0] - 1], out_ref)
        place(sum_ref, table_ref[table_ref.shape[0] - 2], next_ref)


def far_place_kernel(sum_ref, table_ref, near_ref, late_ref, own_ref, *out_refs):
    @pl.when(lax.axis_index("pol") == 1)
    def _():
        for k, out_ref in enumerate(out_refs, 1):
            place(sum_ref, table_ref[k], out_ref)
        place(sum_ref, table_ref[0], own_ref.at[:BLOCK])
        own_ref[BLOCK:] = near_ref[...]

    @pl.when(lax.axis_index("pol") == 0)
    def _():
        own_ref[...] = late_ref[...]


def head_kernel(sets_ref, v_ref, table_ref, near_ref, held_ref, owner_ref, rank_ref, sems, sem):
    count = held_ref.shape[1]
    strips = NS // LANES
    copies = [
        pltpu.make_async_copy(
            v_ref.at[pl.ds(v_ref.shape[0] - count, count), j // strips, :, pl.ds(j % strips * LANES, LANES)],
            held_ref.at[j],
            sems.at[j],
        )
        for j in range(CYL * strips)
    ]
    sets_copy = pltpu.make_async_copy(sets_ref, owner_ref, sem)
    sets_copy.start()
    for copy in copies:
        copy.start()
    for owner in range(table_ref.shape[0]):
        rank_ref[owner] = 0
    table_ref[...] = jnp.zeros_like(table_ref)
    sets_copy.wait()
    row = lax.broadcasted_iota(jnp.int32, (SET_BEAMS, LANES), 0)
    lane = lax.broadcasted_iota(jnp.int32, (SET_BEAMS, LANES), 1)

    def step(index, carry):
        owner = owner_ref[index]
        rank = rank_ref[owner]
        rank_ref[owner] = rank + 1
        column = rank * SET_BEAMS
        tile = column // LANES * LANES
        hit = lane - row == column - tile
        rows = pl.ds(pl.multiple_of(index * SET_BEAMS, SET_BEAMS), SET_BEAMS)
        lanes = pl.ds(pl.multiple_of(tile, LANES), LANES)
        table_ref[lax.axis_index("freq") ^ owner, rows, lanes] = jnp.where(hit, 1.0, 0.0).astype(jnp.bfloat16)
        return carry

    lax.fori_loop(0, owner_ref.shape[0], step, 0, unroll=4)
    for j, copy in enumerate(copies):
        copy.wait()
        near_ref[:, j * LANES : (j + 1) * LANES] = held_ref[j].reshape(2 * count, LANES)


def put(out_ref, sems, blocks):
    copies = []
    for index, (block, frame, k) in enumerate(blocks):
        rows = pl.ds(pl.multiple_of((lax.axis_index("freq") ^ k) * UPCH, UPCH), UPCH)
        at = out_ref.at[pl.ds(frame, block.shape[0]), rows]
        copies.append(pltpu.make_async_copy(block, at, sems.at[index]))
    for copy in copies:
        copy.start()
    for copy in copies:
        copy.wait()


def early_gather_kernel(n_owner, own_ref, *refs):
    near, late, out_ref, sems = refs[: n_owner - 1], refs[n_owner - 1 : -2], refs[-2], refs[-1]
    own = [(own_ref, 0, 0)]

    @pl.when(lax.axis_index("pol") == 0)
    def _():
        put(out_ref, sems, own + [(block, BLOCK, k + 1) for k, block in enumerate(near)])

    @pl.when(lax.axis_index("pol") == 1)
    def _():
        put(out_ref, sems, own + [(block, 0, k + 1) for k, block in enumerate(late)])


def last_gather_kernel(n_owner, *refs):
    far, out_ref, sems = refs[: n_owner - 1], refs[-2], refs[-1]

    @pl.when(lax.axis_index("pol") == 0)
    def _():
        put(out_ref, sems, [(block, 0, k + 1) for k, block in enumerate(far)])


VMEM = pl.BlockSpec(memory_space=pltpu.VMEM)
SMEM = pl.BlockSpec(memory_space=pltpu.SMEM)
ANY = pl.BlockSpec(memory_space=pl.ANY)


def call(body, out_shape, n_in, flops, nbytes, scalars=0, whole=0, after=0, scratch=()):
    many = isinstance(out_shape, (list, tuple))

    def kernel(*refs):
        seen = scalars + n_in + whole
        body(*refs[:seen], *refs[seen + after :])

    return pl.pallas_call(
        kernel,
        out_shape=out_shape,
        in_specs=[SMEM] * scalars + [VMEM] * n_in + [ANY] * (whole + after),
        out_specs=[VMEM] * len(out_shape) if many else VMEM,
        scratch_shapes=list(scratch),
        cost_estimate=pl.CostEstimate(flops=flops, bytes_accessed=nbytes, transcendentals=0),
        compiler_params=pltpu.CompilerParams(vmem_limit_bytes=24 << 20),
    )


def per_device(voltages, feed_gains, owner_table, keep_flags):
    samples = voltages[0, 0]
    gain = feed_gains[0, 0]
    frame_count = samples.shape[0] // UPCH
    kept = frame_count // 2
    n_owner = lax.axis_size("freq")
    assert voltages.shape[1] == 1 and kept == 2 * BLOCK and kept >= TAPS
    assert n_owner & (n_owner - 1) == 0
    n_tm = lax.axis_size("tm")
    most_sets = 2 * owner_table.shape[0] // n_owner
    beams = keep_flags.shape[0]
    width = most_sets * SET_BEAMS
    bf16 = jnp.bfloat16
    filt = jnp.asarray(filter_matrix())
    edge = jnp.asarray(filter_matrix()[:, ROWS : BLOCK * ROWS])
    beam_table = jnp.asarray(beam_matrix())

    pairs = [(i, i + 1) for i in range(n_tm - 1)]

    def ahead(part, source):
        return lax.ppermute(part, ("tm", "pol"), [(i * 2 + source, j * 2 + 1) for i, j in pairs])

    def swap(part):
        return lax.ppermute(part, "pol", [(0, 1), (1, 0)])

    def spread(blocks, source):
        got = []
        for k in range(1, n_owner):
            route = [(i * 2 + source, (i ^ k) * 2 + 1 - source) for i in range(n_owner)]
            got.append(lax.ppermute(blocks[k], ("freq", "pol"), route))
        return got

    def form(body, frames, *arrays, more=()):
        shape = [jax.ShapeDtypeStruct((frames * UPCH, beams), bf16), jax.ShapeDtypeStruct((frames, UPCH, width), bf16)]
        scratch = [pltpu.VMEM((CYL * BLOCK * UPCH, 2 * NS), bf16)]
        return call(
            body, shape + list(more), len(arrays), 4 * 512 * 1024 * 1024, 4 << 20, scratch=scratch
        )(*arrays)

    def rest(body, frames, *arrays, more=(), count=n_owner - 1):
        shape = [jax.ShapeDtypeStruct((frames, UPCH, width), bf16)] * count
        return call(body, list(more) + shape, len(arrays), 1 << 29, 4 << 20)(*arrays)

    keep = keep_flags.reshape(1, -1)
    reach, edge_rows = BLOCK * ROWS, (TAPS - 1 - BLOCK) * ROWS
    blocks = kept // BLOCK
    strips = CYL * NS // LANES
    table, near_rows = pl.pallas_call(
        head_kernel,
        out_shape=[jax.ShapeDtypeStruct((n_owner, beams, width), bf16), jax.ShapeDtypeStruct((reach, CYL * NS), bf16)],
        in_specs=[pl.BlockSpec(memory_space=pltpu.HBM)] * 2,
        out_specs=[VMEM, VMEM],
        scratch_shapes=[
            pltpu.VMEM((strips, BLOCK * UPCH, 2, LANES), bf16),
            pltpu.SMEM(owner_table.shape, jnp.int32),
            pltpu.SMEM((n_owner,), jnp.int32),
            pltpu.SemaphoreType.DMA((strips,)),
            pltpu.SemaphoreType.DMA(()),
        ],
        cost_estimate=pl.CostEstimate(flops=1 << 20, bytes_accessed=4 << 20, transcendentals=0),
        compiler_params=pltpu.CompilerParams(vmem_limit_bytes=24 << 20),
    )(*(pltpu.with_memory_space_constraint(array, pltpu.HBM) for array in (owner_table, samples)))
    near0 = ahead(near_rows, 0)
    near1 = ahead(near_rows, 1)
    samples, table = lax.optimization_barrier((samples, table))
    x = samples.transpose(0, 2, 1, 3).reshape(samples.shape[0] * 2, CYL * NS)
    x = lax.optimization_barrier(x)
    other = swap(x)
    gain_other = swap(gain)
    shape = jax.ShapeDtypeStruct((2 * edge_rows, CYL * NS), bf16)
    far_rows = call(functools.partial(far_rows_kernel, reach), shape, 2, 0, 2 << 20)(x, other)
    far_halo = ahead(far_rows, 1)
    late_own = call(
        functools.partial(late_own_kernel, blocks),
        jax.ShapeDtypeStruct((kept * UPCH, beams), bf16),
        4,
        4 * 512 * 1024 * 1024,
        4 << 20,
        scratch=[pltpu.VMEM((CYL * BLOCK * UPCH, 2 * NS), bf16)],
    )(filt, x, gain, beam_table)
    late_sum, late_last = form(
        functools.partial(late_kernel, blocks), kept, filt, other, gain_other, beam_table, keep, table, late_own
    )
    late = [*rest(functools.partial(place_kernel, 0), kept, late_sum, table), late_last]
    late_got = spread(late, 0)
    common = (gain, gain_other, beam_table, keep, table)
    near_sum, near_last = form(near_kernel, BLOCK, filt, near1, near0, x, other, *common)
    near = [*rest(functools.partial(place_kernel, 1), BLOCK, near_sum, table), near_last]
    near_got = spread(near, 1)
    pre = call(
        ahead_kernel,
        jax.ShapeDtypeStruct((2 * CYL, reach, NS), jnp.float32),
        5,
        2 * 512 * 1024 * 1024,
        4 << 20,
        after=1,
    )(filt, near1, near0, x, other, near[0])
    block_shape = jax.ShapeDtypeStruct((BLOCK, UPCH, width), bf16)
    far_sum, far_last, far_next = form(far_kernel, BLOCK, edge, far_halo, *common, pre, more=[block_shape])
    own, *far = rest(
        far_place_kernel,
        BLOCK,
        far_sum,
        table,
        near[0],
        late[0],
        more=[jax.ShapeDtypeStruct((kept, UPCH, width), bf16)],
        count=n_owner - 3,
    )
    far = [own, *far, far_next, far_last]
    far_got = spread(far, 1)
    own_got = swap(own)
    out_shape = jax.ShapeDtypeStruct((kept, n_owner * UPCH, width), bf16)

    def gather(body, arrays, base=()):
        return pl.pallas_call(
            functools.partial(body, n_owner),
            out_shape=out_shape,
            in_specs=[VMEM] * len(arrays) + [ANY] * len(base),
            out_specs=ANY,
            scratch_shapes=[pltpu.SemaphoreType.DMA((n_owner,))],
            input_output_aliases={len(arrays): 0} if base else {},
            cost_estimate=pl.CostEstimate(flops=0, bytes_accessed=2 << 20, transcendentals=0),
            compiler_params=pltpu.CompilerParams(vmem_limit_bytes=24 << 20),
        )(*arrays, *base)

    out = gather(early_gather_kernel, [own_got, *near_got, *late_got])
    return gather(last_gather_kernel, far_got, base=[out])


def solution(mesh):
    return jax.shard_map(
        per_device,
        mesh=mesh,
        in_specs=(
            P("pol", ("grp", "freq"), "tm", None, None, None),
            P(("grp", "freq"), "pol", None, None, None),
            P(),
            P(),
        ),
        out_specs=P(("grp", "tm", "pol"), None, "freq"),
        check_vma=False,
    )
```

```python
import functools

import jax
import jax.numpy as jnp
import numpy as np
from jax import lax
from jax.experimental import pallas as pl
from jax.experimental.pallas import tpu as pltpu
from jax.sharding import PartitionSpec as P


NS = 256
CYL = 4
UPCH = 16
TAPS = 16
SET_BEAMS = 16
BLOCK = 8
LANES = 128
ROWS = 2 * UPCH


def window_taps():
    span = TAPS * UPCH
    steps = np.arange(span, dtype=np.float64)
    weights = np.sinc((steps - (span - 1) / 2.0) / UPCH) * np.sin(np.pi * (steps + 0.5) / span) ** 2
    return weights / np.sqrt(np.sum(weights * weights))


def filter_matrix():
    weights = window_taps()
    fine = np.arange(UPCH)
    sample = np.arange(TAPS * UPCH)
    phase = 2.0 * np.pi * ((fine[:, None] * sample[None, :]) % UPCH) / UPCH
    cosine = np.cos(phase) * weights
    sine = np.sin(phase) * weights
    table = np.zeros((2, BLOCK, UPCH, TAPS + BLOCK, UPCH, 2))
    for frame in range(BLOCK):
        taps = slice(frame + 1, frame + 1 + TAPS)
        cos_part = cosine.reshape(UPCH, TAPS, UPCH)
        sin_part = sine.reshape(UPCH, TAPS, UPCH)
        table[0, frame, :, taps, :, 0] = cos_part
        table[0, frame, :, taps, :, 1] = sin_part
        table[1, frame, :, taps, :, 0] = -sin_part
        table[1, frame, :, taps, :, 1] = cos_part
    return table.reshape(2 * BLOCK * UPCH, (TAPS + BLOCK) * ROWS).astype(np.float32).astype(jnp.bfloat16)


def beam_matrix():
    rows = np.arange(NS)
    angle = 2.0 * np.pi * (rows[:, None] * rows[None, :] % NS) / NS
    scale = 1.0 / np.sqrt(NS)
    cosine = (np.cos(angle) * scale).astype(np.float32)
    sine = (np.sin(angle) * scale).astype(np.float32)
    upper = np.concatenate([cosine, -sine], axis=1)
    lower = np.concatenate([sine, cosine], axis=1)
    table = np.concatenate([upper, lower], axis=0).astype(jnp.bfloat16)
    table = table.reshape(2 * NS, 2, NS // LANES, LANES).transpose(0, 2, 1, 3).reshape(2 * NS, 2 * NS)
    return (table.astype(np.float32) * 0.5).astype(jnp.bfloat16)


def columns(cyl):
    return slice(cyl * NS, (cyl + 1) * NS)


def form_powers(spectra, gain_ref, beam_ref, cal_ref, emit):
    half = BLOCK * UPCH
    for cyl in range(CYL):
        spec = spectra(cyl)
        real, imag = spec[:half], spec[half:]
        gain_real = gain_ref[cyl, 0:1, :]
        gain_imag = gain_ref[cyl, 1:2, :]
        rows = slice(cyl * half, (cyl + 1) * half)
        cal_ref[rows, :NS] = (real * gain_real - imag * gain_imag).astype(jnp.bfloat16)
        cal_ref[rows, NS:] = (real * gain_imag + imag * gain_real).astype(jnp.bfloat16)
    for strip in range(NS // LANES):
        beam = jnp.dot(
            cal_ref[...],
            beam_ref[:, strip * 2 * LANES : (strip + 1) * 2 * LANES],
            preferred_element_type=jnp.float32,
        )
        beams = [beam[cyl * half : (cyl + 1) * half] for cyl in range(CYL)]
        (r0, i0), (r1, i1), (r2, i2), (r3, i3) = [(b[:, :LANES], b[:, LANES:]) for b in beams]
        pr, pi, mr, mi = r0 + r2, i0 + i2, r0 - r2, i0 - i2
        sr, si, dr, di = r1 + r3, i1 + i3, r1 - r3, i1 - i3
        formed = [(pr + sr, pi + si), (mr + di, mi - dr), (pr - sr, pi - si), (mr - di, mi + dr)]
        for element, (fr, fi) in enumerate(formed):
            emit(element * NS + strip * LANES, fr * fr + fi * fi)


def filtered(terms):
    total = None
    for table, rows in terms:
        term = jnp.dot(table, rows, preferred_element_type=jnp.float32)
        total = term if total is None else total + term
    return total


def keeper(power_ref, at=0):
    rows = pl.ds(at, BLOCK * UPCH)

    def emit(column, power):
        power_ref[rows, column : column + LANES] = power.astype(jnp.bfloat16)

    return emit


def adder(power_ref, keep_ref, sum_ref, at=0):
    rows = pl.ds(at, BLOCK * UPCH)

    def emit(column, power):
        lanes = slice(column, column + LANES)
        total = power_ref[rows, lanes].astype(jnp.float32) + power.astype(jnp.bfloat16).astype(jnp.float32)
        sum_ref[rows, lanes] = (total * keep_ref[:, lanes].astype(jnp.float32)).astype(jnp.bfloat16)

    return emit


def place(sum_ref, table, out_ref):
    placed = jnp.dot(sum_ref[...], table, preferred_element_type=jnp.float32)
    out_ref[...] = placed.astype(jnp.bfloat16).reshape(out_ref.shape)


def place_kernel(pol, sum_ref, table_ref, *out_refs):
    @pl.when(lax.axis_index("pol") == pol)
    def _():
        for k, out_ref in enumerate(out_refs):
            place(sum_ref, table_ref[k], out_ref)


def first_rows_kernel(x_ref, out_ref):
    out_ref[...] = x_ref[: out_ref.shape[0], :]


def far_rows_kernel(x_ref, other_ref, out_ref):
    count = out_ref.shape[0] // 2
    at = x_ref.shape[0] - count

    @pl.when(lax.axis_index("pol") == 1)
    def _():
        out_ref[:count, :] = x_ref[at:, :]
        out_ref[count:, :] = other_ref[at:, :]


def late_spectra(block, filt_ref, x_ref, near_ref):
    first = block * BLOCK * ROWS
    depth = (TAPS + BLOCK) * ROWS
    here = min(depth, x_ref.shape[0] - first)

    def spectra(cyl):
        terms = [(filt_ref[:, :here], x_ref[first : first + here, columns(cyl)])]
        if here < depth:
            terms.append((filt_ref[:, here:], near_ref[: depth - here, columns(cyl)]))
        return filtered(terms)

    return spectra


def late_own_kernel(filt_ref, x_ref, near_ref, gain_ref, beam_ref, out_ref, cal_ref):
    @pl.when(lax.axis_index("pol") == 0)
    def _():
        for block in range(out_ref.shape[0] // (BLOCK * UPCH)):
            spectra = late_spectra(block, filt_ref, x_ref, near_ref)
            form_powers(spectra, gain_ref, beam_ref, cal_ref, keeper(out_ref, block * BLOCK * UPCH))


def late_first_kernel(filt_ref, x_ref, gain_ref, beam_ref, keep_ref, power_ref, sum_ref, cal_ref):
    @pl.when(lax.axis_index("pol") == 0)
    def _():
        spectra = late_spectra(0, filt_ref, x_ref, None)
        form_powers(spectra, gain_ref, beam_ref, cal_ref, adder(power_ref, keep_ref, sum_ref))


def late_kernel(
    filt_ref, x_ref, near_ref, gain_ref, beam_ref, keep_ref, table_ref, power_ref, first_ref, sum_ref, out_ref, cal_ref
):
    done = first_ref.shape[0]

    @pl.when(lax.axis_index("pol") == 0)
    def _():
        sum_ref[:done, :] = first_ref[...]
        for block in range(done // (BLOCK * UPCH), sum_ref.shape[0] // (BLOCK * UPCH)):
            spectra = late_spectra(block, filt_ref, x_ref, near_ref)
            emit = adder(power_ref, keep_ref, sum_ref, block * BLOCK * UPCH)
            form_powers(spectra, gain_ref, beam_ref, cal_ref, emit)
        place(sum_ref, table_ref[table_ref.shape[0] - 1], out_ref)


def near_kernel(
    filt_ref, n0, n1, x0, x1, g0, g1, beam_ref, keep_ref, table_ref, sum_ref, out_ref, cal_ref
):
    reach = BLOCK * ROWS

    @pl.when(lax.axis_index("pol") == 1)
    def _():
        for pol, (n, x, gain) in enumerate(((n0, x0, g0), (n1, x1, g1))):

            def spectra(cyl, n=n, x=x):
                there, here = n[:, columns(cyl)], x[: 2 * reach, columns(cyl)]
                return filtered([(filt_ref[:, :reach], there), (filt_ref[:, reach:], here)])

            emit = adder(sum_ref, keep_ref, sum_ref) if pol else keeper(sum_ref)
            form_powers(spectra, gain, beam_ref, cal_ref, emit)
        place(sum_ref, table_ref[table_ref.shape[0] - 1], out_ref)


def ahead_kernel(filt_ref, n0, n1, x0, x1, pre_ref):
    reach = BLOCK * ROWS

    @pl.when(lax.axis_index("pol") == 1)
    def _():
        for pol, (n, x) in enumerate(((n0, x0), (n1, x1))):
            for cyl in range(CYL):
                there, here = n[:, columns(cyl)], x[:reach, columns(cyl)]
                terms = [(filt_ref[:, reach : 2 * reach], there), (filt_ref[:, 2 * reach :], here)]
                pre_ref[pol * CYL + cyl] = filtered(terms)


def far_kernel(
    edge_ref, far_ref, g0, g1, beam_ref, keep_ref, table_ref, pre_ref, sum_ref, out_ref, next_ref, cal_ref
):
    @pl.when(lax.axis_index("pol") == 1)
    def _():
        count = far_ref.shape[0] // 2
        for pol, gain in enumerate((g0, g1)):

            def spectra(cyl, pol=pol):
                rows = far_ref[pol * count : (pol + 1) * count, columns(cyl)]
                return pre_ref[pol * CYL + cyl] + filtered([(edge_ref[...], rows)])

            emit = adder(sum_ref, keep_ref, sum_ref) if pol else keeper(sum_ref)
            form_powers(spectra, gain, beam_ref, cal_ref, emit)
        place(sum_ref, table_ref[table_ref.shape[0] - 1], out_ref)
        place(sum_ref, table_ref[table_ref.shape[0] - 2], next_ref)


def far_place_kernel(sum_ref, table_ref, near_ref, late_ref, own_ref, *out_refs):
    @pl.when(lax.axis_index("pol") == 1)
    def _():
        for k, out_ref in enumerate(out_refs, 1):
            place(sum_ref, table_ref[k], out_ref)
        place(sum_ref, table_ref[0], own_ref.at[:BLOCK])
        own_ref[BLOCK:] = near_ref[...]

    @pl.when(lax.axis_index("pol") == 0)
    def _():
        own_ref[...] = late_ref[...]


def head_kernel(sets_ref, v_ref, table_ref, near_ref, held_ref, owner_ref, rank_ref, sems, sem):
    count = held_ref.shape[1]
    strips = NS // LANES
    copies = [
        pltpu.make_async_copy(
            v_ref.at[pl.ds(v_ref.shape[0] - count, count), j // strips, :, pl.ds(j % strips * LANES, LANES)],
            held_ref.at[j],
            sems.at[j],
        )
        for j in range(CYL * strips)
    ]
    sets_copy = pltpu.make_async_copy(sets_ref, owner_ref, sem)
    sets_copy.start()
    for copy in copies:
        copy.start()
    for owner in range(table_ref.shape[0]):
        rank_ref[owner] = 0
    table_ref[...] = jnp.zeros_like(table_ref)
    sets_copy.wait()
    row = lax.broadcasted_iota(jnp.int32, (SET_BEAMS, LANES), 0)
    lane = lax.broadcasted_iota(jnp.int32, (SET_BEAMS, LANES), 1)

    def step(index, carry):
        owner = owner_ref[index]
        rank = rank_ref[owner]
        rank_ref[owner] = rank + 1
        column = rank * SET_BEAMS
        tile = column // LANES * LANES
        hit = lane - row == column - tile
        rows = pl.ds(pl.multiple_of(index * SET_BEAMS, SET_BEAMS), SET_BEAMS)
        lanes = pl.ds(pl.multiple_of(tile, LANES), LANES)
        table_ref[lax.axis_index("freq") ^ owner, rows, lanes] = jnp.where(hit, 1.0, 0.0).astype(jnp.bfloat16)
        return carry

    lax.fori_loop(0, owner_ref.shape[0], step, 0, unroll=4)
    for j, copy in enumerate(copies):
        copy.wait()
        near_ref[:, j * LANES : (j + 1) * LANES] = held_ref[j].reshape(2 * count, LANES)


def put(out_ref, sems, blocks):
    copies = []
    for index, (block, frame, k) in enumerate(blocks):
        rows = pl.ds(pl.multiple_of((lax.axis_index("freq") ^ k) * UPCH, UPCH), UPCH)
        at = out_ref.at[pl.ds(frame, block.shape[0]), rows]
        copies.append(pltpu.make_async_copy(block, at, sems.at[index]))
    for copy in copies:
        copy.start()
    for copy in copies:
        copy.wait()


def early_gather_kernel(n_owner, own_ref, *refs):
    near, late, out_ref, sems = refs[: n_owner - 1], refs[n_owner - 1 : -2], refs[-2], refs[-1]
    own = [(own_ref, 0, 0)]

    @pl.when(lax.axis_index("pol") == 0)
    def _():
        put(out_ref, sems, own + [(block, BLOCK, k + 1) for k, block in enumerate(near)])

    @pl.when(lax.axis_index("pol") == 1)
    def _():
        put(out_ref, sems, own + [(block, 0, k + 1) for k, block in enumerate(late)])


def last_gather_kernel(n_owner, *refs):
    far, out_ref, sems = refs[: n_owner - 1], refs[-2], refs[-1]

    @pl.when(lax.axis_index("pol") == 0)
    def _():
        put(out_ref, sems, [(block, 0, k + 1) for k, block in enumerate(far)])


VMEM = pl.BlockSpec(memory_space=pltpu.VMEM)
SMEM = pl.BlockSpec(memory_space=pltpu.SMEM)
ANY = pl.BlockSpec(memory_space=pl.ANY)


def call(body, out_shape, n_in, flops, nbytes, scalars=0, whole=0, after=0, scratch=()):
    many = isinstance(out_shape, (list, tuple))

    def kernel(*refs):
        seen = scalars + n_in + whole
        body(*refs[:seen], *refs[seen + after :])

    return pl.pallas_call(
        kernel,
        out_shape=out_shape,
        in_specs=[SMEM] * scalars + [VMEM] * n_in + [ANY] * (whole + after),
        out_specs=[VMEM] * len(out_shape) if many else VMEM,
        scratch_shapes=list(scratch),
        cost_estimate=pl.CostEstimate(flops=flops, bytes_accessed=nbytes, transcendentals=0),
        compiler_params=pltpu.CompilerParams(vmem_limit_bytes=24 << 20),
    )


def per_device(voltages, feed_gains, owner_table, keep_flags):
    samples = voltages[0, 0]
    gain = feed_gains[0, 0]
    frame_count = samples.shape[0] // UPCH
    kept = frame_count // 2
    n_owner = lax.axis_size("freq")
    assert voltages.shape[1] == 1 and kept == 2 * BLOCK and kept >= TAPS
    assert n_owner & (n_owner - 1) == 0
    n_tm = lax.axis_size("tm")
    most_sets = 2 * owner_table.shape[0] // n_owner
    beams = keep_flags.shape[0]
    width = most_sets * SET_BEAMS
    bf16 = jnp.bfloat16
    filt = jnp.asarray(filter_matrix())
    edge = jnp.asarray(filter_matrix()[:, ROWS : BLOCK * ROWS])
    beam_table = jnp.asarray(beam_matrix())

    pairs = [(i, i + 1) for i in range(n_tm - 1)]

    def ahead(part, source):
        return lax.ppermute(part, ("tm", "pol"), [(i * 2 + source, j * 2 + 1) for i, j in pairs])

    def swap(part):
        return lax.ppermute(part, "pol", [(0, 1), (1, 0)])

    def spread(blocks, source):
        got = []
        for k in range(1, n_owner):
            route = [(i * 2 + source, (i ^ k) * 2 + 1 - source) for i in range(n_owner)]
            got.append(lax.ppermute(blocks[k], ("freq", "pol"), route))
        return got

    def form(body, frames, *arrays, more=()):
        shape = [jax.ShapeDtypeStruct((frames * UPCH, beams), bf16), jax.ShapeDtypeStruct((frames, UPCH, width), bf16)]
        scratch = [pltpu.VMEM((CYL * BLOCK * UPCH, 2 * NS), bf16)]
        return call(
            body, shape + list(more), len(arrays), 4 * 512 * 1024 * 1024, 4 << 20, scratch=scratch
        )(*arrays)

    def rest(body, frames, *arrays, more=(), count=n_owner - 1):
        shape = [jax.ShapeDtypeStruct((frames, UPCH, width), bf16)] * count
        return call(body, list(more) + shape, len(arrays), 1 << 29, 4 << 20)(*arrays)

    keep = keep_flags.reshape(1, -1)
    reach, edge_rows = BLOCK * ROWS, (TAPS - 1 - BLOCK) * ROWS
    strips = CYL * NS // LANES
    table, near_rows = pl.pallas_call(
        head_kernel,
        out_shape=[jax.ShapeDtypeStruct((n_owner, beams, width), bf16), jax.ShapeDtypeStruct((reach, CYL * NS), bf16)],
        in_specs=[pl.BlockSpec(memory_space=pltpu.HBM)] * 2,
        out_specs=[VMEM, VMEM],
        scratch_shapes=[
            pltpu.VMEM((strips, BLOCK * UPCH, 2, LANES), bf16),
            pltpu.SMEM(owner_table.shape, jnp.int32),
            pltpu.SMEM((n_owner,), jnp.int32),
            pltpu.SemaphoreType.DMA((strips,)),
            pltpu.SemaphoreType.DMA(()),
        ],
        cost_estimate=pl.CostEstimate(flops=1 << 20, bytes_accessed=4 << 20, transcendentals=0),
        compiler_params=pltpu.CompilerParams(vmem_limit_bytes=24 << 20),
    )(*(pltpu.with_memory_space_constraint(array, pltpu.HBM) for array in (owner_table, samples)))
    near0 = ahead(near_rows, 0)
    near1 = ahead(near_rows, 1)
    samples, table = lax.optimization_barrier((samples, table))
    rows = samples.transpose(0, 2, 1, 3).reshape(-1, CYL * NS)
    rows = lax.optimization_barrier(rows)
    shape = jax.ShapeDtypeStruct((rows.shape[0] - reach, CYL * NS), bf16)
    x = call(first_rows_kernel, shape, 1, 0, 3 << 20)(rows)
    other = swap(x)
    other_near = swap(near_rows)
    gain_other = swap(gain)
    cal = pltpu.VMEM((CYL * BLOCK * UPCH, 2 * NS), bf16)
    late_own = call(
        late_own_kernel,
        jax.ShapeDtypeStruct((kept * UPCH, beams), bf16),
        5,
        4 * 512 * 1024 * 1024,
        4 << 20,
        scratch=[cal],
    )(filt, x, near_rows, gain, beam_table)
    late_first = call(
        late_first_kernel,
        jax.ShapeDtypeStruct((BLOCK * UPCH, beams), bf16),
        6,
        2 * 512 * 1024 * 1024,
        4 << 20,
        scratch=[cal],
    )(filt, other, gain_other, beam_table, keep, late_own)
    late_sum, late_last = form(
        late_kernel, kept, filt, other, other_near, gain_other, beam_table, keep, table, late_own, late_first
    )
    shape = jax.ShapeDtypeStruct((2 * edge_rows, CYL * NS), bf16)
    far_rows = call(far_rows_kernel, shape, 2, 0, 2 << 20)(x, other)
    far_halo = ahead(far_rows, 1)
    late = [*rest(functools.partial(place_kernel, 0), kept, late_sum, table), late_last]
    late_got = spread(late, 0)
    common = (gain, gain_other, beam_table, keep, table)
    near_sum, near_last = form(near_kernel, BLOCK, filt, near1, near0, x, other, *common)
    near = [*rest(functools.partial(place_kernel, 1), BLOCK, near_sum, table), near_last]
    near_got = spread(near, 1)
    pre = call(
        ahead_kernel,
        jax.ShapeDtypeStruct((2 * CYL, reach, NS), jnp.float32),
        5,
        2 * 512 * 1024 * 1024,
        4 << 20,
        after=1,
    )(filt, near1, near0, x, other, near[0])
    block_shape = jax.ShapeDtypeStruct((BLOCK, UPCH, width), bf16)
    far_sum, far_last, far_next = form(far_kernel, BLOCK, edge, far_halo, *common, pre, more=[block_shape])
    own, *far = rest(
        far_place_kernel,
        BLOCK,
        far_sum,
        table,
        near[0],
        late[0],
        more=[jax.ShapeDtypeStruct((kept, UPCH, width), bf16)],
        count=n_owner - 3,
    )
    far = [own, *far, far_next, far_last]
    far_got = spread(far, 1)
    own_got = swap(own)
    out_shape = jax.ShapeDtypeStruct((kept, n_owner * UPCH, width), bf16)

    def gather(body, arrays, base=()):
        return pl.pallas_call(
            functools.partial(body, n_owner),
            out_shape=out_shape,
            in_specs=[VMEM] * len(arrays) + [ANY] * len(base),
            out_specs=ANY,
            scratch_shapes=[pltpu.SemaphoreType.DMA((n_owner,))],
            input_output_aliases={len(arrays): 0} if base else {},
            cost_estimate=pl.CostEstimate(flops=0, bytes_accessed=2 << 20, transcendentals=0),
            compiler_params=pltpu.CompilerParams(vmem_limit_bytes=24 << 20),
        )(*arrays, *base)

    out = gather(early_gather_kernel, [own_got, *near_got, *late_got])
    return gather(last_gather_kernel, far_got, base=[out])


def solution(mesh):
    return jax.shard_map(
        per_device,
        mesh=mesh,
        in_specs=(
            P("pol", ("grp", "freq"), "tm", None, None, None),
            P(("grp", "freq"), "pol", None, None, None),
            P(),
            P(),
        ),
        out_specs=P(("grp", "tm", "pol"), None, "freq"),
        check_vma=False,
    )
```

```python
import functools

import jax
import jax.numpy as jnp
import numpy as np
from jax import lax
from jax.experimental import pallas as pl
from jax.experimental.pallas import tpu as pltpu
from jax.sharding import PartitionSpec as P


NS = 256
CYL = 4
UPCH = 16
TAPS = 16
SET_BEAMS = 16
BLOCK = 8
LANES = 128
ROWS = 2 * UPCH


def window_taps():
    span = TAPS * UPCH
    steps = np.arange(span, dtype=np.float64)
    weights = np.sinc((steps - (span - 1) / 2.0) / UPCH) * np.sin(np.pi * (steps + 0.5) / span) ** 2
    return weights / np.sqrt(np.sum(weights * weights))


def filter_matrix():
    weights = window_taps()
    fine = np.arange(UPCH)
    sample = np.arange(TAPS * UPCH)
    phase = 2.0 * np.pi * ((fine[:, None] * sample[None, :]) % UPCH) / UPCH
    cosine = np.cos(phase) * weights
    sine = np.sin(phase) * weights
    table = np.zeros((2, BLOCK, UPCH, TAPS + BLOCK, UPCH, 2))
    for frame in range(BLOCK):
        taps = slice(frame + 1, frame + 1 + TAPS)
        cos_part = cosine.reshape(UPCH, TAPS, UPCH)
        sin_part = sine.reshape(UPCH, TAPS, UPCH)
        table[0, frame, :, taps, :, 0] = cos_part
        table[0, frame, :, taps, :, 1] = sin_part
        table[1, frame, :, taps, :, 0] = -sin_part
        table[1, frame, :, taps, :, 1] = cos_part
    return table.reshape(2 * BLOCK * UPCH, (TAPS + BLOCK) * ROWS).astype(np.float32).astype(jnp.bfloat16)


def beam_matrix():
    rows = np.arange(NS)
    angle = 2.0 * np.pi * (rows[:, None] * rows[None, :] % NS) / NS
    scale = 1.0 / np.sqrt(NS)
    cosine = (np.cos(angle) * scale).astype(np.float32)
    sine = (np.sin(angle) * scale).astype(np.float32)
    upper = np.concatenate([cosine, -sine], axis=1)
    lower = np.concatenate([sine, cosine], axis=1)
    table = np.concatenate([upper, lower], axis=0).astype(jnp.bfloat16)
    table = table.reshape(2 * NS, 2, NS // LANES, LANES).transpose(0, 2, 1, 3).reshape(2 * NS, 2 * NS)
    return (table.astype(np.float32) * 0.5).astype(jnp.bfloat16)


def columns(cyl):
    return slice(cyl * NS, (cyl + 1) * NS)


def form_powers(spectra, gain_ref, beam_ref, cal_ref, emit):
    half = BLOCK * UPCH
    for cyl in range(CYL):
        spec = spectra(cyl)
        real, imag = spec[:half], spec[half:]
        gain_real = gain_ref[cyl, 0:1, :]
        gain_imag = gain_ref[cyl, 1:2, :]
        rows = slice(cyl * half, (cyl + 1) * half)
        cal_ref[rows, :NS] = (real * gain_real - imag * gain_imag).astype(jnp.bfloat16)
        cal_ref[rows, NS:] = (real * gain_imag + imag * gain_real).astype(jnp.bfloat16)
    for strip in range(NS // LANES):
        beam = jnp.dot(
            cal_ref[...],
            beam_ref[:, strip * 2 * LANES : (strip + 1) * 2 * LANES],
            preferred_element_type=jnp.float32,
        )
        beams = [beam[cyl * half : (cyl + 1) * half] for cyl in range(CYL)]
        (r0, i0), (r1, i1), (r2, i2), (r3, i3) = [(b[:, :LANES], b[:, LANES:]) for b in beams]
        pr, pi, mr, mi = r0 + r2, i0 + i2, r0 - r2, i0 - i2
        sr, si, dr, di = r1 + r3, i1 + i3, r1 - r3, i1 - i3
        formed = [(pr + sr, pi + si), (mr + di, mi - dr), (pr - sr, pi - si), (mr - di, mi + dr)]
        for element, (fr, fi) in enumerate(formed):
            emit(element * NS + strip * LANES, fr * fr + fi * fi)


def filtered(terms):
    total = None
    for table, rows in terms:
        term = jnp.dot(table, rows, preferred_element_type=jnp.float32)
        total = term if total is None else total + term
    return total


def keeper(power_ref, at=0):
    rows = pl.ds(at, BLOCK * UPCH)

    def emit(column, power):
        power_ref[rows, column : column + LANES] = power.astype(jnp.bfloat16)

    return emit


def adder(power_ref, keep_ref, sum_ref, at=0):
    rows = pl.ds(at, BLOCK * UPCH)

    def emit(column, power):
        lanes = slice(column, column + LANES)
        total = power_ref[rows, lanes].astype(jnp.float32) + power.astype(jnp.bfloat16).astype(jnp.float32)
        sum_ref[rows, lanes] = (total * keep_ref[:, lanes].astype(jnp.float32)).astype(jnp.bfloat16)

    return emit


def place(sum_ref, table, out_ref):
    placed = jnp.dot(sum_ref[...], table, preferred_element_type=jnp.float32)
    out_ref[...] = placed.astype(jnp.bfloat16).reshape(out_ref.shape)


def place_kernel(pol, sum_ref, table_ref, *out_refs):
    @pl.when(lax.axis_index("pol") == pol)
    def _():
        for k, out_ref in enumerate(out_refs):
            place(sum_ref, table_ref[k], out_ref)


def first_rows_kernel(x_ref, out_ref):
    out_ref[...] = x_ref[: out_ref.shape[0], :]


def far_rows_kernel(x_ref, other_ref, out_ref):
    count = out_ref.shape[0] // 2
    at = x_ref.shape[0] - count

    @pl.when(lax.axis_index("pol") == 1)
    def _():
        out_ref[:count, :] = x_ref[at:, :]
        out_ref[count:, :] = other_ref[at:, :]


def late_spectra(block, filt_ref, x_ref, near_ref):
    first = block * BLOCK * ROWS
    depth = (TAPS + BLOCK) * ROWS
    here = min(depth, x_ref.shape[0] - first)

    def spectra(cyl):
        terms = [(filt_ref[:, :here], x_ref[first : first + here, columns(cyl)])]
        if here < depth:
            terms.append((filt_ref[:, here:], near_ref[: depth - here, columns(cyl)]))
        return filtered(terms)

    return spectra


def late_own_kernel(filt_ref, x_ref, near_ref, gain_ref, beam_ref, keep_ref, out_ref, cal_ref):
    del keep_ref

    @pl.when(lax.axis_index("pol") == 0)
    def _():
        for block in range(out_ref.shape[0] // (BLOCK * UPCH)):
            spectra = late_spectra(block, filt_ref, x_ref, near_ref)
            form_powers(spectra, gain_ref, beam_ref, cal_ref, keeper(out_ref, block * BLOCK * UPCH))


def late_first_kernel(filt_ref, x_ref, gain_ref, beam_ref, keep_ref, power_ref, sum_ref, cal_ref):
    @pl.when(lax.axis_index("pol") == 0)
    def _():
        spectra = late_spectra(0, filt_ref, x_ref, None)
        form_powers(spectra, gain_ref, beam_ref, cal_ref, adder(power_ref, keep_ref, sum_ref))


def late_kernel(
    filt_ref, x_ref, near_ref, gain_ref, beam_ref, keep_ref, table_ref, power_ref, first_ref, sum_ref, out_ref, cal_ref
):
    done = first_ref.shape[0]

    @pl.when(lax.axis_index("pol") == 0)
    def _():
        sum_ref[:done, :] = first_ref[...]
        for block in range(done // (BLOCK * UPCH), sum_ref.shape[0] // (BLOCK * UPCH)):
            spectra = late_spectra(block, filt_ref, x_ref, near_ref)
            emit = adder(power_ref, keep_ref, sum_ref, block * BLOCK * UPCH)
            form_powers(spectra, gain_ref, beam_ref, cal_ref, emit)
        place(sum_ref, table_ref[table_ref.shape[0] - 1], out_ref)


def near_kernel(
    filt_ref, n0, n1, x0, x1, g0, g1, beam_ref, keep_ref, table_ref, sum_ref, out_ref, cal_ref
):
    reach = BLOCK * ROWS

    @pl.when(lax.axis_index("pol") == 1)
    def _():
        for pol, (n, x, gain) in enumerate(((n0, x0, g0), (n1, x1, g1))):

            def spectra(cyl, n=n, x=x):
                there, here = n[:, columns(cyl)], x[: 2 * reach, columns(cyl)]
                return filtered([(filt_ref[:, :reach], there), (filt_ref[:, reach:], here)])

            emit = adder(sum_ref, keep_ref, sum_ref) if pol else keeper(sum_ref)
            form_powers(spectra, gain, beam_ref, cal_ref, emit)
        place(sum_ref, table_ref[table_ref.shape[0] - 1], out_ref)


def ahead_kernel(filt_ref, n0, n1, x0, x1, pre_ref):
    reach = BLOCK * ROWS

    @pl.when(lax.axis_index("pol") == 1)
    def _():
        for pol, (n, x) in enumerate(((n0, x0), (n1, x1))):
            for cyl in range(CYL):
                there, here = n[:, columns(cyl)], x[:reach, columns(cyl)]
                terms = [(filt_ref[:, reach : 2 * reach], there), (filt_ref[:, 2 * reach :], here)]
                pre_ref[pol * CYL + cyl] = filtered(terms)


def far_kernel(
    edge_ref, far_ref, g0, g1, beam_ref, keep_ref, table_ref, pre_ref, sum_ref, out_ref, next_ref, cal_ref
):
    @pl.when(lax.axis_index("pol") == 1)
    def _():
        count = far_ref.shape[0] // 2
        for pol, gain in enumerate((g0, g1)):

            def spectra(cyl, pol=pol):
                rows = far_ref[pol * count : (pol + 1) * count, columns(cyl)]
                return pre_ref[pol * CYL + cyl] + filtered([(edge_ref[...], rows)])

            emit = adder(sum_ref, keep_ref, sum_ref) if pol else keeper(sum_ref)
            form_powers(spectra, gain, beam_ref, cal_ref, emit)
        place(sum_ref, table_ref[table_ref.shape[0] - 1], out_ref)
        place(sum_ref, table_ref[table_ref.shape[0] - 2], next_ref)


def far_place_kernel(sum_ref, table_ref, near_ref, late_ref, own_ref, *out_refs):
    @pl.when(lax.axis_index("pol") == 1)
    def _():
        for k, out_ref in enumerate(out_refs, 1):
            place(sum_ref, table_ref[k], out_ref)
        place(sum_ref, table_ref[0], own_ref.at[:BLOCK])
        own_ref[BLOCK:] = near_ref[...]

    @pl.when(lax.axis_index("pol") == 0)
    def _():
        own_ref[...] = late_ref[...]


def head_kernel(sets_ref, v_ref, table_ref, near_ref, held_ref, owner_ref, rank_ref, sems, sem):
    count = held_ref.shape[1]
    strips = NS // LANES
    copies = [
        pltpu.make_async_copy(
            v_ref.at[pl.ds(v_ref.shape[0] - count, count), j // strips, :, pl.ds(j % strips * LANES, LANES)],
            held_ref.at[j],
            sems.at[j],
        )
        for j in range(CYL * strips)
    ]
    sets_copy = pltpu.make_async_copy(sets_ref, owner_ref, sem)
    sets_copy.start()
    for copy in copies:
        copy.start()
    for owner in range(table_ref.shape[0]):
        rank_ref[owner] = 0
    table_ref[...] = jnp.zeros_like(table_ref)
    sets_copy.wait()
    row = lax.broadcasted_iota(jnp.int32, (SET_BEAMS, LANES), 0)
    lane = lax.broadcasted_iota(jnp.int32, (SET_BEAMS, LANES), 1)

    def step(index, carry):
        owner = owner_ref[index]
        rank = rank_ref[owner]
        rank_ref[owner] = rank + 1
        column = rank * SET_BEAMS
        tile = column // LANES * LANES
        hit = lane - row == column - tile
        rows = pl.ds(pl.multiple_of(index * SET_BEAMS, SET_BEAMS), SET_BEAMS)
        lanes = pl.ds(pl.multiple_of(tile, LANES), LANES)
        table_ref[lax.axis_index("freq") ^ owner, rows, lanes] = jnp.where(hit, 1.0, 0.0).astype(jnp.bfloat16)
        return carry

    lax.fori_loop(0, owner_ref.shape[0], step, 0, unroll=True)
    for j, copy in enumerate(copies):
        copy.wait()
        near_ref[:, j * LANES : (j + 1) * LANES] = held_ref[j].reshape(2 * count, LANES)


def put(out_ref, sems, blocks):
    copies = []
    for index, (block, frame, k) in enumerate(blocks):
        rows = pl.ds(pl.multiple_of((lax.axis_index("freq") ^ k) * UPCH, UPCH), UPCH)
        at = out_ref.at[pl.ds(frame, block.shape[0]), rows]
        copies.append(pltpu.make_async_copy(block, at, sems.at[index]))
    for copy in copies:
        copy.start()
    for copy in copies:
        copy.wait()


def early_gather_kernel(n_owner, own_ref, *refs):
    near, late, out_ref, sems = refs[: n_owner - 1], refs[n_owner - 1 : -2], refs[-2], refs[-1]
    own = [(own_ref, 0, 0)]

    @pl.when(lax.axis_index("pol") == 0)
    def _():
        put(out_ref, sems, own + [(block, BLOCK, k + 1) for k, block in enumerate(near)])

    @pl.when(lax.axis_index("pol") == 1)
    def _():
        put(out_ref, sems, own + [(block, 0, k + 1) for k, block in enumerate(late)])


def last_gather_kernel(n_owner, *refs):
    far, out_ref, sems = refs[: n_owner - 1], refs[-2], refs[-1]

    @pl.when(lax.axis_index("pol") == 0)
    def _():
        put(out_ref, sems, [(block, 0, k + 1) for k, block in enumerate(far)])


VMEM = pl.BlockSpec(memory_space=pltpu.VMEM)
SMEM = pl.BlockSpec(memory_space=pltpu.SMEM)
ANY = pl.BlockSpec(memory_space=pl.ANY)


def call(body, out_shape, n_in, flops, nbytes, scalars=0, whole=0, after=0, scratch=()):
    many = isinstance(out_shape, (list, tuple))

    def kernel(*refs):
        seen = scalars + n_in + whole
        body(*refs[:seen], *refs[seen + after :])

    return pl.pallas_call(
        kernel,
        out_shape=out_shape,
        in_specs=[SMEM] * scalars + [VMEM] * n_in + [ANY] * (whole + after),
        out_specs=[VMEM] * len(out_shape) if many else VMEM,
        scratch_shapes=list(scratch),
        cost_estimate=pl.CostEstimate(flops=flops, bytes_accessed=nbytes, transcendentals=0),
        compiler_params=pltpu.CompilerParams(vmem_limit_bytes=24 << 20),
    )


def per_device(voltages, feed_gains, owner_table, keep_flags):
    samples = voltages[0, 0]
    gain = feed_gains[0, 0]
    frame_count = samples.shape[0] // UPCH
    kept = frame_count // 2
    n_owner = lax.axis_size("freq")
    assert voltages.shape[1] == 1 and kept == 2 * BLOCK and kept >= TAPS
    assert n_owner & (n_owner - 1) == 0
    n_tm = lax.axis_size("tm")
    most_sets = 2 * owner_table.shape[0] // n_owner
    beams = keep_flags.shape[0]
    width = most_sets * SET_BEAMS
    bf16 = jnp.bfloat16
    filt = jnp.asarray(filter_matrix())
    edge = jnp.asarray(filter_matrix()[:, ROWS : BLOCK * ROWS])
    beam_table = jnp.asarray(beam_matrix())

    pairs = [(i, i + 1) for i in range(n_tm - 1)]

    def ahead(part, source):
        return lax.ppermute(part, ("tm", "pol"), [(i * 2 + source, j * 2 + 1) for i, j in pairs])

    def swap(part):
        return lax.ppermute(part, "pol", [(0, 1), (1, 0)])

    def spread(blocks, source):
        got = []
        for k in range(1, n_owner):
            route = [(i * 2 + source, (i ^ k) * 2 + 1 - source) for i in range(n_owner)]
            got.append(lax.ppermute(blocks[k], ("freq", "pol"), route))
        return got

    def form(body, frames, *arrays, more=()):
        shape = [jax.ShapeDtypeStruct((frames * UPCH, beams), bf16), jax.ShapeDtypeStruct((frames, UPCH, width), bf16)]
        scratch = [pltpu.VMEM((CYL * BLOCK * UPCH, 2 * NS), bf16)]
        return call(
            body, shape + list(more), len(arrays), 4 * 512 * 1024 * 1024, 4 << 20, scratch=scratch
        )(*arrays)

    def rest(body, frames, *arrays, more=(), count=n_owner - 1):
        shape = [jax.ShapeDtypeStruct((frames, UPCH, width), bf16)] * count
        return call(body, list(more) + shape, len(arrays), 1 << 29, 4 << 20)(*arrays)

    keep = keep_flags.reshape(1, -1)
    reach, edge_rows = BLOCK * ROWS, (TAPS - 1 - BLOCK) * ROWS
    strips = CYL * NS // LANES
    table, near_rows = pl.pallas_call(
        head_kernel,
        out_shape=[jax.ShapeDtypeStruct((n_owner, beams, width), bf16), jax.ShapeDtypeStruct((reach, CYL * NS), bf16)],
        in_specs=[pl.BlockSpec(memory_space=pltpu.HBM)] * 2,
        out_specs=[VMEM, VMEM],
        scratch_shapes=[
            pltpu.VMEM((strips, BLOCK * UPCH, 2, LANES), bf16),
            pltpu.SMEM(owner_table.shape, jnp.int32),
            pltpu.SMEM((n_owner,), jnp.int32),
            pltpu.SemaphoreType.DMA((strips,)),
            pltpu.SemaphoreType.DMA(()),
        ],
        cost_estimate=pl.CostEstimate(flops=1 << 20, bytes_accessed=4 << 20, transcendentals=0),
        compiler_params=pltpu.CompilerParams(vmem_limit_bytes=24 << 20),
    )(*(pltpu.with_memory_space_constraint(array, pltpu.HBM) for array in (owner_table, samples)))
    near0 = ahead(near_rows, 0)
    near1 = ahead(near_rows, 1)
    samples, table = lax.optimization_barrier((samples, table))
    rows = samples.transpose(0, 2, 1, 3).reshape(-1, CYL * NS)
    rows = lax.optimization_barrier(rows)
    shape = jax.ShapeDtypeStruct((rows.shape[0] - reach, CYL * NS), bf16)
    x = call(first_rows_kernel, shape, 1, 0, 3 << 20)(rows)
    other = swap(x)
    other_near = swap(near_rows)
    gain_other = swap(gain)
    cal = pltpu.VMEM((CYL * BLOCK * UPCH, 2 * NS), bf16)
    late_own = call(
        late_own_kernel,
        jax.ShapeDtypeStruct((kept * UPCH, beams), bf16),
        6,
        4 * 512 * 1024 * 1024,
        4 << 20,
        scratch=[cal],
    )(filt, x, near_rows, gain, beam_table, keep)
    late_first = call(
        late_first_kernel,
        jax.ShapeDtypeStruct((BLOCK * UPCH, beams), bf16),
        6,
        2 * 512 * 1024 * 1024,
        4 << 20,
        scratch=[cal],
    )(filt, other, gain_other, beam_table, keep, late_own)
    late_sum, late_last = form(
        late_kernel, kept, filt, other, other_near, gain_other, beam_table, keep, table, late_own, late_first
    )
    shape = jax.ShapeDtypeStruct((2 * edge_rows, CYL * NS), bf16)
    far_rows = call(far_rows_kernel, shape, 2, 0, 2 << 20)(x, other)
    far_halo = ahead(far_rows, 1)
    late = [*rest(functools.partial(place_kernel, 0), kept, late_sum, table), late_last]
    late_got = spread(late, 0)
    common = (gain, gain_other, beam_table, keep, table)
    near_sum, near_last = form(near_kernel, BLOCK, filt, near1, near0, x, other, *common)
    near = [*rest(functools.partial(place_kernel, 1), BLOCK, near_sum, table), near_last]
    near_got = spread(near, 1)
    pre = call(
        ahead_kernel,
        jax.ShapeDtypeStruct((2 * CYL, reach, NS), jnp.float32),
        5,
        2 * 512 * 1024 * 1024,
        4 << 20,
        after=1,
    )(filt, near1, near0, x, other, near[0])
    block_shape = jax.ShapeDtypeStruct((BLOCK, UPCH, width), bf16)
    far_sum, far_last, far_next = form(far_kernel, BLOCK, edge, far_halo, *common, pre, more=[block_shape])
    own, *far = rest(
        far_place_kernel,
        BLOCK,
        far_sum,
        table,
        near[0],
        late[0],
        more=[jax.ShapeDtypeStruct((kept, UPCH, width), bf16)],
        count=n_owner - 3,
    )
    far = [own, *far, far_next, far_last]
    far_got = spread(far, 1)
    own_got = swap(own)
    out_shape = jax.ShapeDtypeStruct((kept, n_owner * UPCH, width), bf16)

    def gather(body, arrays, base=()):
        return pl.pallas_call(
            functools.partial(body, n_owner),
            out_shape=out_shape,
            in_specs=[VMEM] * len(arrays) + [ANY] * len(base),
            out_specs=ANY,
            scratch_shapes=[pltpu.SemaphoreType.DMA((n_owner,))],
            input_output_aliases={len(arrays): 0} if base else {},
            cost_estimate=pl.CostEstimate(flops=0, bytes_accessed=2 << 20, transcendentals=0),
            compiler_params=pltpu.CompilerParams(vmem_limit_bytes=24 << 20),
        )(*arrays, *base)

    out = gather(early_gather_kernel, [own_got, *near_got, *late_got])
    return gather(last_gather_kernel, far_got, base=[out])


def solution(mesh):
    return jax.shard_map(
        per_device,
        mesh=mesh,
        in_specs=(
            P("pol", ("grp", "freq"), "tm", None, None, None),
            P(("grp", "freq"), "pol", None, None, None),
            P(),
            P(),
        ),
        out_specs=P(("grp", "tm", "pol"), None, "freq"),
        check_vma=False,
    )
```
